128 devices in a mesh: view: 2 (over z_lo), ty: 8 (over z_hi, y), tx: 8 (over x, core).
Axes of the slice: x: 4, y: 4, z: 4 (z_hi: 2, z_lo: 2; z = z_hi * 2 + z_lo), core: 2. Of those that a mesh axis runs over, the one named last changes fastest.
Arguments:
- views_data: float32 [2, 64, 256, 4096], P('view', None, 'ty', 'tx'), may hold values from 0.5 to 2
- psf_axial: float32 [2, 21], P('view'), may hold values from 0.2 to 1
- psf_rows: float32 [2, 7], P('view'), may hold values from 0.2 to 1
- psf_cols: float32 [2, 7], P('view'), may hold values from 0.2 to 1
Outputs:
- estimate: float32 [64, 256, 4096], P(None, 'ty', 'tx')
The draws below stay inside these ranges and needn't reach their ends.
All inputs are finite; a program needn't handle non-finite values.
Results may differ from the reference program's by a relative error of at most 0.0001.
Values sent between devices are 32-bit elements; how exact they have to be, the bound alone decides.
No kernel may reach another device: no remote copies, remote signals or barrier semaphores. Data moves between devices by JAX's collectives and lax.ppermute only.
A program may use at most 128 MiB of HBM per device.

```python
import math
import jax
import jax.numpy as jnp
from jax import lax

PLANES = 64
KZ = 21
KL = 7
ITERS = 2
NY = 256
NX = 4096


def steps_of(stream_key, extent, shards, smallest, top_value):
    level = 1.0
    for axis_at, blocks in shards:
        steps = jax.random.uniform(jax.random.fold_in(jax.random.fold_in(stream_key, 6), axis_at), (blocks,), jnp.float32, smallest / len(shards), top_value / len(shards))
        level = level * jnp.repeat(jnp.exp(steps), extent[axis_at] // blocks).reshape((-1,) + (1,) * (len(extent) - 1 - axis_at))
    return level


def setup_inputs(seed: int = 0) -> dict:
    arg_keys = jax.random.split(jax.random.key(seed), 5)
    return {
        "views_data": jnp.clip(0.5 + 1.5 * jax.random.uniform(arg_keys[0], (2, PLANES, NY, NX), jnp.float32) ** steps_of(arg_keys[0], (2, PLANES, NY, NX), ((0, 2), (2, 8), (3, 8)), -0.2, 0.2), 0.5, 2.0),
        "psf_axial": jnp.clip(jnp.exp(math.log(1.0) - 1.609438 * jax.random.uniform(arg_keys[1], (2, KZ), jnp.float32) ** steps_of(arg_keys[1], (2, KZ), ((0, 2),), -0.2, 0.2)), 0.2, 1.0),
        "psf_rows": jnp.clip(jnp.exp(math.log(1.0) - 1.609438 * jax.random.uniform(arg_keys[2], (2, KL), jnp.float32) ** steps_of(arg_keys[2], (2, KL), ((0, 2),), -0.2, 0.2)), 0.2, 1.0),
        "psf_cols": jnp.clip(jnp.exp(math.log(1.0) - 1.609438 * jax.random.uniform(arg_keys[3], (2, KL), jnp.float32) ** steps_of(arg_keys[3], (2, KL), ((0, 2),), -0.2, 0.2)), 0.2, 1.0),
    }


def taps_pass(field, kernel, axis, length):
    running = kernel[0] * lax.slice_in_dim(field, 0, length, axis=axis)
    for offset in range(1, kernel.shape[0]):
        running = running + kernel[offset] * lax.slice_in_dim(field, offset, offset + length, axis=axis)
    return running


def padded_pass(field, kernel, axis):
    half_width = kernel.shape[0] // 2
    widths = [(0, 0), (0, 0), (0, 0)]
    widths[axis] = (half_width, half_width)
    return taps_pass(jnp.pad(field, widths), kernel, axis, field.shape[axis])


def blur_forward(field, kernel_z, kernel_y, kernel_x):
    field = padded_pass(field, kernel_z, 0)
    field = padded_pass(field, kernel_y, 1)
    return padded_pass(field, kernel_x, 2)


def blur_adjoint(field, kernel_z, kernel_y, kernel_x):
    field = padded_pass(field, kernel_x[::-1], 2)
    field = padded_pass(field, kernel_y[::-1], 1)
    return padded_pass(field, kernel_z[::-1], 0)


def reference(views_data, psf_axial, psf_rows, psf_cols):
    estimate = (views_data[0] + views_data[1]) * 0.5
    kernels = []
    for viewer in range(2):
        kernels.append((psf_axial[viewer] / jnp.sum(psf_axial[viewer]),
                        psf_rows[viewer] / jnp.sum(psf_rows[viewer]),
                        psf_cols[viewer] / jnp.sum(psf_cols[viewer])))
    for repeat in range(ITERS):
        factors = []
        for viewer in range(2):
            kernel_z, kernel_y, kernel_x = kernels[viewer]
            blurred = blur_forward(estimate, kernel_z, kernel_y, kernel_x)
            ratio = views_data[viewer] / blurred
            factors.append(blur_adjoint(ratio, kernel_z, kernel_y, kernel_x))
        estimate = estimate * ((factors[0] + factors[1]) * 0.5)
    return estimate
```

```python
import functools

import jax
import jax.numpy as jnp
from jax import lax
from jax.experimental import pallas as pl
from jax.experimental.pallas import tpu as pltpu
from jax.sharding import PartitionSpec as P

ITERS = 2
Z = 64
LANES = 128
ROWS = 32
HALF = 256
CHUNK = 128
PAD = 6
SIDE = 8
EXT_R = ROWS + 2 * PAD
EXT_C = HALF + 2 * SIDE
VMEM_BYTES = 48 * 1024 * 1024
TINY = 1e-30


def params(**kwargs):
    return pltpu.CompilerParams(vmem_limit_bytes=VMEM_BYTES, **kwargs)


def blocks_of(total, largest=96):
    out, at = [], 0
    while at < total:
        size = min(largest, total - at)
        out.append((at, size))
        at += size
    return out


def matrices_kernel(kz_ref, blur_ref, adj_ref):
    taps = kz_ref.shape[0]
    lane = lax.broadcasted_iota(jnp.int32, (Z, LANES), 1)
    row = lax.broadcasted_iota(jnp.int32, (Z, LANES), 0)
    offset = row - lax.rem(lane, Z) + taps // 2
    mat = jnp.zeros((Z, LANES), jnp.float32)
    for t in range(taps):
        mat = mat + jnp.where(offset == t, kz_ref[t : t + 1, :], 0.0)
    high = mat.astype(jnp.bfloat16)
    low = (mat - high.astype(jnp.float32)).astype(jnp.bfloat16)
    blur_ref[0:Z, 0:LANES] = high
    blur_ref[0:Z, LANES:] = low
    blur_ref[Z:, 0:LANES] = high
    blur_ref[Z:, LANES:] = jnp.zeros((Z, LANES), jnp.bfloat16)
    adj = jnp.concatenate([mat, mat], axis=0).T * 0.5
    ahigh = adj.astype(jnp.bfloat16).astype(jnp.float32)
    alow = adj - ahigh
    first = lax.broadcasted_iota(jnp.int32, (LANES, LANES), 1) < Z
    adj_ref[0:LANES, :] = jnp.where(first, ahigh, alow).astype(jnp.bfloat16)
    adj_ref[LANES:, :] = jnp.where(first, ahigh, 0.0).astype(jnp.bfloat16)


def matrices(kz):
    return pl.pallas_call(
        matrices_kernel,
        out_shape=(
            jax.ShapeDtypeStruct((2 * Z, 2 * LANES), jnp.bfloat16),
            jax.ShapeDtypeStruct((2 * LANES, LANES), jnp.bfloat16),
        ),
        compiler_params=params(),
        name="matrices",
    )(kz)


def turn_kernel(where_ref, own_ref, other_ref, out_ref):
    rows = own_ref.shape[2]
    own = own_ref.reshape(Z * rows, CHUNK)
    other = other_ref.reshape(Z * rows, CHUNK)
    first = where_ref[1] == 0
    for y in range(rows):
        mine = own[pl.ds(y, Z, stride=rows), :]
        theirs = other[pl.ds(y, Z, stride=rows), :]
        pair = jnp.concatenate(
            [jnp.where(first, mine, theirs), jnp.where(first, theirs, mine)], axis=0
        )
        out_ref[y] = pair.T


def turn(where, recorded, received):
    rows = 8
    return pl.pallas_call(
        turn_kernel,
        out_shape=jax.ShapeDtypeStruct((ROWS, CHUNK, LANES), jnp.float32),
        grid_spec=pltpu.PrefetchScalarGridSpec(
            num_scalar_prefetch=1,
            grid=(ROWS // rows,),
            in_specs=[
                pl.BlockSpec((1, Z, rows, CHUNK), lambda i, w: (0, 0, i, w[0])),
                pl.BlockSpec((Z, rows, CHUNK), lambda i, w: (0, i, 0)),
            ],
            out_specs=pl.BlockSpec((rows, CHUNK, LANES), lambda i, w: (i, 0, 0)),
        ),
        cost_estimate=pl.CostEstimate(flops=0, bytes_accessed=4 << 20, transcendentals=0),
        compiler_params=params(),
        name="turn",
    )(where, recorded, received)


def iterate_kernel(first, start, width, final, *refs):
    if first:
        field = None
        recorded, refs = refs[:5], refs[5:]
    else:
        field, recorded, refs = refs[:5], refs[5:10], refs[10:]
    taps_ref, blur_ref, adj_ref, out_ref = refs[:4]
    r_buf, e_buf, xz_buf, xr_buf, tmp, r_sem, e_sem = refs[4:]

    groups = [(0, PAD)] + [(PAD + 8 * i, 8) for i in range(ROWS // 8)] + [(EXT_R - PAD, PAD)]

    def copies(pieces, buf, sems, group):
        top, left, mid, right, bottom = pieces
        row, count = groups[group]
        stop = start + width
        out = []
        if group == 0 or group == len(groups) - 1:
            src = top if group == 0 else bottom
            out.append((src.at[:, pl.ds(start, width), :], buf.at[pl.ds(row, count), :, :]))
        else:
            for src, lo, hi in (
                (left, 0, SIDE),
                (mid, SIDE, SIDE + HALF),
                (right, SIDE + HALF, EXT_C),
            ):
                a, b = max(lo, start), min(hi, stop)
                if a < b:
                    out.append(
                        (
                            src.at[pl.ds(row - PAD, count), pl.ds(a - lo, b - a), :],
                            buf.at[pl.ds(row, count), pl.ds(a - start, b - a), :],
                        )
                    )
        return [
            pltpu.make_async_copy(src, dst, sems.at[group, k])
            for k, (src, dst) in enumerate(out)
        ]

    r_copies = [copies(recorded, r_buf, r_sem, g) for g in range(len(groups))]
    e_copies = [[] for _ in groups] if first else [copies(field, e_buf, e_sem, g) for g in range(len(groups))]
    if first:
        for g in range(len(groups)):
            for c in r_copies[g]:
                c.start()
    else:
        for g in range(len(groups)):
            for c in e_copies[g]:
                c.start()
        for g in range(len(groups)):
            for c in r_copies[g]:
                c.start()

    kx = [taps_ref[t : t + 1, :] for t in range(7)]
    ky = [taps_ref[8 + t : 9 + t, :] for t in range(7)]
    col_blocks = blocks_of(width)
    lower = lax.broadcasted_iota(jnp.int32, (width, LANES), 1) < Z

    def cols_pass(slot, taps, dst_ref, row):
        for at, size in col_blocks:
            acc = taps[0] * tmp[slot, pl.ds(5 + at, size), :]
            for t in range(1, 7):
                acc = acc + taps[t] * tmp[slot, pl.ds(5 + t + at, size), :]
            dst_ref[row, pl.ds(at, size), :] = acc

    def blur_row(slot, row):
        if first:
            r = r_buf[row]
            e = (r + pltpu.roll(r, Z, 1)) * 0.5
            e_buf[row] = e
        else:
            e = e_buf[row]
        high = e.astype(jnp.bfloat16).astype(jnp.float32)
        split = jnp.where(lower, high, e - high).astype(jnp.bfloat16)
        both = jnp.dot(split, blur_ref[...], preferred_element_type=jnp.float32)
        tmp[slot, pl.ds(8, width), :] = both[:, :LANES] + both[:, LANES:]
        cols_pass(slot, kx, xz_buf, row)

    for slot in range(2):
        tmp[slot, pl.ds(0, 8), :] = jnp.zeros((8, LANES), jnp.float32)
        tmp[slot, pl.ds(8 + width, 8), :] = jnp.zeros((8, LANES), jnp.float32)

    for g, (row0, count) in enumerate(groups):
        for c in r_copies[g] if first else e_copies[g]:
            c.wait()

        def body(i, carry, row0=row0):
            blur_row(0, row0 + 2 * i)
            blur_row(1, row0 + 2 * i + 1)
            return carry

        lax.fori_loop(0, count // 2, body, 0)

    if not first:
        for g in range(len(groups)):
            for c in r_copies[g]:
                c.wait()

    def rows_pass(src_ref, taps, row, at, size):
        acc = taps[0] * src_ref[row - 3, pl.ds(at, size), :]
        for t in range(1, 7):
            acc = acc + taps[t] * src_ref[row - 3 + t, pl.ds(at, size), :]
        return acc

    def ratio_row(slot, row):
        for at, size in col_blocks:
            blurred = rows_pass(xz_buf, ky, row, at, size)
            ratio = r_buf[row, pl.ds(at, size), :] / jnp.maximum(blurred, TINY)
            tmp[slot, pl.ds(8 + at, size), :] = ratio
        cols_pass(slot, kx[::-1], xr_buf, row)

    def ratio_body(i, carry):
        ratio_row(0, 3 + 2 * i)
        ratio_row(1, 4 + 2 * i)
        return carry

    lax.fori_loop(0, (EXT_R - 6) // 2, ratio_body, 0)

    inner = width - 2 * SIDE

    def update_row(row):
        spread = []
        for at, size in blocks_of(inner, 64):
            spread.append(rows_pass(xr_buf, ky[::-1], row, SIDE + at, size))
        spread = jnp.concatenate(spread, axis=0)
        high = spread.astype(jnp.bfloat16)
        low = (spread - high.astype(jnp.float32)).astype(jnp.bfloat16)
        both = jnp.dot(
            jnp.concatenate([high, low], axis=1), adj_ref[...], preferred_element_type=jnp.float32
        )
        factor = both + pltpu.roll(both, Z, 1)
        return e_buf[row, pl.ds(SIDE, inner), :] * factor

    if final:
        flat = out_ref.reshape(Z * ROWS, CHUNK)

    def update_body(i, carry):
        for k in range(2):
            y = 2 * i + k
            new = update_row(PAD + y)
            if final:
                flat[pl.ds(y, Z, stride=ROWS), :] = new.T[:Z]
            else:
                out_ref[y] = new
        return carry

    lax.fori_loop(0, ROWS // 2, update_body, 0)


def iterate(field, recorded, taps, blur, adj, *, first, start, width, final):
    inner = width - 2 * SIDE
    out = (Z, ROWS, inner) if final else (ROWS, inner, LANES)
    pieces = list(recorded) if first else list(field) + list(recorded)
    row = pltpu.VMEM((EXT_R, width, LANES), jnp.float32)
    vregs = EXT_R * width // 8
    return pl.pallas_call(
        functools.partial(iterate_kernel, first, start, width, final),
        out_shape=jax.ShapeDtypeStruct(out, jnp.float32),
        in_specs=[pl.BlockSpec(memory_space=pl.ANY)] * len(pieces)
        + [pl.BlockSpec(memory_space=pltpu.VMEM)] * 3,
        out_specs=pl.BlockSpec(memory_space=pltpu.VMEM),
        scratch_shapes=[
            row,
            row,
            row,
            row,
            pltpu.VMEM((2, width + 16, LANES), jnp.float32),
            pltpu.SemaphoreType.DMA((6, 3)),
            pltpu.SemaphoreType.DMA((6, 3)),
        ],
        cost_estimate=pl.CostEstimate(
            flops=vregs * 1024 * 70, bytes_accessed=vregs * 4096 * 3, transcendentals=0
        ),
        compiler_params=params(),
        name="iterate",
    )(*pieces, taps, blur, adj)


def place_kernel(where_ref, *refs):
    refs[-1][...] = refs[0][...]


def place(where, block, whole):
    rows = 16
    spec = pl.BlockSpec((rows, ROWS, CHUNK), lambda i, w: (i, 0, 0))
    args = [where, block]
    in_specs = [spec]
    aliases = {}
    if whole is not None:
        args.append(whole)
        in_specs.append(pl.BlockSpec(memory_space=pl.ANY))
        aliases = {2: 0}
    return pl.pallas_call(
        place_kernel,
        out_shape=jax.ShapeDtypeStruct((Z, ROWS, 2 * HALF), jnp.float32),
        grid_spec=pltpu.PrefetchScalarGridSpec(
            num_scalar_prefetch=1,
            grid=(Z // rows,),
            in_specs=in_specs,
            out_specs=pl.BlockSpec((rows, ROWS, CHUNK), lambda i, w: (i, 0, w[0])),
        ),
        input_output_aliases=aliases,
        cost_estimate=pl.CostEstimate(flops=0, bytes_accessed=2 << 20, transcendentals=0),
        compiler_params=params(),
        name="place",
    )(*args)


def neighbours(views, tiles):
    right = []
    for v in range(views):
        for t in range(tiles):
            if (t + v) % 2 == 0:
                right.append((v * tiles + t, (1 - v) * tiles + t))
            elif t + 1 < tiles:
                right.append((v * tiles + t, v * tiles + t + 1))
    return right


def per_device(views_data, psf_axial, psf_rows, psf_cols):
    views, tiles, bands = lax.axis_size("view"), lax.axis_size("tx"), lax.axis_size("ty")
    swap = [(0, 1), (1, 0)]
    right = neighbours(views, tiles)
    left = [(b, a) for a, b in right]
    down = [(i, i + 1) for i in range(bands - 1)]
    up = [(b, a) for a, b in down]
    half = lax.rem(lax.axis_index("tx") + lax.axis_index("view"), 2)

    def other_block(j):
        at = (1 - half) * HALF + j * CHUNK
        return lax.dynamic_slice(views_data, (0, 0, 0, at), (1, Z, ROWS, CHUNK))[0]

    incoming = [lax.ppermute(other_block(j), "view", swap) for j in range(2)]

    norm = lambda k: k[0] / jnp.sum(k[0])
    own = jnp.concatenate([norm(psf_axial), norm(psf_rows), norm(psf_cols)])
    other = lax.ppermute(own, "view", swap)
    view = lax.axis_index("view")
    lanes = jnp.concatenate(
        [
            jnp.broadcast_to(jnp.where(view == 0, own, other)[:, None], (own.shape[0], Z)),
            jnp.broadcast_to(jnp.where(view == 0, other, own)[:, None], (own.shape[0], Z)),
        ],
        axis=1,
    )
    blur, adj = matrices(lanes[:21])
    taps = jnp.zeros((16, LANES), jnp.float32)
    taps = taps.at[0:7].set(lanes[28:35]).at[8:15].set(lanes[21:28])

    mid = jnp.concatenate(
        [
            turn(jnp.stack([half * 2 + j, view]).astype(jnp.int32), views_data, incoming[j])
            for j in range(2)
        ],
        axis=1,
    )

    def extend(block):
        west = lax.ppermute(block[:, HALF - SIDE :], ("view", "tx"), right)
        east = lax.ppermute(block[:, :SIDE], ("view", "tx"), left)

        def edge(rows):
            return jnp.concatenate([west[rows], block[rows], east[rows]], axis=1)

        north = lax.ppermute(edge(slice(ROWS - PAD, ROWS)), "ty", down)
        south = lax.ppermute(edge(slice(0, PAD)), "ty", up)
        return north, west, block, east, south

    recorded = extend(mid)
    estimate = iterate(
        None, recorded, taps, blur, adj, first=True, start=0, width=EXT_C, final=False
    )
    field = extend(estimate)
    outs = [
        iterate(
            field,
            recorded,
            taps,
            blur,
            adj,
            first=False,
            start=j * CHUNK,
            width=CHUNK + 2 * SIDE,
            final=True,
        )
        for j in range(2)
    ]
    theirs = [lax.ppermute(o, "view", swap) for o in outs]
    whole = None
    for j, block in enumerate(outs):
        whole = place((half * 2 + j).astype(jnp.int32)[None], block, whole)
    for j, block in enumerate(theirs):
        whole = place(((1 - half) * 2 + j).astype(jnp.int32)[None], block, whole)
    return whole


def solution(mesh):
    placed = (P("view", None, "ty", "tx"), P("view", None), P("view", None), P("view", None))
    return jax.shard_map(
        per_device, mesh=mesh, in_specs=placed, out_specs=P(None, "ty", "tx"), check_vma=False
    )
```

```python
import functools

import jax
import jax.numpy as jnp
from jax import lax
from jax.experimental import pallas as pl
from jax.experimental.pallas import tpu as pltpu
from jax.sharding import PartitionSpec as P

ITERS = 2
Z = 64
LANES = 128
ROWS = 32
HALF = 256
CHUNK = 128
PAD = 6
SIDE = 8
MARGIN = 16
GROUP = 8
EXT_R = ROWS + 2 * PAD
EXT_C = HALF + 2 * MARGIN
VMEM_BYTES = 48 * 1024 * 1024
TINY = 1e-30


def params(**kwargs):
    return pltpu.CompilerParams(vmem_limit_bytes=VMEM_BYTES, **kwargs)


def blocks_of(total, largest=96):
    out, at = [], 0
    while at < total:
        size = min(largest, total - at)
        out.append((at, size))
        at += size
    return out


def matrices_kernel(kz_ref, blur_ref, adj_ref):
    taps = kz_ref.shape[0]
    lane = lax.broadcasted_iota(jnp.int32, (Z, LANES), 1)
    row = lax.broadcasted_iota(jnp.int32, (Z, LANES), 0)
    offset = row - lax.rem(lane, Z) + taps // 2
    mat = jnp.zeros((Z, LANES), jnp.float32)
    for t in range(taps):
        mat = mat + jnp.where(offset == t, kz_ref[t : t + 1, :], 0.0)
    high = mat.astype(jnp.bfloat16)
    low = (mat - high.astype(jnp.float32)).astype(jnp.bfloat16)
    blur_ref[0:Z, 0:LANES] = high
    blur_ref[0:Z, LANES:] = low
    blur_ref[Z:, 0:LANES] = high
    blur_ref[Z:, LANES:] = jnp.zeros((Z, LANES), jnp.bfloat16)
    adj = jnp.concatenate([mat, mat], axis=0).T * 0.5
    ahigh = adj.astype(jnp.bfloat16).astype(jnp.float32)
    alow = adj - ahigh
    first = lax.broadcasted_iota(jnp.int32, (LANES, LANES), 1) < Z
    adj_ref[0:LANES, :] = jnp.where(first, ahigh, alow).astype(jnp.bfloat16)
    adj_ref[LANES:, :] = jnp.where(first, ahigh, 0.0).astype(jnp.bfloat16)


def matrices(kz):
    return pl.pallas_call(
        matrices_kernel,
        out_shape=(
            jax.ShapeDtypeStruct((2 * Z, 2 * LANES), jnp.bfloat16),
            jax.ShapeDtypeStruct((2 * LANES, LANES), jnp.bfloat16),
        ),
        compiler_params=params(),
        name="matrices",
    )(kz)


def turn_kernel(where_ref, own_ref, other_ref, out_ref):
    own = own_ref.reshape(Z * GROUP, CHUNK)
    other = other_ref.reshape(Z * GROUP, CHUNK)
    first = where_ref[1] == 0
    for y in range(GROUP):
        mine = own[pl.ds(y, Z, stride=GROUP), :]
        theirs = other[pl.ds(y, Z, stride=GROUP), :]
        pair = jnp.concatenate(
            [jnp.where(first, mine, theirs), jnp.where(first, theirs, mine)], axis=0
        )
        out_ref[y] = pair.T


def turn(where, recorded, received, first_group, group_step):
    return pl.pallas_call(
        turn_kernel,
        out_shape=jax.ShapeDtypeStruct((2 * GROUP, HALF, LANES), jnp.float32),
        grid_spec=pltpu.PrefetchScalarGridSpec(
            num_scalar_prefetch=1,
            grid=(2, 2),
            in_specs=[
                pl.BlockSpec(
                    (1, Z, GROUP, CHUNK),
                    lambda i, j, w: (0, 0, first_group + group_step * i, 2 * w[0] + j),
                ),
                pl.BlockSpec((Z, GROUP, CHUNK), lambda i, j, w: (0, i, j)),
            ],
            out_specs=pl.BlockSpec((GROUP, CHUNK, LANES), lambda i, j, w: (i, j, 0)),
        ),
        cost_estimate=pl.CostEstimate(flops=0, bytes_accessed=4 << 20, transcendentals=0),
        compiler_params=params(),
        name="turn",
    )(where, recorded, received)


SPANS = ((0, PAD),) + tuple((PAD + GROUP * g, GROUP) for g in range(4)) + ((EXT_R - PAD, PAD),)
HOMES = ((0, 0), (1, 0), (1, GROUP), (0, GROUP))


def iterate_kernel(first, row0, n_out, *refs):
    n_in = n_out + 2 * PAD
    width = EXT_C if first else EXT_C - 2 * SIDE
    shift = 0 if first else SIDE
    inner = width - 2 * SIDE
    fold = (EXT_C - 2 * SIDE) // 2
    recorded, refs = refs[:8], refs[8:]
    if not first:
        field, refs = refs[:3], refs[3:]
    taps_ref, blur_ref, adj_ref = refs[:3]
    refs = refs[3:]
    if first:
        out_ref, top_ref, low_ref = refs[:3]
        refs = refs[3:]
    else:
        out_ref, refs = refs[0], refs[1:]
    r_buf, e_buf, xz_buf, xr_buf, pack, tmp, r_sem, e_sem = refs
    north, south = recorded[0], recorded[7]
    lower = lax.broadcasted_iota(jnp.int32, (width, LANES), 1) < Z

    def window(span, lo, hi):
        at, count = span
        a, b = max(at, lo), min(at + count, hi)
        return (a, b) if a < b else None

    def r_copies(k):
        got = window(SPANS[k], row0 + (0 if first else 3), row0 + n_in - (0 if first else 3))
        if got is None:
            return []
        a, b = got
        rows = pl.ds(a - row0, b - a)
        pairs = []
        if k in (0, 5):
            src = north if k == 0 else south
            pairs.append(
                (
                    src.at[pl.ds(a - SPANS[k][0], b - a), pl.ds(shift, width), :],
                    r_buf.at[rows, :, :],
                )
            )
        else:
            home, base = HOMES[k - 1]
            west, mid, east = recorded[1 + 3 * home : 4 + 3 * home]
            for src, lo, hi in (
                (west, 0, MARGIN),
                (mid, MARGIN, MARGIN + HALF),
                (east, MARGIN + HALF, EXT_C),
            ):
                c, d = max(lo, shift), min(hi, shift + width)
                pairs.append(
                    (
                        src.at[pl.ds(base + a - SPANS[k][0], b - a), pl.ds(c - lo, d - c), :],
                        r_buf.at[rows, pl.ds(c - shift, d - c), :],
                    )
                )
        return [
            pltpu.make_async_copy(src, dst, r_sem.at[k, n]) for n, (src, dst) in enumerate(pairs)
        ]

    def e_copies(k):
        got = window(SPANS[k], row0, row0 + n_in)
        if first or got is None:
            return []
        a, b = got
        at = a - SPANS[k][0]
        if k in (0, 5):
            src, dst = (field[0] if k == 0 else field[2]), pack.at[0 if k == 0 else 1]
            return [pltpu.make_async_copy(src, dst, e_sem.at[k])]
        src = field[1].at[pl.ds(GROUP * (k - 1) + at, b - a), :, :]
        return [pltpu.make_async_copy(src, e_buf.at[pl.ds(a - row0, b - a), :, :], e_sem.at[k])]

    recorded_in = [r_copies(k) for k in range(6)]
    field_in = [e_copies(k) for k in range(6)]
    for group in field_in + recorded_in:
        for c in group:
            c.start()

    kx = [taps_ref[t : t + 1, :] for t in range(7)]
    ky = [taps_ref[8 + t : 9 + t, :] for t in range(7)]
    col_blocks = blocks_of(width)

    def cols_pass(slot, taps, dst_ref, row):
        for at, size in col_blocks:
            acc = taps[0] * tmp[slot, pl.ds(5 + at, size), :]
            for t in range(1, 7):
                acc = acc + taps[t] * tmp[slot, pl.ds(5 + t + at, size), :]
            dst_ref[row, pl.ds(at, size), :] = acc

    def blur_row(slot, row):
        if first:
            r = r_buf[row]
            e = (r + pltpu.roll(r, Z, 1)) * 0.5
            e_buf[row] = e
        else:
            e = e_buf[row]
        high = e.astype(jnp.bfloat16).astype(jnp.float32)
        split = jnp.where(lower, high, e - high).astype(jnp.bfloat16)
        both = jnp.dot(split, blur_ref[...], preferred_element_type=jnp.float32)
        tmp[slot, pl.ds(8, width), :] = both[:, :LANES] + both[:, LANES:]
        cols_pass(slot, kx, xz_buf, row)

    for slot in range(2):
        tmp[slot, pl.ds(0, 8), :] = jnp.zeros((8, LANES), jnp.float32)
        tmp[slot, pl.ds(8 + width, 8), :] = jnp.zeros((8, LANES), jnp.float32)

    for k in range(6):
        got = window(SPANS[k], row0, row0 + n_in)
        if got is None:
            continue
        for c in recorded_in[k] if first else field_in[k]:
            c.wait()
        base, count = got[0] - row0, got[1] - got[0]

        def body(i, carry, k=k, base=base):
            for slot in range(2):
                row = base + 2 * i + slot
                if not first and k in (0, 5):
                    packed = pack[0 if k == 0 else 1, 2 * i + slot]
                    turned = pltpu.roll(packed, Z, 1)
                    e_buf[row, pl.ds(0, fold), :] = jnp.where(lower[:fold], packed, turned)
                    e_buf[row, pl.ds(fold, fold), :] = jnp.where(lower[:fold], turned, packed)
                blur_row(slot, row)
            return carry

        lax.fori_loop(0, count // 2, body, 0)

    if not first:
        for group in recorded_in:
            for c in group:
                c.wait()

    def rows_pass(src_ref, taps, row, at, size):
        acc = taps[0] * src_ref[row - 3, pl.ds(at, size), :]
        for t in range(1, 7):
            acc = acc + taps[t] * src_ref[row - 3 + t, pl.ds(at, size), :]
        return acc

    def ratio_body(i, carry):
        for slot in range(2):
            row = 3 + 2 * i + slot
            for at, size in col_blocks:
                blurred = rows_pass(xz_buf, ky, row, at, size)
                ratio = r_buf[row, pl.ds(at, size), :] / jnp.maximum(blurred, TINY)
                tmp[slot, pl.ds(8 + at, size), :] = ratio
            cols_pass(slot, kx[::-1], xr_buf, row)
        return carry

    lax.fori_loop(0, (n_in - 6) // 2, ratio_body, 0)

    def update_row(row):
        spread = []
        for at, size in blocks_of(inner, 64):
            spread.append(rows_pass(xr_buf, ky[::-1], row, SIDE + at, size))
        spread = jnp.concatenate(spread, axis=0)
        high = spread.astype(jnp.bfloat16)
        low = (spread - high.astype(jnp.float32)).astype(jnp.bfloat16)
        both = jnp.dot(
            jnp.concatenate([high, low], axis=1), adj_ref[...], preferred_element_type=jnp.float32
        )
        factor = both + pltpu.roll(both, Z, 1)
        return e_buf[row, pl.ds(SIDE, inner), :] * factor

    def update_body(i, carry, base=0):
        for k in range(2):
            y = base + 2 * i + k
            new = update_row(PAD + y)
            if first:
                out_ref[y] = new
            else:
                for j in range(2):
                    flat = out_ref.at[j].reshape(Z * GROUP, CHUNK)
                    flat[pl.ds(y, Z, stride=GROUP), :] = new[j * CHUNK : (j + 1) * CHUNK].T[:Z]
        return carry

    lax.fori_loop(0, n_out // 2, update_body, 0)
    if first:
        for y in range(PAD):
            for ref, row in ((top_ref, y), (low_ref, ROWS - PAD + y)):
                ref[y] = jnp.where(
                    lower[:fold], out_ref[row, pl.ds(0, fold), :], out_ref[row, pl.ds(fold, fold), :]
                )


def iterate(recorded, field, taps, blur, adj, *, first, row0, n_out):
    n_in = n_out + 2 * PAD
    width = EXT_C if first else EXT_C - 2 * SIDE
    fold = (EXT_C - 2 * SIDE) // 2
    if first:
        edge = jax.ShapeDtypeStruct((PAD, fold, LANES), jnp.float32)
        out = (jax.ShapeDtypeStruct((ROWS, EXT_C - 2 * SIDE, LANES), jnp.float32), edge, edge)
        out_specs = (pl.BlockSpec(memory_space=pltpu.VMEM),) * 3
        pieces = list(recorded)
    else:
        out = jax.ShapeDtypeStruct((2, Z, GROUP, CHUNK), jnp.float32)
        out_specs = pl.BlockSpec(memory_space=pltpu.VMEM)
        pieces = list(recorded) + list(field)
    row = pltpu.VMEM((n_in, width, LANES), jnp.float32)
    vregs = n_in * width // 8
    return pl.pallas_call(
        functools.partial(iterate_kernel, first, row0, n_out),
        out_shape=out,
        in_specs=[pl.BlockSpec(memory_space=pl.ANY)] * len(pieces)
        + [pl.BlockSpec(memory_space=pltpu.VMEM)] * 3,
        out_specs=out_specs,
        scratch_shapes=[
            row,
            row,
            row,
            row,
            pltpu.VMEM((2, PAD, fold, LANES), jnp.float32),
            pltpu.VMEM((2, width + 16, LANES), jnp.float32),
            pltpu.SemaphoreType.DMA((6, 3)),
            pltpu.SemaphoreType.DMA((6,)),
        ],
        cost_estimate=pl.CostEstimate(
            flops=vregs * 1024 * 70, bytes_accessed=vregs * 4096 * 3, transcendentals=0
        ),
        compiler_params=params(),
        name="iterate",
    )(*pieces, taps, blur, adj)


def place_kernel(where_ref, *refs):
    refs[-1][...] = refs[0][0]


def place(where, block, whole, group):
    args = [where, block]
    in_specs = [pl.BlockSpec((1, Z, GROUP, CHUNK), lambda j, w: (j, 0, 0, 0))]
    aliases = {}
    if whole is not None:
        args.append(whole)
        in_specs.append(pl.BlockSpec(memory_space=pl.ANY))
        aliases = {2: 0}
    return pl.pallas_call(
        place_kernel,
        out_shape=jax.ShapeDtypeStruct((Z, ROWS, 2 * HALF), jnp.float32),
        grid_spec=pltpu.PrefetchScalarGridSpec(
            num_scalar_prefetch=1,
            grid=(2,),
            in_specs=in_specs,
            out_specs=pl.BlockSpec((Z, GROUP, CHUNK), lambda j, w: (0, group, 2 * w[0] + j)),
        ),
        input_output_aliases=aliases,
        cost_estimate=pl.CostEstimate(flops=0, bytes_accessed=1 << 20, transcendentals=0),
        compiler_params=params(),
        name="place",
    )(*args)


def neighbours(views, tiles):
    right = []
    for v in range(views):
        for t in range(tiles):
            if (t + v) % 2 == 0:
                right.append((v * tiles + t, (1 - v) * tiles + t))
            elif t + 1 < tiles:
                right.append((v * tiles + t, v * tiles + t + 1))
    return right


def per_device(views_data, psf_axial, psf_rows, psf_cols):
    views, tiles, bands = lax.axis_size("view"), lax.axis_size("tx"), lax.axis_size("ty")
    swap = [(0, 1), (1, 0)]
    right = neighbours(views, tiles)
    left = [(b, a) for a, b in right]
    down = [(i, i + 1) for i in range(bands - 1)]
    up = [(b, a) for a, b in down]
    half = lax.rem(lax.axis_index("tx") + lax.axis_index("view"), 2)

    def other_rows(*starts):
        at = (1 - half) * HALF
        return jnp.concatenate(
            [
                lax.dynamic_slice(views_data, (0, 0, row, at), (1, Z, rows, HALF))[0]
                for row, rows in starts
            ],
            axis=1,
        )

    border_in = lax.ppermute(other_rows((0, GROUP), (ROWS - GROUP, GROUP)), "view", swap)
    inner_in = lax.ppermute(other_rows((GROUP, 2 * GROUP)), "view", swap)

    norm = lambda k: k[0] / jnp.sum(k[0])
    own = jnp.concatenate([norm(psf_axial), norm(psf_rows), norm(psf_cols)])
    other = lax.ppermute(own, "view", swap)
    view = lax.axis_index("view")
    lanes = jnp.concatenate(
        [
            jnp.broadcast_to(jnp.where(view == 0, own, other)[:, None], (own.shape[0], Z)),
            jnp.broadcast_to(jnp.where(view == 0, other, own)[:, None], (own.shape[0], Z)),
        ],
        axis=1,
    )
    blur, adj = matrices(lanes[:21])
    taps = jnp.zeros((16, LANES), jnp.float32)
    taps = taps.at[0:7].set(lanes[28:35]).at[8:15].set(lanes[21:28])

    where = jnp.stack([half, view]).astype(jnp.int32)
    there = (1 - half).astype(jnp.int32)[None]

    def widen(block):
        west = lax.ppermute(block[:, HALF - MARGIN :], ("view", "tx"), right)
        east = lax.ppermute(block[:, :MARGIN], ("view", "tx"), left)
        return west, block, east

    border = widen(turn(where, views_data, border_in, 0, 3))

    def edge(rows):
        return jnp.concatenate([part[rows] for part in border], axis=1)

    north = lax.ppermute(edge(slice(2 * GROUP - PAD, 2 * GROUP)), "ty", down)
    south = lax.ppermute(edge(slice(0, PAD)), "ty", up)
    inner = widen(turn(where, views_data, inner_in, 1, 1))
    recorded = (north,) + border + inner + (south,)

    estimate, top, low = iterate(
        recorded, None, taps, blur, adj, first=True, row0=0, n_out=ROWS
    )
    field = (lax.ppermute(low, "ty", down), estimate, lax.ppermute(top, "ty", up))
    whole = None
    theirs = []
    for group in (1, 2, 0, 3):
        block = iterate(
            recorded, field, taps, blur, adj, first=False, row0=GROUP * group, n_out=GROUP
        )
        theirs.append((group, lax.ppermute(block, "view", swap)))
        whole = place(where[:1], block, whole, group)
    for group, block in theirs:
        whole = place(there, block, whole, group)
    return whole


def solution(mesh):
    placed = (P("view", None, "ty", "tx"), P("view", None), P("view", None), P("view", None))
    return jax.shard_map(
        per_device, mesh=mesh, in_specs=placed, out_specs=P(None, "ty", "tx"), check_vma=False
    )
```

```python
import functools

import jax
import jax.numpy as jnp
from jax import lax
from jax.experimental import pallas as pl
from jax.experimental.pallas import tpu as pltpu
from jax.sharding import PartitionSpec as P

ITERS = 2
Z = 64
LANES = 128
ROWS = 32
HALF = 256
CHUNK = 128
PAD = 6
SIDE = 8
MARGIN = 16
GROUP = 8
EXT_R = ROWS + 2 * PAD
EXT_C = HALF + 2 * MARGIN
MIB = 1024 * 1024
TINY = 1e-30


def params(mib):
    return pltpu.CompilerParams(vmem_limit_bytes=mib * MIB)


def blocks_of(total, largest=96):
    out, at = [], 0
    while at < total:
        size = min(largest, total - at)
        out.append((at, size))
        at += size
    return out


def matrices_kernel(kz_ref, blur_ref, adj_ref):
    taps = kz_ref.shape[0]
    lane = lax.broadcasted_iota(jnp.int32, (Z, LANES), 1)
    row = lax.broadcasted_iota(jnp.int32, (Z, LANES), 0)
    offset = row - lax.rem(lane, Z) + taps // 2
    mat = jnp.zeros((Z, LANES), jnp.float32)
    for t in range(taps):
        mat = mat + jnp.where(offset == t, kz_ref[t : t + 1, :], 0.0)
    high = mat.astype(jnp.bfloat16)
    low = (mat - high.astype(jnp.float32)).astype(jnp.bfloat16)
    blur_ref[0:Z, 0:LANES] = high
    blur_ref[0:Z, LANES:] = low
    blur_ref[Z:, 0:LANES] = high
    blur_ref[Z:, LANES:] = jnp.zeros((Z, LANES), jnp.bfloat16)
    adj = jnp.concatenate([mat, mat], axis=0).T * 0.5
    ahigh = adj.astype(jnp.bfloat16).astype(jnp.float32)
    alow = adj - ahigh
    first = lax.broadcasted_iota(jnp.int32, (LANES, LANES), 1) < Z
    adj_ref[0:LANES, :] = jnp.where(first, ahigh, alow).astype(jnp.bfloat16)
    adj_ref[LANES:, :] = jnp.where(first, ahigh, 0.0).astype(jnp.bfloat16)


def matrices(kz):
    return pl.pallas_call(
        matrices_kernel,
        out_shape=(
            jax.ShapeDtypeStruct((2 * Z, 2 * LANES), jnp.bfloat16),
            jax.ShapeDtypeStruct((2 * LANES, LANES), jnp.bfloat16),
        ),
        compiler_params=params(4),
        name="matrices",
    )(kz)


def turn_kernel(where_ref, own_ref, other_ref, out_ref):
    own = own_ref.reshape(Z * GROUP, CHUNK)
    other = other_ref.reshape(Z * GROUP, CHUNK)
    first = where_ref[1] == 0
    for y in range(GROUP):
        mine = own[pl.ds(y, Z, stride=GROUP), :]
        theirs = other[pl.ds(y, Z, stride=GROUP), :]
        pair = jnp.concatenate(
            [jnp.where(first, mine, theirs), jnp.where(first, theirs, mine)], axis=0
        )
        out_ref[y] = pair.T


def turn(where, recorded, received, first_group, group_step):
    count = received.shape[1] // GROUP
    return pl.pallas_call(
        turn_kernel,
        out_shape=jax.ShapeDtypeStruct((count * GROUP, HALF, LANES), jnp.float32),
        grid_spec=pltpu.PrefetchScalarGridSpec(
            num_scalar_prefetch=1,
            grid=(count, 2),
            in_specs=[
                pl.BlockSpec(
                    (1, Z, GROUP, CHUNK),
                    lambda i, j, w: (0, 0, first_group + group_step * i, 2 * w[0] + j),
                ),
                pl.BlockSpec((Z, GROUP, CHUNK), lambda i, j, w: (0, i, j)),
            ],
            out_specs=pl.BlockSpec((GROUP, CHUNK, LANES), lambda i, j, w: (i, j, 0)),
        ),
        cost_estimate=pl.CostEstimate(
            flops=0, bytes_accessed=count << 21, transcendentals=0
        ),
        compiler_params=params(8),
        name="turn",
    )(where, recorded, received)


SPANS = ((0, PAD),) + tuple((PAD + GROUP * g, GROUP) for g in range(4)) + ((EXT_R - PAD, PAD),)
HOMES = ((0, 0), (1, 0), (2, 0), (0, GROUP))


def iterate_kernel(first, row0, n_out, present, *refs):
    n_in = n_out + 2 * PAD
    width = EXT_C if first else EXT_C - 2 * SIDE
    shift = 0 if first else SIDE
    inner = width - 2 * SIDE
    fold = (EXT_C - 2 * SIDE) // 2
    pieces = iter(refs)
    taken = [next(pieces) if there else None for there in present]
    recorded, field, refs = taken[:11], taken[11:], tuple(pieces)
    taps_ref, blur_ref, adj_ref = refs[:3]
    refs = refs[3:]
    if first:
        out_ref, top_ref, low_ref = refs[:3]
        refs = refs[3:]
    else:
        out_ref, refs = refs[0], refs[1:]
    r_buf, e_buf, xz_buf, xr_buf, pack, tmp, r_sem, e_sem = refs
    north, south = recorded[0], recorded[10]
    lower = lax.broadcasted_iota(jnp.int32, (width, LANES), 1) < Z

    def window(span, lo, hi):
        at, count = span
        a, b = max(at, lo), min(at + count, hi)
        return (a, b) if a < b else None

    def r_copies(k):
        got = window(SPANS[k], row0 + (0 if first else 3), row0 + n_in - (0 if first else 3))
        if got is None:
            return []
        a, b = got
        rows = pl.ds(a - row0, b - a)
        pairs = []
        if k in (0, 5):
            src = north if k == 0 else south
            pairs.append(
                (
                    src.at[pl.ds(a - SPANS[k][0], b - a), pl.ds(shift, width), :],
                    r_buf.at[rows, :, :],
                )
            )
        else:
            home, base = HOMES[k - 1]
            west, mid, east = recorded[1 + 3 * home : 4 + 3 * home]
            for src, lo, hi in (
                (west, 0, MARGIN),
                (mid, MARGIN, MARGIN + HALF),
                (east, MARGIN + HALF, EXT_C),
            ):
                c, d = max(lo, shift), min(hi, shift + width)
                pairs.append(
                    (
                        src.at[pl.ds(base + a - SPANS[k][0], b - a), pl.ds(c - lo, d - c), :],
                        r_buf.at[rows, pl.ds(c - shift, d - c), :],
                    )
                )
        return [
            pltpu.make_async_copy(src, dst, r_sem.at[k, n]) for n, (src, dst) in enumerate(pairs)
        ]

    def e_copies(k):
        got = window(SPANS[k], row0, row0 + n_in)
        if first or got is None:
            return []
        a, b = got
        at = a - SPANS[k][0]
        if k in (0, 5):
            src, dst = (field[0] if k == 0 else field[2]), pack.at[0 if k == 0 else 1]
            return [pltpu.make_async_copy(src, dst, e_sem.at[k])]
        src = field[1].at[pl.ds(GROUP * (k - 1) + at, b - a), :, :]
        return [pltpu.make_async_copy(src, e_buf.at[pl.ds(a - row0, b - a), :, :], e_sem.at[k])]

    recorded_in = [r_copies(k) for k in range(6)]
    field_in = [e_copies(k) for k in range(6)]
    for group in field_in + recorded_in:
        for c in group:
            c.start()

    kx = [taps_ref[t : t + 1, :] for t in range(7)]
    ky = [taps_ref[8 + t : 9 + t, :] for t in range(7)]
    col_blocks = blocks_of(width)

    def cols_pass(slot, taps, dst_ref, row):
        for at, size in col_blocks:
            acc = taps[0] * tmp[slot, pl.ds(5 + at, size), :]
            for t in range(1, 7):
                acc = acc + taps[t] * tmp[slot, pl.ds(5 + t + at, size), :]
            dst_ref[row, pl.ds(at, size), :] = acc

    def blur_row(slot, row):
        if first:
            r = r_buf[row]
            e = (r + pltpu.roll(r, Z, 1)) * 0.5
            e_buf[row] = e
        else:
            e = e_buf[row]
        high = e.astype(jnp.bfloat16).astype(jnp.float32)
        split = jnp.where(lower, high, e - high).astype(jnp.bfloat16)
        both = jnp.dot(split, blur_ref[...], preferred_element_type=jnp.float32)
        tmp[slot, pl.ds(8, width), :] = both[:, :LANES] + both[:, LANES:]
        cols_pass(slot, kx, xz_buf, row)

    for slot in range(2):
        tmp[slot, pl.ds(0, 8), :] = jnp.zeros((8, LANES), jnp.float32)
        tmp[slot, pl.ds(8 + width, 8), :] = jnp.zeros((8, LANES), jnp.float32)

    for k in range(6):
        got = window(SPANS[k], row0, row0 + n_in)
        if got is None:
            continue
        for c in recorded_in[k] if first else field_in[k]:
            c.wait()
        base, count = got[0] - row0, got[1] - got[0]

        def body(i, carry, k=k, base=base):
            for slot in range(2):
                row = base + 2 * i + slot
                if not first and k in (0, 5):
                    packed = pack[0 if k == 0 else 1, 2 * i + slot]
                    turned = pltpu.roll(packed, Z, 1)
                    e_buf[row, pl.ds(0, fold), :] = jnp.where(lower[:fold], packed, turned)
                    e_buf[row, pl.ds(fold, fold), :] = jnp.where(lower[:fold], turned, packed)
                blur_row(slot, row)
            return carry

        lax.fori_loop(0, count // 2, body, 0)

    if not first:
        for group in recorded_in:
            for c in group:
                c.wait()

    def rows_pass(src_ref, taps, row, at, size):
        acc = taps[0] * src_ref[row - 3, pl.ds(at, size), :]
        for t in range(1, 7):
            acc = acc + taps[t] * src_ref[row - 3 + t, pl.ds(at, size), :]
        return acc

    def ratio_body(i, carry):
        for slot in range(2):
            row = 3 + 2 * i + slot
            for at, size in col_blocks:
                blurred = rows_pass(xz_buf, ky, row, at, size)
                ratio = r_buf[row, pl.ds(at, size), :] / jnp.maximum(blurred, TINY)
                tmp[slot, pl.ds(8 + at, size), :] = ratio
            cols_pass(slot, kx[::-1], xr_buf, row)
        return carry

    lax.fori_loop(0, (n_in - 6) // 2, ratio_body, 0)

    def update_row(row):
        spread = []
        for at, size in blocks_of(inner, 64):
            spread.append(rows_pass(xr_buf, ky[::-1], row, SIDE + at, size))
        spread = jnp.concatenate(spread, axis=0)
        high = spread.astype(jnp.bfloat16)
        low = (spread - high.astype(jnp.float32)).astype(jnp.bfloat16)
        both = jnp.dot(
            jnp.concatenate([high, low], axis=1), adj_ref[...], preferred_element_type=jnp.float32
        )
        factor = both + pltpu.roll(both, Z, 1)
        return e_buf[row, pl.ds(SIDE, inner), :] * factor

    def update_body(i, carry, base=0):
        for k in range(2):
            y = base + 2 * i + k
            new = update_row(PAD + y)
            if first:
                out_ref[y] = new
            else:
                for j in range(2):
                    flat = out_ref.at[j].reshape(Z * GROUP, CHUNK)
                    flat[pl.ds(y, Z, stride=GROUP), :] = new[j * CHUNK : (j + 1) * CHUNK].T[:Z]
        return carry

    lax.fori_loop(0, n_out // 2, update_body, 0)
    if first:
        for y in range(PAD):
            for ref, row in ((top_ref, y), (low_ref, ROWS - PAD + y)):
                ref[y] = jnp.where(
                    lower[:fold], out_ref[row, pl.ds(0, fold), :], out_ref[row, pl.ds(fold, fold), :]
                )


def iterate(recorded, field, taps, blur, adj, *, first, row0, n_out):
    n_in = n_out + 2 * PAD
    width = EXT_C if first else EXT_C - 2 * SIDE
    fold = (EXT_C - 2 * SIDE) // 2
    pieces = list(recorded) + (list(field) if field is not None else [])
    if not first and row0 >= PAD:
        pieces[0] = pieces[11] = None
    if not first and row0 + n_in <= EXT_R - PAD:
        pieces[10] = pieces[13] = None
    present = tuple(piece is not None for piece in pieces)
    pieces = [piece for piece in pieces if piece is not None]
    if first:
        edge = jax.ShapeDtypeStruct((PAD, fold, LANES), jnp.float32)
        out = (jax.ShapeDtypeStruct((ROWS, EXT_C - 2 * SIDE, LANES), jnp.float32), edge, edge)
        out_specs = (pl.BlockSpec(memory_space=pltpu.VMEM),) * 3
    else:
        out = jax.ShapeDtypeStruct((2, Z, GROUP, CHUNK), jnp.float32)
        out_specs = pl.BlockSpec(memory_space=pltpu.VMEM)
    row = pltpu.VMEM((n_in, width, LANES), jnp.float32)
    vregs = n_in * width // 8
    return pl.pallas_call(
        functools.partial(iterate_kernel, first, row0, n_out, present),
        out_shape=out,
        in_specs=[pl.BlockSpec(memory_space=pl.ANY)] * len(pieces)
        + [pl.BlockSpec(memory_space=pltpu.VMEM)] * 3,
        out_specs=out_specs,
        scratch_shapes=[
            row,
            row,
            row,
            row,
            pltpu.VMEM((2, PAD, fold, LANES), jnp.float32),
            pltpu.VMEM((2, width + 16, LANES), jnp.float32),
            pltpu.SemaphoreType.DMA((6, 3)),
            pltpu.SemaphoreType.DMA((6,)),
        ],
        cost_estimate=pl.CostEstimate(
            flops=vregs * 1024 * 70, bytes_accessed=vregs * 4096 * 3, transcendentals=0
        ),
        compiler_params=params(36 if first else 16),
        name="iterate",
    )(*pieces, taps, blur, adj)


def place_kernel(where_ref, *refs):
    refs[-1][...] = refs[0][0]


def place(where, block, whole, group):
    args = [where, block]
    in_specs = [pl.BlockSpec((1, Z, GROUP, CHUNK), lambda j, w: (j, 0, 0, 0))]
    aliases = {}
    if whole is not None:
        args.append(whole)
        in_specs.append(pl.BlockSpec(memory_space=pl.ANY))
        aliases = {2: 0}
    return pl.pallas_call(
        place_kernel,
        out_shape=jax.ShapeDtypeStruct((Z, ROWS, 2 * HALF), jnp.float32),
        grid_spec=pltpu.PrefetchScalarGridSpec(
            num_scalar_prefetch=1,
            grid=(2,),
            in_specs=in_specs,
            out_specs=pl.BlockSpec((Z, GROUP, CHUNK), lambda j, w: (0, group, 2 * w[0] + j)),
        ),
        input_output_aliases=aliases,
        cost_estimate=pl.CostEstimate(flops=0, bytes_accessed=1 << 20, transcendentals=0),
        compiler_params=params(4),
        name="place",
    )(*args)


def neighbours(views, tiles):
    right = []
    for v in range(views):
        for t in range(tiles):
            if (t + v) % 2 == 0:
                right.append((v * tiles + t, (1 - v) * tiles + t))
            elif t + 1 < tiles:
                right.append((v * tiles + t, v * tiles + t + 1))
    return right


def per_device(views_data, psf_axial, psf_rows, psf_cols):
    views, tiles, bands = lax.axis_size("view"), lax.axis_size("tx"), lax.axis_size("ty")
    swap = [(0, 1), (1, 0)]
    right = neighbours(views, tiles)
    left = [(b, a) for a, b in right]
    down = [(i, i + 1) for i in range(bands - 1)]
    up = [(b, a) for a, b in down]
    half = lax.rem(lax.axis_index("tx") + lax.axis_index("view"), 2)

    def other_rows(*starts):
        at = (1 - half) * HALF
        return jnp.concatenate(
            [
                lax.dynamic_slice(views_data, (0, 0, row, at), (1, Z, rows, HALF))[0]
                for row, rows in starts
            ],
            axis=1,
        )

    border_in = lax.ppermute(other_rows((0, GROUP), (ROWS - GROUP, GROUP)), "view", swap)
    raw = jnp.concatenate([psf_axial[0], psf_rows[0], psf_cols[0]])
    raw_other = lax.ppermute(raw, "view", swap)
    upper, raw_other = lax.optimization_barrier((other_rows((GROUP, GROUP)), raw_other))
    upper_in = lax.ppermute(upper, "view", swap)

    def norm(taps):
        parts = (taps[:21], taps[21:28], taps[28:35])
        return jnp.concatenate([part / jnp.sum(part) for part in parts])

    own, other = norm(raw), norm(raw_other)
    view = lax.axis_index("view")
    lanes = jnp.concatenate(
        [
            jnp.broadcast_to(jnp.where(view == 0, own, other)[:, None], (own.shape[0], Z)),
            jnp.broadcast_to(jnp.where(view == 0, other, own)[:, None], (own.shape[0], Z)),
        ],
        axis=1,
    )
    blur, adj = matrices(lanes[:21])
    taps = jnp.zeros((16, LANES), jnp.float32)
    taps = taps.at[0:7].set(lanes[28:35]).at[8:15].set(lanes[21:28])

    where = jnp.stack([half, view]).astype(jnp.int32)
    there = (1 - half).astype(jnp.int32)[None]

    def widen(block):
        west = lax.ppermute(block[:, HALF - MARGIN :], ("view", "tx"), right)
        east = lax.ppermute(block[:, :MARGIN], ("view", "tx"), left)
        return west, block, east

    border = widen(turn(where, views_data, border_in, 0, 3))
    lower, border = lax.optimization_barrier((other_rows((2 * GROUP, GROUP)), border))
    lower_in = lax.ppermute(lower, "view", swap)

    def edge(rows):
        return jnp.concatenate([part[rows] for part in border], axis=1)

    north = lax.ppermute(edge(slice(2 * GROUP - PAD, 2 * GROUP)), "ty", down)
    south = lax.ppermute(edge(slice(0, PAD)), "ty", up)
    upper = widen(turn(where, views_data, upper_in, 1, 1))
    lower = widen(turn(where, views_data, lower_in, 2, 1))
    recorded = (north,) + border + upper + lower + (south,)

    estimate, top, low = iterate(
        recorded, None, taps, blur, adj, first=True, row0=0, n_out=ROWS
    )
    field = (lax.ppermute(low, "ty", down), estimate, lax.ppermute(top, "ty", up))
    whole = None
    theirs = []
    for group in (1, 2, 0, 3):
        block = iterate(
            recorded, field, taps, blur, adj, first=False, row0=GROUP * group, n_out=GROUP
        )
        theirs.append((group, lax.ppermute(block, "view", swap)))
        whole = place(where[:1], block, whole, group)
    for group, block in theirs:
        whole = place(there, block, whole, group)
    return whole


def solution(mesh):
    placed = (P("view", None, "ty", "tx"), P("view", None), P("view", None), P("view", None))
    return jax.shard_map(
        per_device, mesh=mesh, in_specs=placed, out_specs=P(None, "ty", "tx"), check_vma=False
    )
```

```python
import functools

import jax
import jax.numpy as jnp
from jax import lax
from jax.experimental import pallas as pl
from jax.experimental.pallas import tpu as pltpu
from jax.sharding import PartitionSpec as P

ITERS = 2
Z = 64
LANES = 128
ROWS = 32
HALF = 256
CHUNK = 128
PAD = 6
SIDE = 8
MARGIN = 16
GROUP = 8
EXT_R = ROWS + 2 * PAD
EXT_C = HALF + 2 * MARGIN
MIB = 1024 * 1024
UNROLL = 8
UPDATE = 128
TINY = 1e-30


def params(mib):
    return pltpu.CompilerParams(vmem_limit_bytes=mib * MIB)


def blocks_of(total, largest=96):
    out, at = [], 0
    while at < total:
        size = min(largest, total - at)
        out.append((at, size))
        at += size
    return out


def matrices_kernel(kz_ref, blur_ref, adj_ref):
    taps = kz_ref.shape[0]
    lane = lax.broadcasted_iota(jnp.int32, (Z, LANES), 1)
    row = lax.broadcasted_iota(jnp.int32, (Z, LANES), 0)
    offset = row - lax.rem(lane, Z) + taps // 2
    mat = jnp.zeros((Z, LANES), jnp.float32)
    for t in range(taps):
        mat = mat + jnp.where(offset == t, kz_ref[t : t + 1, :], 0.0)
    high = mat.astype(jnp.bfloat16)
    low = (mat - high.astype(jnp.float32)).astype(jnp.bfloat16)
    blur_ref[0:Z, 0:LANES] = high
    blur_ref[0:Z, LANES:] = low
    blur_ref[Z:, 0:LANES] = high
    blur_ref[Z:, LANES:] = jnp.zeros((Z, LANES), jnp.bfloat16)
    adj = jnp.concatenate([mat, mat], axis=0).T * 0.5
    ahigh = adj.astype(jnp.bfloat16).astype(jnp.float32)
    alow = adj - ahigh
    first = lax.broadcasted_iota(jnp.int32, (LANES, LANES), 1) < Z
    adj_ref[0:LANES, :] = jnp.where(first, ahigh, alow).astype(jnp.bfloat16)
    adj_ref[LANES:, :] = jnp.where(first, ahigh, 0.0).astype(jnp.bfloat16)


def matrices(kz):
    return pl.pallas_call(
        matrices_kernel,
        out_shape=(
            jax.ShapeDtypeStruct((2 * Z, 2 * LANES), jnp.bfloat16),
            jax.ShapeDtypeStruct((2 * LANES, LANES), jnp.bfloat16),
        ),
        compiler_params=params(4),
        name="matrices",
    )(kz)


def turn_kernel(groups, where_ref, own_ref, other_ref, out_ref, west_ref, east_ref, own, other, sems):
    half, first = where_ref[0], where_ref[1] == 0
    blocks = [(i, j) for i in range(len(groups)) for j in range(2)]
    copies = []
    for n, (i, j) in enumerate(blocks):
        at = pl.multiple_of(half * HALF + j * CHUNK, CHUNK)
        mine = own_ref.at[0, :, pl.ds(groups[i] * GROUP, GROUP), pl.ds(at, CHUNK)]
        theirs = other_ref.at[:, pl.ds(i * GROUP, GROUP), pl.ds(j * CHUNK, CHUNK)]
        copies.append(
            (
                pltpu.make_async_copy(mine, own.at[n], sems.at[0, n]),
                pltpu.make_async_copy(theirs, other.at[n], sems.at[1, n]),
            )
        )
    for pair in copies:
        for c in pair:
            c.start()
    for n, (i, j) in enumerate(blocks):
        for c in copies[n]:
            c.wait()
        flat = own.at[n].reshape(Z * GROUP, CHUNK)
        flat_other = other.at[n].reshape(Z * GROUP, CHUNK)
        for y in range(GROUP):
            mine = flat[pl.ds(y, Z, stride=GROUP), :]
            theirs = flat_other[pl.ds(y, Z, stride=GROUP), :]
            pair = jnp.concatenate(
                [jnp.where(first, mine, theirs), jnp.where(first, theirs, mine)], axis=0
            ).T
            row = i * GROUP + y
            out_ref[row, pl.ds(j * CHUNK, CHUNK), :] = pair
            if j == 0:
                east_ref[row] = pair[:MARGIN]
            else:
                west_ref[row] = pair[CHUNK - MARGIN :]


def turn(where, recorded, received, groups):
    rows = len(groups) * GROUP
    block = pltpu.VMEM((2 * len(groups), Z, GROUP, CHUNK), jnp.float32)
    strip = jax.ShapeDtypeStruct((rows, MARGIN, LANES), jnp.float32)
    return pl.pallas_call(
        functools.partial(turn_kernel, groups),
        out_shape=(jax.ShapeDtypeStruct((rows, HALF, LANES), jnp.float32), strip, strip),
        in_specs=[
            pl.BlockSpec(memory_space=pltpu.SMEM),
            pl.BlockSpec(memory_space=pltpu.HBM),
            pl.BlockSpec(memory_space=pl.ANY),
        ],
        out_specs=(pl.BlockSpec(memory_space=pltpu.VMEM),) * 3,
        scratch_shapes=[block, block, pltpu.SemaphoreType.DMA((2, 2 * len(groups)))],
        cost_estimate=pl.CostEstimate(
            flops=0, bytes_accessed=len(groups) << 21, transcendentals=0
        ),
        compiler_params=params(10),
        name="turn",
    )(where, recorded, received)


SPANS = ((0, PAD),) + tuple((PAD + GROUP * g, GROUP) for g in range(4)) + ((EXT_R - PAD, PAD),)
HOMES = (((1, 0), (2, 0), (3, 0)), ((4, 0), (5, 0), (7, 0)), ((4, 8), (6, 0), (7, 8)), ((1, 8), (2, 8), (3, 8)))


def iterate_kernel(first, row0, n_out, present, *refs):
    n_in = n_out + 2 * PAD
    width = EXT_C if first else EXT_C - 2 * SIDE
    shift = 0 if first else SIDE
    inner = width - 2 * SIDE
    fold = (EXT_C - 2 * SIDE) // 2
    pieces = iter(refs)
    taken = [next(pieces) if there else None for there in present]
    recorded, field, refs = taken[:9], taken[9:], tuple(pieces)
    taps_ref, blur_ref, adj_ref = refs[:3]
    refs = refs[3:]
    if first:
        out_ref, top_ref, low_ref = refs[:3]
        refs = refs[3:]
    else:
        out_ref, refs = refs[0], refs[1:]
    r_buf, e_buf, xz_buf, xr_buf, pack, tmp, r_sem, e_sem = refs
    north, south = recorded[0], recorded[8]
    lower = lax.broadcasted_iota(jnp.int32, (width, LANES), 1) < Z

    def window(span, lo, hi):
        at, count = span
        a, b = max(at, lo), min(at + count, hi)
        return (a, b) if a < b else None

    def r_copies(k):
        got = window(SPANS[k], row0 + (0 if first else 3), row0 + n_in - (0 if first else 3))
        if got is None:
            return []
        a, b = got
        rows = pl.ds(a - row0, b - a)
        pairs = []
        if k in (0, 5):
            src = north if k == 0 else south
            pairs.append(
                (
                    src.at[pl.ds(a - SPANS[k][0], b - a), pl.ds(shift, width), :],
                    r_buf.at[rows, :, :],
                )
            )
        else:
            ranges = ((0, MARGIN), (MARGIN, MARGIN + HALF), (MARGIN + HALF, EXT_C))
            for (home, base), (lo, hi) in zip(HOMES[k - 1], ranges):
                src = recorded[home]
                c, d = max(lo, shift), min(hi, shift + width)
                pairs.append(
                    (
                        src.at[pl.ds(base + a - SPANS[k][0], b - a), pl.ds(c - lo, d - c), :],
                        r_buf.at[rows, pl.ds(c - shift, d - c), :],
                    )
                )
        return [
            pltpu.make_async_copy(src, dst, r_sem.at[k, n]) for n, (src, dst) in enumerate(pairs)
        ]

    def e_copies(k):
        got = window(SPANS[k], row0, row0 + n_in)
        if first or got is None:
            return []
        a, b = got
        at = a - SPANS[k][0]
        if k in (0, 5):
            src, dst = (field[0] if k == 0 else field[2]), pack.at[0 if k == 0 else 1]
            return [pltpu.make_async_copy(src, dst, e_sem.at[k])]
        src = field[1].at[pl.ds(GROUP * (k - 1) + at, b - a), :, :]
        return [pltpu.make_async_copy(src, e_buf.at[pl.ds(a - row0, b - a), :, :], e_sem.at[k])]

    recorded_in = [r_copies(k) for k in range(6)]
    field_in = [e_copies(k) for k in range(6)]
    for group in field_in + recorded_in:
        for c in group:
            c.start()

    def over_rows(start, count, steps, unroll):
        def rows_from(at, many):
            for step in steps:
                for slot in range(many):
                    step(slot, at + slot)

        def body(i, carry):
            rows_from(start + unroll * i, unroll)
            return carry

        lax.fori_loop(0, count // unroll, body, 0)
        if count % unroll:
            rows_from(start + count - count % unroll, count % unroll)

    kx = [taps_ref[t : t + 1, :] for t in range(7)]
    ky = [taps_ref[8 + t : 9 + t, :] for t in range(7)]
    col_blocks = blocks_of(width)

    def cols_pass(slot, taps, dst_ref, row):
        for at, size in col_blocks:
            acc = taps[0] * tmp[slot, pl.ds(5 + at, size), :]
            for t in range(1, 7):
                acc = acc + taps[t] * tmp[slot, pl.ds(5 + t + at, size), :]
            dst_ref[row, pl.ds(at, size), :] = acc

    def blur_row(slot, row):
        if first:
            r = r_buf[row]
            e = (r + pltpu.roll(r, Z, 1)) * 0.5
            e_buf[row] = e
        else:
            e = e_buf[row]
        high = e.astype(jnp.bfloat16).astype(jnp.float32)
        split = jnp.where(lower, high, e - high).astype(jnp.bfloat16)
        both = jnp.dot(split, blur_ref[...], preferred_element_type=jnp.float32)
        tmp[slot, pl.ds(8, width), :] = both[:, :LANES] + both[:, LANES:]

    for slot in range(UNROLL):
        tmp[slot, pl.ds(0, 8), :] = jnp.zeros((8, LANES), jnp.float32)
        tmp[slot, pl.ds(8 + width, 8), :] = jnp.zeros((8, LANES), jnp.float32)

    for k in range(6):
        got = window(SPANS[k], row0, row0 + n_in)
        if got is None:
            continue
        for c in recorded_in[k] if first else field_in[k]:
            c.wait()
        base, count = got[0] - row0, got[1] - got[0]

        def halo_row(slot, row, k=k, base=base):
            if not first and k in (0, 5):
                packed = pack[0 if k == 0 else 1, row - base]
                turned = pltpu.roll(packed, Z, 1)
                e_buf[row, pl.ds(0, fold), :] = jnp.where(lower[:fold], packed, turned)
                e_buf[row, pl.ds(fold, fold), :] = jnp.where(lower[:fold], turned, packed)
            blur_row(slot, row)

        over_rows(base, count, (halo_row, lambda slot, row: cols_pass(slot, kx, xz_buf, row)), UNROLL)

    if not first:
        for group in recorded_in:
            for c in group:
                c.wait()

    def rows_pass(src_ref, taps, row, at, size):
        acc = taps[0] * src_ref[row - 3, pl.ds(at, size), :]
        for t in range(1, 7):
            acc = acc + taps[t] * src_ref[row - 3 + t, pl.ds(at, size), :]
        return acc

    def ratio_row(slot, row):
        for at, size in col_blocks:
            blurred = rows_pass(xz_buf, ky, row, at, size)
            ratio = r_buf[row, pl.ds(at, size), :] / jnp.maximum(blurred, TINY)
            tmp[slot, pl.ds(8 + at, size), :] = ratio

    over_rows(3, n_in - 6, (ratio_row, lambda slot, row: cols_pass(slot, kx[::-1], xr_buf, row)), UNROLL)

    def update_row(slot, y):
        row = PAD + y
        for at, size in blocks_of(inner, UPDATE):
            spread = rows_pass(xr_buf, ky[::-1], row, SIDE + at, size)
            high = spread.astype(jnp.bfloat16)
            low = (spread - high.astype(jnp.float32)).astype(jnp.bfloat16)
            both = jnp.dot(
                jnp.concatenate([high, low], axis=1),
                adj_ref[...],
                preferred_element_type=jnp.float32,
            )
            factor = both + pltpu.roll(both, Z, 1)
            new = e_buf[row, pl.ds(SIDE + at, size), :] * factor
            if first:
                out_ref[y, pl.ds(at, size), :] = new
            else:
                flat = out_ref.at[at // CHUNK].reshape(Z * GROUP, CHUNK)
                flat[pl.ds(y, Z, stride=GROUP), :] = new.T[:Z]

    over_rows(0, n_out, (update_row,), UNROLL)
    if first:
        for y in range(PAD):
            for ref, row in ((top_ref, y), (low_ref, ROWS - PAD + y)):
                ref[y] = jnp.where(
                    lower[:fold], out_ref[row, pl.ds(0, fold), :], out_ref[row, pl.ds(fold, fold), :]
                )


def iterate(recorded, field, taps, blur, adj, *, first, row0, n_out):
    n_in = n_out + 2 * PAD
    width = EXT_C if first else EXT_C - 2 * SIDE
    fold = (EXT_C - 2 * SIDE) // 2
    pieces = list(recorded) + (list(field) if field is not None else [])
    if not first and row0 >= PAD:
        pieces[0] = pieces[9] = None
    if not first and row0 + n_in <= EXT_R - PAD:
        pieces[8] = pieces[11] = None
    present = tuple(piece is not None for piece in pieces)
    pieces = [piece for piece in pieces if piece is not None]
    if first:
        edge = jax.ShapeDtypeStruct((PAD, fold, LANES), jnp.float32)
        out = (jax.ShapeDtypeStruct((ROWS, EXT_C - 2 * SIDE, LANES), jnp.float32), edge, edge)
        out_specs = (pl.BlockSpec(memory_space=pltpu.VMEM),) * 3
    else:
        out = jax.ShapeDtypeStruct((2, Z, GROUP, CHUNK), jnp.float32)
        out_specs = pl.BlockSpec(memory_space=pltpu.VMEM)
    row = pltpu.VMEM((n_in, width, LANES), jnp.float32)
    vregs = n_in * width // 8
    return pl.pallas_call(
        functools.partial(iterate_kernel, first, row0, n_out, present),
        out_shape=out,
        in_specs=[pl.BlockSpec(memory_space=pl.ANY)] * len(pieces)
        + [pl.BlockSpec(memory_space=pltpu.VMEM)] * 3,
        out_specs=out_specs,
        scratch_shapes=[
            row,
            row,
            row,
            row,
            pltpu.VMEM((2, PAD, fold, LANES), jnp.float32),
            pltpu.VMEM((UNROLL, width + 16, LANES), jnp.float32),
            pltpu.SemaphoreType.DMA((6, 3)),
            pltpu.SemaphoreType.DMA((6,)),
        ],
        cost_estimate=pl.CostEstimate(
            flops=0, bytes_accessed=vregs * 4096 if first else 4096, transcendentals=0
        ),
        compiler_params=params(30 if first else 13),
        name="iterate",
    )(*pieces, taps, blur, adj)


def place_kernel(where_ref, *refs):
    refs[-1][...] = refs[0][0]


def place(where, block, whole, group):
    args = [where, block]
    in_specs = [pl.BlockSpec((1, Z, GROUP, CHUNK), lambda j, w: (j, 0, 0, 0))]
    aliases = {}
    if whole is not None:
        args.append(whole)
        in_specs.append(pl.BlockSpec(memory_space=pl.ANY))
        aliases = {2: 0}
    return pl.pallas_call(
        place_kernel,
        out_shape=jax.ShapeDtypeStruct((Z, ROWS, 2 * HALF), jnp.float32),
        grid_spec=pltpu.PrefetchScalarGridSpec(
            num_scalar_prefetch=1,
            grid=(2,),
            in_specs=in_specs,
            out_specs=pl.BlockSpec((Z, GROUP, CHUNK), lambda j, w: (0, group, 2 * w[0] + j)),
        ),
        input_output_aliases=aliases,
        cost_estimate=pl.CostEstimate(flops=0, bytes_accessed=1 << 20, transcendentals=0),
        compiler_params=params(4),
        name="place",
    )(*args)


def neighbours(views, tiles):
    right = []
    for v in range(views):
        for t in range(tiles):
            if (t + v) % 2 == 0:
                right.append((v * tiles + t, (1 - v) * tiles + t))
            elif t + 1 < tiles:
                right.append((v * tiles + t, v * tiles + t + 1))
    return right


def per_device(views_data, psf_axial, psf_rows, psf_cols):
    views, tiles, bands = lax.axis_size("view"), lax.axis_size("tx"), lax.axis_size("ty")
    swap = [(0, 1), (1, 0)]
    right = neighbours(views, tiles)
    left = [(b, a) for a, b in right]
    down = [(i, i + 1) for i in range(bands - 1)]
    up = [(b, a) for a, b in down]
    half = lax.rem(lax.axis_index("tx") + lax.axis_index("view"), 2)

    def other_rows(views_data, *starts):
        at = (1 - half) * HALF
        return jnp.concatenate(
            [
                lax.dynamic_slice(views_data, (0, 0, row, at), (1, Z, rows, HALF))[0]
                for row, rows in starts
            ],
            axis=1,
        )

    raw = jnp.concatenate([psf_axial[0], psf_rows[0], psf_cols[0]])
    raw_other = lax.ppermute(raw, "view", swap)
    border = other_rows(views_data, (0, GROUP), (ROWS - GROUP, GROUP))
    raw, border = lax.optimization_barrier((raw, border))
    border_in = lax.ppermute(border, "view", swap)
    later, border = lax.optimization_barrier((views_data, border))
    upper_in = lax.ppermute(other_rows(later, (GROUP, GROUP)), "view", swap)

    def norm(taps):
        parts = (taps[:21], taps[21:28], taps[28:35])
        return jnp.concatenate([part / jnp.sum(part) for part in parts])

    own, other = norm(raw), norm(raw_other)
    view = lax.axis_index("view")
    lanes = jnp.concatenate(
        [
            jnp.broadcast_to(jnp.where(view == 0, own, other)[:, None], (own.shape[0], Z)),
            jnp.broadcast_to(jnp.where(view == 0, other, own)[:, None], (own.shape[0], Z)),
        ],
        axis=1,
    )
    blur, adj = matrices(lanes[:21])
    taps = jnp.zeros((16, LANES), jnp.float32)
    taps = taps.at[0:7].set(lanes[28:35]).at[8:15].set(lanes[21:28])

    where = jnp.stack([half, view]).astype(jnp.int32)
    there = (1 - half).astype(jnp.int32)[None]

    def sides(west, east):
        return lax.ppermute(west, ("view", "tx"), right), lax.ppermute(east, ("view", "tx"), left)

    middle, to_east, to_west = turn(where, views_data, border_in, (0, 3))
    west, east = sides(to_east, to_west)
    last, west, east = lax.optimization_barrier(
        (other_rows(later, (2 * GROUP, GROUP)), west, east)
    )
    border = (west, middle, east)
    lower_in = lax.ppermute(last, "view", swap)

    def edge(rows):
        return jnp.concatenate([part[rows] for part in border], axis=1)

    north = lax.ppermute(edge(slice(2 * GROUP - PAD, 2 * GROUP)), "ty", down)
    south = lax.ppermute(edge(slice(0, PAD)), "ty", up)
    upper, upper_east, upper_west = turn(where, views_data, upper_in, (1,))
    lower, lower_east, lower_west = turn(where, views_data, lower_in, (2,))
    west, east = sides(
        jnp.concatenate([upper_east, lower_east]), jnp.concatenate([upper_west, lower_west])
    )
    recorded = (north,) + border + (west, upper, lower, east, south)

    estimate, top, low = iterate(
        recorded, None, taps, blur, adj, first=True, row0=0, n_out=ROWS
    )
    def piece(group, field):
        return iterate(
            recorded, field, taps, blur, adj, first=False, row0=GROUP * group, n_out=GROUP
        )

    field = (lax.ppermute(low, "ty", down), estimate, lax.ppermute(top, "ty", up))
    theirs = []
    whole = None
    for group in (1, 2, 0, 3):
        block = piece(group, field)
        theirs.append((group, lax.ppermute(block, "view", swap)))
        whole = place(where[:1], block, whole, group)
    for group, block in theirs:
        whole = place(there, block, whole, group)
    return whole


def solution(mesh):
    placed = (P("view", None, "ty", "tx"), P("view", None), P("view", None), P("view", None))
    return jax.shard_map(
        per_device, mesh=mesh, in_specs=placed, out_specs=P(None, "ty", "tx"), check_vma=False
    )
```

```python
import functools

import jax
import jax.numpy as jnp
from jax import lax
from jax.experimental import pallas as pl
from jax.experimental.pallas import tpu as pltpu
from jax.sharding import PartitionSpec as P

ITERS = 2
Z = 64
LANES = 128
ROWS = 32
HALF = 256
CHUNK = 128
PAD = 6
REACH = 3
SIDE = 8
MARGIN = 16
GROUP = 8
EXT_R = ROWS + 2 * PAD
EXT_C = HALF + 2 * MARGIN
MIB = 1024 * 1024
UNROLL = 8
UPDATE = 128
TINY = 1e-30


def params(mib):
    return pltpu.CompilerParams(vmem_limit_bytes=mib * MIB)


def in_hbm(array):
    return pltpu.with_memory_space_constraint(array, pltpu.HBM)


def blocks_of(total, largest=96):
    out, at = [], 0
    while at < total:
        size = min(largest, total - at)
        out.append((at, size))
        at += size
    return out


def matrices_kernel(kz_ref, blur_ref, adj_ref):
    taps = kz_ref.shape[0]
    lane = lax.broadcasted_iota(jnp.int32, (Z, LANES), 1)
    row = lax.broadcasted_iota(jnp.int32, (Z, LANES), 0)
    offset = row - lax.rem(lane, Z) + taps // 2
    mat = jnp.zeros((Z, LANES), jnp.float32)
    for t in range(taps):
        mat = mat + jnp.where(offset == t, kz_ref[t : t + 1, :], 0.0)
    high = mat.astype(jnp.bfloat16)
    low = (mat - high.astype(jnp.float32)).astype(jnp.bfloat16)
    blur_ref[0:Z, 0:LANES] = high
    blur_ref[0:Z, LANES:] = low
    blur_ref[Z:, 0:LANES] = high
    blur_ref[Z:, LANES:] = jnp.zeros((Z, LANES), jnp.bfloat16)
    adj = jnp.concatenate([mat, mat], axis=0).T * 0.5
    ahigh = adj.astype(jnp.bfloat16).astype(jnp.float32)
    alow = adj - ahigh
    first = lax.broadcasted_iota(jnp.int32, (LANES, LANES), 1) < Z
    adj_ref[0:LANES, :] = jnp.where(first, ahigh, alow).astype(jnp.bfloat16)
    adj_ref[LANES:, :] = jnp.where(first, ahigh, 0.0).astype(jnp.bfloat16)


def matrices(kz):
    return pl.pallas_call(
        matrices_kernel,
        out_shape=(
            jax.ShapeDtypeStruct((2 * Z, 2 * LANES), jnp.bfloat16),
            jax.ShapeDtypeStruct((2 * LANES, LANES), jnp.bfloat16),
        ),
        compiler_params=params(4),
        name="matrices",
    )(kz)


def turn_kernel(groups, where_ref, own_ref, other_ref, out_ref, west_ref, east_ref, *refs):
    own, other, sems = refs[-3:]
    half, first = where_ref[0], where_ref[1] == 0
    blocks = [(i, j) for i in range(len(groups)) for j in range(2)]
    copies = []
    for n, (i, j) in enumerate(blocks):
        at = pl.multiple_of(half * HALF + j * CHUNK, CHUNK)
        mine = own_ref.at[0, :, pl.ds(groups[i] * GROUP, GROUP), pl.ds(at, CHUNK)]
        theirs = other_ref.at[:, pl.ds(i * GROUP, GROUP), pl.ds(j * CHUNK, CHUNK)]
        copies.append(
            (
                pltpu.make_async_copy(mine, own.at[n], sems.at[0, n]),
                pltpu.make_async_copy(theirs, other.at[n], sems.at[1, n]),
            )
        )
    for pair in copies:
        for c in pair:
            c.start()
    for n, (i, j) in enumerate(blocks):
        for c in copies[n]:
            c.wait()
        flat = own.at[n].reshape(Z * GROUP, CHUNK)
        flat_other = other.at[n].reshape(Z * GROUP, CHUNK)
        for y in range(GROUP):
            mine = flat[pl.ds(y, Z, stride=GROUP), :]
            theirs = flat_other[pl.ds(y, Z, stride=GROUP), :]
            pair = jnp.concatenate(
                [jnp.where(first, mine, theirs), jnp.where(first, theirs, mine)], axis=0
            ).T
            row = i * GROUP + y
            out_ref[row, pl.ds(j * CHUNK, CHUNK), :] = pair
            if j == 0:
                east_ref[row] = pair[:MARGIN]
            else:
                west_ref[row] = pair[CHUNK - MARGIN :]
    if len(groups) == 1:
        return
    up_ref, down_ref = refs[:2]
    lower = lax.broadcasted_iota(jnp.int32, (CHUNK, LANES), 1) < Z
    low = 2 * GROUP - PAD
    for ref, near, far in ((up_ref, 0, REACH), (down_ref, low + REACH, low)):
        for y in range(REACH):
            ref[y, pl.ds(0, HALF), :] = out_ref[near + y]
            ends = []
            for j in range(2):
                r = out_ref[far + y, pl.ds(j * CHUNK, CHUNK), :]
                ends.append((r + pltpu.roll(r, Z, 1)) * 0.5)
            ref[y, pl.ds(HALF, CHUNK), :] = jnp.where(lower, ends[0], ends[1])


def turn(where, recorded, received, groups):
    rows = len(groups) * GROUP
    block = pltpu.VMEM((2 * len(groups), Z, GROUP, CHUNK), jnp.float32)
    strip = jax.ShapeDtypeStruct((rows, MARGIN, LANES), jnp.float32)
    out = [jax.ShapeDtypeStruct((rows, HALF, LANES), jnp.float32), strip, strip]
    if len(groups) > 1:
        out += [jax.ShapeDtypeStruct((REACH, HALF + CHUNK, LANES), jnp.float32)] * 2
    return pl.pallas_call(
        functools.partial(turn_kernel, groups),
        out_shape=tuple(out),
        in_specs=[
            pl.BlockSpec(memory_space=pltpu.SMEM),
            pl.BlockSpec(memory_space=pltpu.HBM),
            pl.BlockSpec(memory_space=pl.ANY),
        ],
        out_specs=(pl.BlockSpec(memory_space=pltpu.VMEM),) * len(out),
        scratch_shapes=[block, block, pltpu.SemaphoreType.DMA((2, 2 * len(groups)))],
        cost_estimate=pl.CostEstimate(
            flops=0, bytes_accessed=1024, transcendentals=0
        ),
        compiler_params=params(10),
        name="turn",
    )(where, in_hbm(recorded), received)


GROUPS = tuple((PAD + GROUP * g, GROUP) for g in range(4))
SPANS = ((REACH, REACH),) + GROUPS + ((EXT_R - PAD, REACH),)
FIRST_SPANS = ((0, REACH),) + SPANS + ((EXT_R - REACH, REACH),)
NEXT_SPANS = ((0, PAD),) + GROUPS + ((EXT_R - PAD, PAD),)
HOMES = (
    ((2, 8), (0, 0), (7, 8)),
    ((1, 0), (3, 0), (6, 0)),
    ((1, 16), (4, 0), (6, 16)),
    ((2, 0), (5, 0), (7, 0)),
    ((1, 8), (3, 8), (6, 8)),
    ((2, 14), (8, 0), (7, 14)),
)
OUTER = (11, 17)


def iterate_kernel(first, row0, n_out, present, *refs):
    n_in = n_out + 2 * PAD
    width = EXT_C if first else EXT_C - 2 * SIDE
    shift = 0 if first else SIDE
    inner = width - 2 * SIDE
    fold = (EXT_C - 2 * SIDE) // 2
    pieces = iter(refs)
    taken = [next(pieces) if there else None for there in present]
    recorded, field, refs = taken[:9], taken[9:], tuple(pieces)
    taps_ref, blur_hbm, adj_hbm = refs[:3]
    refs = refs[3:]
    if first:
        out_ref, top_ref, low_ref = refs[:3]
        refs = refs[3:]
    else:
        out_ref, refs = refs[0], refs[1:]
    r_buf, e_buf, xz_buf, xr_buf, pack, tmp, blur_ref, adj_ref, r_sem, e_sem, m_sem = refs
    north, south = recorded[0], recorded[8]
    lower = lax.broadcasted_iota(jnp.int32, (width, LANES), 1) < Z

    def window(span, lo, hi):
        at, count = span
        a, b = max(at, lo), min(at + count, hi)
        return (a, b) if a < b else None

    def r_copies(k):
        got = window(SPANS[k], row0 + REACH, row0 + n_in - REACH)
        if got is None:
            return []
        a, b = got
        rows = pl.ds(a - row0, b - a)
        pairs = []
        ranges = ((0, MARGIN), (MARGIN, MARGIN + HALF), (MARGIN + HALF, EXT_C))
        for (home, base), (lo, hi) in zip(HOMES[k], ranges):
            src = recorded[home]
            c, d = max(lo, shift), min(hi, shift + width)
            pairs.append(
                (
                    src.at[pl.ds(base + a - SPANS[k][0], b - a), pl.ds(c - lo, d - c), :],
                    r_buf.at[rows, pl.ds(c - shift, d - c), :],
                )
            )
        return [
            pltpu.make_async_copy(src, dst, r_sem.at[k, n]) for n, (src, dst) in enumerate(pairs)
        ]

    def e_copies(k):
        if first:
            if 0 < k < 7:
                return []
            n = 0 if k == 0 else 1
            halo, rows = (north if n == 0 else south), pl.ds(OUTER[n], REACH)
            pairs = (
                (recorded[2].at[rows, :, :], pl.ds(0, MARGIN)),
                (halo.at[:, pl.ds(HALF, CHUNK), :], pl.ds(MARGIN, CHUNK)),
                (recorded[7].at[rows, :, :], pl.ds(MARGIN + CHUNK, MARGIN)),
            )
            return [
                pltpu.make_async_copy(src, pack.at[n, :, cols, :], e_sem.at[k, i])
                for i, (src, cols) in enumerate(pairs)
            ]
        got = window(NEXT_SPANS[k], row0, row0 + n_in)
        if got is None:
            return []
        a, b = got
        if k in (0, 5):
            src, dst = (field[0] if k == 0 else field[2]), pack.at[0 if k == 0 else 1]
        else:
            at = GROUP * (k - 1) + a - NEXT_SPANS[k][0]
            src, dst = field[1].at[pl.ds(at, b - a), :, :], e_buf.at[pl.ds(a - row0, b - a), :, :]
        return [pltpu.make_async_copy(src, dst, e_sem.at[k, 0])]

    recorded_in = [r_copies(k) for k in range(6)]
    e_spans = FIRST_SPANS if first else NEXT_SPANS
    field_in = [e_copies(k) for k in range(len(e_spans))]
    matrices_in = [
        pltpu.make_async_copy(blur_hbm, blur_ref, m_sem.at[0]),
        pltpu.make_async_copy(adj_hbm, adj_ref, m_sem.at[1]),
    ]
    for group in [matrices_in] + field_in + recorded_in:
        for c in group:
            c.start()

    def over_rows(start, count, steps, unroll):
        def rows_from(at, many):
            for step in steps:
                for slot in range(many):
                    step(slot, at + slot)

        def body(i, carry):
            rows_from(start + unroll * i, unroll)
            return carry

        lax.fori_loop(0, count // unroll, body, 0)
        if count % unroll:
            rows_from(start + count - count % unroll, count % unroll)

    kx = [taps_ref[t : t + 1, :] for t in range(7)]
    ky = [taps_ref[8 + t : 9 + t, :] for t in range(7)]
    col_blocks = blocks_of(width)

    def cols_pass(slot, taps, dst_ref, row):
        for at, size in col_blocks:
            acc = taps[0] * tmp[slot, pl.ds(5 + at, size), :]
            for t in range(1, 7):
                acc = acc + taps[t] * tmp[slot, pl.ds(5 + t + at, size), :]
            dst_ref[row, pl.ds(at, size), :] = acc

    def blur_row(slot, row, started):
        if not started:
            r = r_buf[row]
            e = (r + pltpu.roll(r, Z, 1)) * 0.5
            e_buf[row] = e
        else:
            e = e_buf[row]
        high = e.astype(jnp.bfloat16).astype(jnp.float32)
        split = jnp.where(lower, high, e - high).astype(jnp.bfloat16)
        both = jnp.dot(split, blur_ref[...], preferred_element_type=jnp.float32)
        tmp[slot, pl.ds(8, width), :] = both[:, :LANES] + both[:, LANES:]

    for slot in range(UNROLL):
        tmp[slot, pl.ds(0, 8), :] = jnp.zeros((8, LANES), jnp.float32)
        tmp[slot, pl.ds(8 + width, 8), :] = jnp.zeros((8, LANES), jnp.float32)

    def both_halves(packed, turned, size, low_first):
        keep = lower[:size] if low_first else jnp.logical_not(lower[:size])
        return jnp.where(keep, packed, turned)

    for c in matrices_in:
        c.wait()
    for k, span in enumerate(e_spans):
        got = window(span, row0, row0 + n_in)
        if got is None:
            continue
        for c in field_in[k]:
            c.wait()
        halo = k in (0, len(e_spans) - 1)
        if first and not halo:
            for c in recorded_in[k - 1]:
                c.wait()
        base, count = got[0] - row0, got[1] - got[0]

        def halo_row(slot, row, halo=halo, k=k, base=base):
            if halo:
                packed = pack[0 if k == 0 else 1, row - base]
                turned = pltpu.roll(packed, Z, 1)
                if first:
                    parts = (
                        (0, 0, MARGIN, False),
                        (MARGIN, MARGIN, CHUNK, True),
                        (MARGIN + CHUNK, MARGIN, CHUNK, False),
                        (MARGIN + HALF, MARGIN + CHUNK, MARGIN, True),
                    )
                else:
                    parts = ((0, 0, fold, True), (fold, 0, fold, False))
                for to, at, size, low_first in parts:
                    e_buf[row, pl.ds(to, size), :] = both_halves(
                        packed[at : at + size], turned[at : at + size], size, low_first
                    )
            blur_row(slot, row, halo or not first)

        over_rows(
            base,
            count,
            (halo_row, lambda slot, row: cols_pass(slot, kx, xz_buf, row)),
            UNROLL,
        )

    if not first:
        for group in recorded_in:
            for c in group:
                c.wait()

    def rows_pass(src_ref, taps, row, at, size):
        acc = taps[0] * src_ref[row - 3, pl.ds(at, size), :]
        for t in range(1, 7):
            acc = acc + taps[t] * src_ref[row - 3 + t, pl.ds(at, size), :]
        return acc

    def ratio_row(slot, row):
        for at, size in col_blocks:
            blurred = rows_pass(xz_buf, ky, row, at, size)
            ratio = r_buf[row, pl.ds(at, size), :] / jnp.maximum(blurred, TINY)
            tmp[slot, pl.ds(8 + at, size), :] = ratio

    over_rows(3, n_in - 6, (ratio_row, lambda slot, row: cols_pass(slot, kx[::-1], xr_buf, row)), UNROLL)

    def update_row(slot, y):
        row = PAD + y
        for at, size in blocks_of(inner, UPDATE):
            spread = rows_pass(xr_buf, ky[::-1], row, SIDE + at, size)
            high = spread.astype(jnp.bfloat16)
            low = (spread - high.astype(jnp.float32)).astype(jnp.bfloat16)
            both = jnp.dot(
                jnp.concatenate([high, low], axis=1),
                adj_ref[...],
                preferred_element_type=jnp.float32,
            )
            factor = both + pltpu.roll(both, Z, 1)
            new = e_buf[row, pl.ds(SIDE + at, size), :] * factor
            if first:
                out_ref[y, pl.ds(at, size), :] = new
            else:
                flat = out_ref.at[at // CHUNK].reshape(Z * GROUP, CHUNK)
                flat[pl.ds(y, Z, stride=GROUP), :] = new.T[:Z]

    over_rows(0, n_out, (update_row,), UNROLL)
    if first:
        for y in range(PAD):
            for ref, row in ((top_ref, y), (low_ref, ROWS - PAD + y)):
                ref[y] = jnp.where(
                    lower[:fold], out_ref[row, pl.ds(0, fold), :], out_ref[row, pl.ds(fold, fold), :]
                )


def iterate(recorded, field, taps, blur, adj, *, first, row0, n_out):
    n_in = n_out + 2 * PAD
    width = EXT_C if first else EXT_C - 2 * SIDE
    fold = (EXT_C - 2 * SIDE) // 2
    pieces = list(recorded) + (list(field) if field is not None else [])
    if not first and row0 >= PAD:
        pieces[0] = pieces[9] = None
    if not first and row0 + n_in <= EXT_R - PAD:
        pieces[8] = pieces[11] = None
    for k in (0, 5, 8):
        if pieces[k] is not None:
            pieces[k] = in_hbm(pieces[k])
    present = tuple(piece is not None for piece in pieces)
    pieces = [piece for piece in pieces if piece is not None]
    if first:
        edge = jax.ShapeDtypeStruct((PAD, fold, LANES), jnp.float32)
        out = (jax.ShapeDtypeStruct((ROWS, EXT_C - 2 * SIDE, LANES), jnp.float32), edge, edge)
        out_specs = (pl.BlockSpec(memory_space=pltpu.VMEM),) * 3
    else:
        out = jax.ShapeDtypeStruct((2, Z, GROUP, CHUNK), jnp.float32)
        out_specs = pl.BlockSpec(memory_space=pltpu.VMEM)
    row = pltpu.VMEM((n_in, width, LANES), jnp.float32)
    vregs = n_in * width // 8
    return pl.pallas_call(
        functools.partial(iterate_kernel, first, row0, n_out, present),
        out_shape=out,
        in_specs=[pl.BlockSpec(memory_space=pl.ANY)] * len(pieces)
        + [pl.BlockSpec(memory_space=pltpu.VMEM)]
        + [pl.BlockSpec(memory_space=pl.ANY)] * 2,
        out_specs=out_specs,
        scratch_shapes=[
            row,
            row,
            row,
            row,
            pltpu.VMEM(
                (2, REACH, CHUNK + 2 * MARGIN, LANES) if first else (2, PAD, fold, LANES),
                jnp.float32,
            ),
            pltpu.VMEM((UNROLL, width + 16, LANES), jnp.float32),
            pltpu.VMEM((2 * Z, 2 * LANES), jnp.bfloat16),
            pltpu.VMEM((2 * LANES, LANES), jnp.bfloat16),
            pltpu.SemaphoreType.DMA((6, 3)),
            pltpu.SemaphoreType.DMA((8, 3)),
            pltpu.SemaphoreType.DMA((2,)),
        ],
        cost_estimate=pl.CostEstimate(
            flops=0, bytes_accessed=vregs * 4096 if first else 4096, transcendentals=0
        ),
        compiler_params=params(30 if first else 13),
        name="iterate",
    )(*pieces, taps, in_hbm(blur), in_hbm(adj))


def place_kernel(where_ref, *refs):
    refs[-1][...] = refs[0][0]


def place(where, block, whole, group):
    args = [where, block]
    in_specs = [pl.BlockSpec((1, Z, GROUP, CHUNK), lambda j, w: (j, 0, 0, 0))]
    aliases = {}
    if whole is not None:
        args.append(whole)
        in_specs.append(pl.BlockSpec(memory_space=pl.ANY))
        aliases = {2: 0}
    return pl.pallas_call(
        place_kernel,
        out_shape=jax.ShapeDtypeStruct((Z, ROWS, 2 * HALF), jnp.float32),
        grid_spec=pltpu.PrefetchScalarGridSpec(
            num_scalar_prefetch=1,
            grid=(2,),
            in_specs=in_specs,
            out_specs=pl.BlockSpec((Z, GROUP, CHUNK), lambda j, w: (0, group, 2 * w[0] + j)),
        ),
        input_output_aliases=aliases,
        cost_estimate=pl.CostEstimate(flops=0, bytes_accessed=1 << 20, transcendentals=0),
        compiler_params=params(4),
        name="place",
    )(*args)


def neighbours(views, tiles):
    right = []
    for v in range(views):
        for t in range(tiles):
            if (t + v) % 2 == 0:
                right.append((v * tiles + t, (1 - v) * tiles + t))
            elif t + 1 < tiles:
                right.append((v * tiles + t, v * tiles + t + 1))
    return right


def per_device(views_data, psf_axial, psf_rows, psf_cols):
    views, tiles, bands = lax.axis_size("view"), lax.axis_size("tx"), lax.axis_size("ty")
    swap = [(0, 1), (1, 0)]
    right = neighbours(views, tiles)
    left = [(b, a) for a, b in right]
    down = [(i, i + 1) for i in range(bands - 1)]
    up = [(b, a) for a, b in down]
    half = lax.rem(lax.axis_index("tx") + lax.axis_index("view"), 2)

    def other_rows(views_data, *starts):
        at = (1 - half) * HALF
        return jnp.concatenate(
            [
                lax.dynamic_slice(views_data, (0, 0, row, at), (1, Z, rows, HALF))[0]
                for row, rows in starts
            ],
            axis=1,
        )

    raw = jnp.concatenate([psf_axial[0], psf_rows[0], psf_cols[0]])
    raw_other = lax.ppermute(raw, "view", swap)
    border = other_rows(views_data, (0, GROUP), (ROWS - GROUP, GROUP))
    raw, border = lax.optimization_barrier((raw, border))
    border_in = lax.ppermute(border, "view", swap)
    later, border = lax.optimization_barrier((views_data, border))
    upper_in = lax.ppermute(other_rows(later, (GROUP, GROUP)), "view", swap)
    lower_in = lax.ppermute(other_rows(later, (2 * GROUP, GROUP)), "view", swap)

    def norm(taps):
        parts = (taps[:21], taps[21:28], taps[28:35])
        return jnp.concatenate([part / jnp.sum(part) for part in parts])

    own, other = norm(raw), norm(raw_other)
    view = lax.axis_index("view")
    lanes = jnp.concatenate(
        [
            jnp.broadcast_to(jnp.where(view == 0, own, other)[:, None], (own.shape[0], Z)),
            jnp.broadcast_to(jnp.where(view == 0, other, own)[:, None], (own.shape[0], Z)),
        ],
        axis=1,
    )
    blur, adj = matrices(lanes[:21])
    taps = jnp.zeros((16, LANES), jnp.float32)
    taps = taps.at[0:7].set(lanes[28:35]).at[8:15].set(lanes[21:28])

    where = jnp.stack([half, view]).astype(jnp.int32)
    there = (1 - half).astype(jnp.int32)[None]

    def sides(west, east):
        return lax.ppermute(west, ("view", "tx"), right), lax.ppermute(east, ("view", "tx"), left)

    border, border_east, border_west, to_up, to_down = turn(where, views_data, border_in, (0, 3))
    north = lax.ppermute(to_down, "ty", down)
    south = lax.ppermute(to_up, "ty", up)
    upper_in, blur, adj = lax.optimization_barrier((upper_in, blur, adj))
    upper, upper_east, upper_west = turn(where, views_data, upper_in, (1,))
    west, east = sides(
        jnp.concatenate([border_east, upper_east]), jnp.concatenate([border_west, upper_west])
    )
    lower_in, north, south = lax.optimization_barrier((lower_in, north, south))
    lower, lower_east, lower_west = turn(where, views_data, lower_in, (2,))

    def last_strip(strip, at, packed_at):
        parts = [strip]
        for halo in (north, south):
            parts.append(halo[:, at : at + MARGIN])
            parts.append(halo[:, HALF + packed_at : HALF + packed_at + MARGIN])
        return jnp.concatenate(parts)

    last_west, last_east = sides(
        last_strip(lower_east, HALF - MARGIN, CHUNK - MARGIN), last_strip(lower_west, 0, 0)
    )
    recorded = (north, west, last_west, border, upper, lower, east, last_east, south)

    estimate, top, low = iterate(
        recorded, None, taps, blur, adj, first=True, row0=0, n_out=ROWS
    )
    def piece(group, field):
        return iterate(
            recorded, field, taps, blur, adj, first=False, row0=GROUP * group, n_out=GROUP
        )

    field = (lax.ppermute(low, "ty", down), estimate, lax.ppermute(top, "ty", up))
    theirs = []
    whole = None
    for group in (1, 2, 0, 3):
        block = piece(group, field)
        theirs.append((group, lax.ppermute(block, "view", swap)))
        whole = place(where[:1], block, whole, group)
    for group, block in theirs:
        whole = place(there, block, whole, group)
    return whole


def solution(mesh):
    placed = (P("view", None, "ty", "tx"), P("view", None), P("view", None), P("view", None))
    return jax.shard_map(
        per_device, mesh=mesh, in_specs=placed, out_specs=P(None, "ty", "tx"), check_vma=False
    )
```

```python
import functools

import jax
import jax.numpy as jnp
from jax import lax
from jax.experimental import pallas as pl
from jax.experimental.pallas import tpu as pltpu
from jax.sharding import PartitionSpec as P

ITERS = 2
Z = 64
LANES = 128
ROWS = 32
HALF = 256
CHUNK = 128
PAD = 6
REACH = 3
SIDE = 8
MARGIN = 16
GROUP = 8
EXT_R = ROWS + 2 * PAD
EXT_C = HALF + 2 * MARGIN
MIB = 1024 * 1024
UNROLL = 8
UPDATE = 128
TINY = 1e-30


def params(mib):
    return pltpu.CompilerParams(vmem_limit_bytes=mib * MIB)


def in_hbm(array):
    return pltpu.with_memory_space_constraint(array, pltpu.HBM)


def blocks_of(total, largest=96):
    out, at = [], 0
    while at < total:
        size = min(largest, total - at)
        out.append((at, size))
        at += size
    return out


def matrices_kernel(kz_ref, blur_ref, adj_ref):
    taps = kz_ref.shape[0]
    lane = lax.broadcasted_iota(jnp.int32, (Z, LANES), 1)
    row = lax.broadcasted_iota(jnp.int32, (Z, LANES), 0)
    offset = row - lax.rem(lane, Z) + taps // 2
    mat = jnp.zeros((Z, LANES), jnp.float32)
    for t in range(taps):
        mat = mat + jnp.where(offset == t, kz_ref[t : t + 1, :], 0.0)
    high = mat.astype(jnp.bfloat16)
    low = (mat - high.astype(jnp.float32)).astype(jnp.bfloat16)
    blur_ref[0:Z, 0:LANES] = high
    blur_ref[0:Z, LANES:] = low
    blur_ref[Z:, 0:LANES] = high
    blur_ref[Z:, LANES:] = jnp.zeros((Z, LANES), jnp.bfloat16)
    adj = jnp.concatenate([mat, mat], axis=0).T * 0.5
    ahigh = adj.astype(jnp.bfloat16).astype(jnp.float32)
    alow = adj - ahigh
    first = lax.broadcasted_iota(jnp.int32, (LANES, LANES), 1) < Z
    adj_ref[0:LANES, :] = jnp.where(first, ahigh, alow).astype(jnp.bfloat16)
    adj_ref[LANES:, :] = jnp.where(first, ahigh, 0.0).astype(jnp.bfloat16)


def matrices(kz):
    return pl.pallas_call(
        matrices_kernel,
        out_shape=(
            jax.ShapeDtypeStruct((2 * Z, 2 * LANES), jnp.bfloat16),
            jax.ShapeDtypeStruct((2 * LANES, LANES), jnp.bfloat16),
        ),
        compiler_params=params(4),
        name="matrices",
    )(kz)


def turn_kernel(groups, corners, where_ref, own_ref, other_ref, *refs):
    if corners:
        halos, refs = refs[:2], refs[2:]
    out_ref, west_ref, east_ref = refs[:3]
    refs = refs[3:]
    own, other, sems, corner_sems = refs[-4:]
    corner_copies = []
    if corners:
        columns = (
            (west_ref, HALF - MARGIN, HALF + CHUNK - MARGIN),
            (east_ref, 0, HALF),
        )
        for side, (strip, near, far) in enumerate(columns):
            for n, halo in enumerate(halos):
                for m, at in enumerate((near, far)):
                    row = GROUP + REACH * (2 * n + m)
                    corner_copies.append(
                        pltpu.make_async_copy(
                            halo.at[:, pl.ds(at, MARGIN), :],
                            strip.at[pl.ds(row, REACH), :, :],
                            corner_sems.at[4 * side + 2 * n + m],
                        )
                    )
    for c in corner_copies:
        c.start()
    half, first = where_ref[0], where_ref[1] == 0
    blocks = [(i, j) for i in range(len(groups)) for j in range(2)]
    copies = []
    for n, (i, j) in enumerate(blocks):
        at = pl.multiple_of(half * HALF + j * CHUNK, CHUNK)
        mine = own_ref.at[0, :, pl.ds(groups[i] * GROUP, GROUP), pl.ds(at, CHUNK)]
        theirs = other_ref.at[:, pl.ds(i * GROUP, GROUP), pl.ds(j * CHUNK, CHUNK)]
        copies.append(
            (
                pltpu.make_async_copy(mine, own.at[n], sems.at[0, n]),
                pltpu.make_async_copy(theirs, other.at[n], sems.at[1, n]),
            )
        )
    for pair in copies:
        for c in pair:
            c.start()
    for n, (i, j) in enumerate(blocks):
        for c in copies[n]:
            c.wait()
        flat = own.at[n].reshape(Z * GROUP, CHUNK)
        flat_other = other.at[n].reshape(Z * GROUP, CHUNK)
        for y in range(GROUP):
            mine = flat[pl.ds(y, Z, stride=GROUP), :]
            theirs = flat_other[pl.ds(y, Z, stride=GROUP), :]
            pair = jnp.concatenate(
                [jnp.where(first, mine, theirs), jnp.where(first, theirs, mine)], axis=0
            ).T
            row = i * GROUP + y
            out_ref[row, pl.ds(j * CHUNK, CHUNK), :] = pair
            if j == 0:
                east_ref[row] = pair[:MARGIN]
            else:
                west_ref[row] = pair[CHUNK - MARGIN :]
    for c in corner_copies:
        c.wait()
    if len(groups) == 1:
        return
    up_ref, down_ref = refs[:2]
    lower = lax.broadcasted_iota(jnp.int32, (CHUNK, LANES), 1) < Z
    low = 2 * GROUP - PAD
    for ref, near, far in ((up_ref, 0, REACH), (down_ref, low + REACH, low)):
        for y in range(REACH):
            ref[y, pl.ds(0, HALF), :] = out_ref[near + y]
            ends = []
            for j in range(2):
                r = out_ref[far + y, pl.ds(j * CHUNK, CHUNK), :]
                ends.append((r + pltpu.roll(r, Z, 1)) * 0.5)
            ref[y, pl.ds(HALF, CHUNK), :] = jnp.where(lower, ends[0], ends[1])


def turn(where, recorded, received, groups, halos=()):
    rows = len(groups) * GROUP
    block = pltpu.VMEM((2 * len(groups), Z, GROUP, CHUNK), jnp.float32)
    strip_rows = rows + (4 * REACH if halos else 0)
    strip = jax.ShapeDtypeStruct((strip_rows, MARGIN, LANES), jnp.float32)
    out = [jax.ShapeDtypeStruct((rows, HALF, LANES), jnp.float32), strip, strip]
    if len(groups) > 1:
        out += [jax.ShapeDtypeStruct((REACH, HALF + CHUNK, LANES), jnp.float32)] * 2
    return pl.pallas_call(
        functools.partial(turn_kernel, groups, bool(halos)),
        out_shape=tuple(out),
        in_specs=[
            pl.BlockSpec(memory_space=pltpu.SMEM),
            pl.BlockSpec(memory_space=pltpu.HBM),
            pl.BlockSpec(memory_space=pl.ANY),
        ]
        + [pl.BlockSpec(memory_space=pl.ANY)] * len(halos),
        out_specs=(pl.BlockSpec(memory_space=pltpu.VMEM),) * len(out),
        scratch_shapes=[
            block,
            block,
            pltpu.SemaphoreType.DMA((2, 2 * len(groups))),
            pltpu.SemaphoreType.DMA((8,)),
        ],
        cost_estimate=pl.CostEstimate(
            flops=0, bytes_accessed=1024, transcendentals=0
        ),
        compiler_params=params(10),
        name="turn",
    )(where, in_hbm(recorded), received, *halos)


GROUPS = tuple((PAD + GROUP * g, GROUP) for g in range(4))
SPANS = ((REACH, REACH),) + GROUPS + ((EXT_R - PAD, REACH),)
FIRST_SPANS = ((0, REACH),) + SPANS + ((EXT_R - REACH, REACH),)
NEXT_SPANS = ((0, PAD),) + GROUPS + ((EXT_R - PAD, PAD),)
HOMES = (
    ((2, 8), (0, 0), (7, 8)),
    ((1, 0), (3, 0), (6, 0)),
    ((1, 16), (4, 0), (6, 16)),
    ((2, 0), (5, 0), (7, 0)),
    ((1, 8), (3, 8), (6, 8)),
    ((2, 14), (8, 0), (7, 14)),
)
OUTER = (11, 17)


def iterate_kernel(first, row0, n_out, present, *refs):
    n_in = n_out + 2 * PAD
    width = EXT_C if first else EXT_C - 2 * SIDE
    shift = 0 if first else SIDE
    inner = width - 2 * SIDE
    fold = (EXT_C - 2 * SIDE) // 2
    pieces = iter(refs)
    taken = [next(pieces) if there else None for there in present]
    recorded, field, refs = taken[:9], taken[9:], tuple(pieces)
    taps_ref, blur_hbm, adj_hbm = refs[:3]
    refs = refs[3:]
    if first:
        out_ref, top_ref, low_ref = refs[:3]
        refs = refs[3:]
    else:
        out_ref, refs = refs[0], refs[1:]
    r_buf, e_buf, xz_buf, xr_buf, pack, tmp, blur_ref, adj_ref, r_sem, e_sem, m_sem = refs
    north, south = recorded[0], recorded[8]
    lower = lax.broadcasted_iota(jnp.int32, (width, LANES), 1) < Z

    def window(span, lo, hi):
        at, count = span
        a, b = max(at, lo), min(at + count, hi)
        return (a, b) if a < b else None

    def r_copies(k):
        got = window(SPANS[k], row0 + REACH, row0 + n_in - REACH)
        if got is None:
            return []
        a, b = got
        rows = pl.ds(a - row0, b - a)
        pairs = []
        ranges = ((0, MARGIN), (MARGIN, MARGIN + HALF), (MARGIN + HALF, EXT_C))
        for (home, base), (lo, hi) in zip(HOMES[k], ranges):
            src = recorded[home]
            c, d = max(lo, shift), min(hi, shift + width)
            pairs.append(
                (
                    src.at[pl.ds(base + a - SPANS[k][0], b - a), pl.ds(c - lo, d - c), :],
                    r_buf.at[rows, pl.ds(c - shift, d - c), :],
                )
            )
        return [
            pltpu.make_async_copy(src, dst, r_sem.at[k, n]) for n, (src, dst) in enumerate(pairs)
        ]

    def e_copies(k):
        if first:
            if 0 < k < 7:
                return []
            n = 0 if k == 0 else 1
            halo, rows = (north if n == 0 else south), pl.ds(OUTER[n], REACH)
            pairs = (
                (recorded[2].at[rows, :, :], pl.ds(0, MARGIN)),
                (halo.at[:, pl.ds(HALF, CHUNK), :], pl.ds(MARGIN, CHUNK)),
                (recorded[7].at[rows, :, :], pl.ds(MARGIN + CHUNK, MARGIN)),
            )
            return [
                pltpu.make_async_copy(src, pack.at[n, :, cols, :], e_sem.at[k, i])
                for i, (src, cols) in enumerate(pairs)
            ]
        got = window(NEXT_SPANS[k], row0, row0 + n_in)
        if got is None:
            return []
        a, b = got
        if k in (0, 5):
            src, dst = (field[0] if k == 0 else field[2]), pack.at[0 if k == 0 else 1]
        else:
            at = GROUP * (k - 1) + a - NEXT_SPANS[k][0]
            src, dst = field[1].at[pl.ds(at, b - a), :, :], e_buf.at[pl.ds(a - row0, b - a), :, :]
        return [pltpu.make_async_copy(src, dst, e_sem.at[k, 0])]

    recorded_in = [r_copies(k) for k in range(6)]
    e_spans = FIRST_SPANS if first else NEXT_SPANS
    field_in = [e_copies(k) for k in range(len(e_spans))]
    matrices_in = [
        pltpu.make_async_copy(blur_hbm, blur_ref, m_sem.at[0]),
        pltpu.make_async_copy(adj_hbm, adj_ref, m_sem.at[1]),
    ]
    for group in [matrices_in] + field_in + recorded_in:
        for c in group:
            c.start()

    def over_rows(start, count, steps, unroll):
        def rows_from(at, many):
            for step in steps:
                for slot in range(many):
                    step(slot, at + slot)

        def body(i, carry):
            rows_from(start + unroll * i, unroll)
            return carry

        lax.fori_loop(0, count // unroll, body, 0)
        if count % unroll:
            rows_from(start + count - count % unroll, count % unroll)

    kx = [taps_ref[t : t + 1, :] for t in range(7)]
    ky = [taps_ref[8 + t : 9 + t, :] for t in range(7)]
    col_blocks = blocks_of(width)

    def cols_pass(slot, taps, dst_ref, row):
        for at, size in col_blocks:
            acc = taps[0] * tmp[slot, pl.ds(5 + at, size), :]
            for t in range(1, 7):
                acc = acc + taps[t] * tmp[slot, pl.ds(5 + t + at, size), :]
            dst_ref[row, pl.ds(at, size), :] = acc

    def blur_row(slot, row, started):
        if not started:
            r = r_buf[row]
            e = (r + pltpu.roll(r, Z, 1)) * 0.5
            e_buf[row] = e
        else:
            e = e_buf[row]
        high = e.astype(jnp.bfloat16).astype(jnp.float32)
        split = jnp.where(lower, high, e - high).astype(jnp.bfloat16)
        both = jnp.dot(split, blur_ref[...], preferred_element_type=jnp.float32)
        tmp[slot, pl.ds(8, width), :] = both[:, :LANES] + both[:, LANES:]

    for slot in range(UNROLL):
        tmp[slot, pl.ds(0, 8), :] = jnp.zeros((8, LANES), jnp.float32)
        tmp[slot, pl.ds(8 + width, 8), :] = jnp.zeros((8, LANES), jnp.float32)

    def both_halves(packed, turned, size, low_first):
        keep = lower[:size] if low_first else jnp.logical_not(lower[:size])
        return jnp.where(keep, packed, turned)

    for c in matrices_in:
        c.wait()
    for k, span in enumerate(e_spans):
        got = window(span, row0, row0 + n_in)
        if got is None:
            continue
        for c in field_in[k]:
            c.wait()
        halo = k in (0, len(e_spans) - 1)
        if first and not halo:
            for c in recorded_in[k - 1]:
                c.wait()
        base, count = got[0] - row0, got[1] - got[0]

        def halo_row(slot, row, halo=halo, k=k, base=base):
            if halo:
                packed = pack[0 if k == 0 else 1, row - base]
                turned = pltpu.roll(packed, Z, 1)
                if first:
                    parts = (
                        (0, 0, MARGIN, False),
                        (MARGIN, MARGIN, CHUNK, True),
                        (MARGIN + CHUNK, MARGIN, CHUNK, False),
                        (MARGIN + HALF, MARGIN + CHUNK, MARGIN, True),
                    )
                else:
                    parts = ((0, 0, fold, True), (fold, 0, fold, False))
                for to, at, size, low_first in parts:
                    e_buf[row, pl.ds(to, size), :] = both_halves(
                        packed[at : at + size], turned[at : at + size], size, low_first
                    )
            blur_row(slot, row, halo or not first)

        over_rows(
            base,
            count,
            (halo_row, lambda slot, row: cols_pass(slot, kx, xz_buf, row)),
            UNROLL,
        )

    if not first:
        for group in recorded_in:
            for c in group:
                c.wait()

    def rows_pass(src_ref, taps, row, at, size):
        acc = taps[0] * src_ref[row - 3, pl.ds(at, size), :]
        for t in range(1, 7):
            acc = acc + taps[t] * src_ref[row - 3 + t, pl.ds(at, size), :]
        return acc

    def ratio_row(slot, row):
        for at, size in col_blocks:
            blurred = rows_pass(xz_buf, ky, row, at, size)
            ratio = r_buf[row, pl.ds(at, size), :] / jnp.maximum(blurred, TINY)
            tmp[slot, pl.ds(8 + at, size), :] = ratio

    over_rows(3, n_in - 6, (ratio_row, lambda slot, row: cols_pass(slot, kx[::-1], xr_buf, row)), UNROLL)

    def update_row(slot, y):
        row = PAD + y
        for at, size in blocks_of(inner, UPDATE):
            spread = rows_pass(xr_buf, ky[::-1], row, SIDE + at, size)
            high = spread.astype(jnp.bfloat16)
            low = (spread - high.astype(jnp.float32)).astype(jnp.bfloat16)
            both = jnp.dot(
                jnp.concatenate([high, low], axis=1),
                adj_ref[...],
                preferred_element_type=jnp.float32,
            )
            factor = both + pltpu.roll(both, Z, 1)
            new = e_buf[row, pl.ds(SIDE + at, size), :] * factor
            if first:
                out_ref[y, pl.ds(at, size), :] = new
            else:
                flat = out_ref.at[at // CHUNK].reshape(Z * GROUP, CHUNK)
                flat[pl.ds(y, Z, stride=GROUP), :] = new.T[:Z]

    over_rows(0, n_out, (update_row,), UNROLL)
    if first:
        for y in range(PAD):
            for ref, row in ((top_ref, y), (low_ref, ROWS - PAD + y)):
                ref[y] = jnp.where(
                    lower[:fold], out_ref[row, pl.ds(0, fold), :], out_ref[row, pl.ds(fold, fold), :]
                )


def iterate(recorded, field, taps, blur, adj, *, first, row0, n_out):
    n_in = n_out + 2 * PAD
    width = EXT_C if first else EXT_C - 2 * SIDE
    fold = (EXT_C - 2 * SIDE) // 2
    pieces = list(recorded) + (list(field) if field is not None else [])
    if not first and row0 >= PAD:
        pieces[0] = pieces[9] = None
    if not first and row0 + n_in <= EXT_R - PAD:
        pieces[8] = pieces[11] = None
    for k in (0, 5, 8):
        if pieces[k] is not None:
            pieces[k] = in_hbm(pieces[k])
    present = tuple(piece is not None for piece in pieces)
    pieces = [piece for piece in pieces if piece is not None]
    if first:
        edge = jax.ShapeDtypeStruct((PAD, fold, LANES), jnp.float32)
        out = (jax.ShapeDtypeStruct((ROWS, EXT_C - 2 * SIDE, LANES), jnp.float32), edge, edge)
        out_specs = (pl.BlockSpec(memory_space=pltpu.VMEM),) * 3
    else:
        out = jax.ShapeDtypeStruct((2, Z, GROUP, CHUNK), jnp.float32)
        out_specs = pl.BlockSpec(memory_space=pltpu.VMEM)
    row = pltpu.VMEM((n_in, width, LANES), jnp.float32)
    vregs = n_in * width // 8
    return pl.pallas_call(
        functools.partial(iterate_kernel, first, row0, n_out, present),
        out_shape=out,
        in_specs=[pl.BlockSpec(memory_space=pl.ANY)] * len(pieces)
        + [pl.BlockSpec(memory_space=pltpu.VMEM)]
        + [pl.BlockSpec(memory_space=pl.ANY)] * 2,
        out_specs=out_specs,
        scratch_shapes=[
            row,
            row,
            row,
            row,
            pltpu.VMEM(
                (2, REACH, CHUNK + 2 * MARGIN, LANES) if first else (2, PAD, fold, LANES),
                jnp.float32,
            ),
            pltpu.VMEM((UNROLL, width + 16, LANES), jnp.float32),
            pltpu.VMEM((2 * Z, 2 * LANES), jnp.bfloat16),
            pltpu.VMEM((2 * LANES, LANES), jnp.bfloat16),
            pltpu.SemaphoreType.DMA((6, 3)),
            pltpu.SemaphoreType.DMA((8, 3)),
            pltpu.SemaphoreType.DMA((2,)),
        ],
        cost_estimate=pl.CostEstimate(
            flops=0, bytes_accessed=vregs * 4096 if first else 4096, transcendentals=0
        ),
        compiler_params=params(30 if first else 13),
        name="iterate",
    )(*pieces, taps, in_hbm(blur), in_hbm(adj))


def place_kernel(where_ref, *refs):
    refs[-1][...] = refs[0][0]


def place(where, block, whole, group):
    args = [where, block]
    in_specs = [pl.BlockSpec((1, Z, GROUP, CHUNK), lambda j, w: (j, 0, 0, 0))]
    aliases = {}
    if whole is not None:
        args.append(whole)
        in_specs.append(pl.BlockSpec(memory_space=pl.ANY))
        aliases = {2: 0}
    return pl.pallas_call(
        place_kernel,
        out_shape=jax.ShapeDtypeStruct((Z, ROWS, 2 * HALF), jnp.float32),
        grid_spec=pltpu.PrefetchScalarGridSpec(
            num_scalar_prefetch=1,
            grid=(2,),
            in_specs=in_specs,
            out_specs=pl.BlockSpec((Z, GROUP, CHUNK), lambda j, w: (0, group, 2 * w[0] + j)),
        ),
        input_output_aliases=aliases,
        cost_estimate=pl.CostEstimate(flops=0, bytes_accessed=1 << 20, transcendentals=0),
        compiler_params=params(4),
        name="place",
    )(*args)


def neighbours(views, tiles):
    right = []
    for v in range(views):
        for t in range(tiles):
            if (t + v) % 2 == 0:
                right.append((v * tiles + t, (1 - v) * tiles + t))
            elif t + 1 < tiles:
                right.append((v * tiles + t, v * tiles + t + 1))
    return right


def per_device(views_data, psf_axial, psf_rows, psf_cols):
    views, tiles, bands = lax.axis_size("view"), lax.axis_size("tx"), lax.axis_size("ty")
    swap = [(0, 1), (1, 0)]
    right = neighbours(views, tiles)
    left = [(b, a) for a, b in right]
    down = [(i, i + 1) for i in range(bands - 1)]
    up = [(b, a) for a, b in down]
    half = lax.rem(lax.axis_index("tx") + lax.axis_index("view"), 2)

    def other_rows(views_data, *starts):
        at = (1 - half) * HALF
        return jnp.concatenate(
            [
                lax.dynamic_slice(views_data, (0, 0, row, at), (1, Z, rows, HALF))[0]
                for row, rows in starts
            ],
            axis=1,
        )

    raw = jnp.concatenate([psf_axial[0], psf_rows[0], psf_cols[0]])
    raw_other = lax.ppermute(raw, "view", swap)
    border = other_rows(views_data, (0, GROUP), (ROWS - GROUP, GROUP))
    raw, border = lax.optimization_barrier((raw, border))
    border_in = lax.ppermute(border, "view", swap)
    later, border = lax.optimization_barrier((views_data, border))
    upper_in = lax.ppermute(other_rows(later, (GROUP, GROUP)), "view", swap)
    last_rows, raw_other = lax.optimization_barrier(
        (other_rows(later, (2 * GROUP, GROUP)), raw_other)
    )
    lower_in = lax.ppermute(last_rows, "view", swap)

    def norm(taps):
        parts = (taps[:21], taps[21:28], taps[28:35])
        return jnp.concatenate([part / jnp.sum(part) for part in parts])

    own, other = norm(raw), norm(raw_other)
    view = lax.axis_index("view")
    lanes = jnp.concatenate(
        [
            jnp.broadcast_to(jnp.where(view == 0, own, other)[:, None], (own.shape[0], Z)),
            jnp.broadcast_to(jnp.where(view == 0, other, own)[:, None], (own.shape[0], Z)),
        ],
        axis=1,
    )
    blur, adj = matrices(lanes[:21])
    taps = jnp.zeros((16, LANES), jnp.float32)
    taps = taps.at[0:7].set(lanes[28:35]).at[8:15].set(lanes[21:28])

    where = jnp.stack([half, view]).astype(jnp.int32)
    there = (1 - half).astype(jnp.int32)[None]

    def sides(west, east):
        return lax.ppermute(west, ("view", "tx"), right), lax.ppermute(east, ("view", "tx"), left)

    border, border_east, border_west, to_up, to_down = turn(where, views_data, border_in, (0, 3))
    north = lax.ppermute(to_down, "ty", down)
    south = lax.ppermute(to_up, "ty", up)
    upper_in, blur, adj = lax.optimization_barrier((upper_in, blur, adj))
    upper, upper_east, upper_west = turn(where, views_data, upper_in, (1,))
    west, east = sides(
        jnp.concatenate([border_east, upper_east]), jnp.concatenate([border_west, upper_west])
    )
    lower, lower_east, lower_west = turn(
        where, views_data, lower_in, (2,), (in_hbm(north), in_hbm(south))
    )
    last_west, last_east = sides(lower_east, lower_west)
    recorded = (north, west, last_west, border, upper, lower, east, last_east, south)

    estimate, top, low = iterate(
        recorded, None, taps, blur, adj, first=True, row0=0, n_out=ROWS
    )
    def piece(group, field):
        return iterate(
            recorded, field, taps, blur, adj, first=False, row0=GROUP * group, n_out=GROUP
        )

    field = (lax.ppermute(low, "ty", down), estimate, lax.ppermute(top, "ty", up))
    theirs = []
    whole = None
    for group in (1, 2, 0, 3):
        block = piece(group, field)
        theirs.append((group, lax.ppermute(block, "view", swap)))
        whole = place(where[:1], block, whole, group)
    for group, block in theirs:
        whole = place(there, block, whole, group)
    return whole


def solution(mesh):
    placed = (P("view", None, "ty", "tx"), P("view", None), P("view", None), P("view", None))
    return jax.shard_map(
        per_device, mesh=mesh, in_specs=placed, out_specs=P(None, "ty", "tx"), check_vma=False
    )
```

```python
import functools

import jax
import jax.numpy as jnp
from jax import lax
from jax.experimental import pallas as pl
from jax.experimental.pallas import tpu as pltpu
from jax.sharding import PartitionSpec as P

ITERS = 2
Z = 64
LANES = 128
ROWS = 32
HALF = 256
CHUNK = 128
PAD = 6
REACH = 3
SIDE = 8
MARGIN = 16
GROUP = 8
EXT_R = ROWS + 2 * PAD
EXT_C = HALF + 2 * MARGIN
MIB = 1024 * 1024
UNROLL = 8
UPDATE = 128
TINY = 1e-30


def params(mib):
    return pltpu.CompilerParams(vmem_limit_bytes=mib * MIB)


def in_hbm(array):
    return pltpu.with_memory_space_constraint(array, pltpu.HBM)


def blocks_of(total, largest=96):
    out, at = [], 0
    while at < total:
        size = min(largest, total - at)
        out.append((at, size))
        at += size
    return out


def matrices_kernel(kz_ref, blur_ref, adj_ref):
    taps = kz_ref.shape[0]
    lane = lax.broadcasted_iota(jnp.int32, (Z, LANES), 1)
    row = lax.broadcasted_iota(jnp.int32, (Z, LANES), 0)
    offset = row - lax.rem(lane, Z) + taps // 2
    mat = jnp.zeros((Z, LANES), jnp.float32)
    for t in range(taps):
        mat = mat + jnp.where(offset == t, kz_ref[t : t + 1, :], 0.0)
    high = mat.astype(jnp.bfloat16)
    low = (mat - high.astype(jnp.float32)).astype(jnp.bfloat16)
    blur_ref[0:Z, 0:LANES] = high
    blur_ref[0:Z, LANES:] = low
    blur_ref[Z:, 0:LANES] = high
    blur_ref[Z:, LANES:] = jnp.zeros((Z, LANES), jnp.bfloat16)
    adj = jnp.concatenate([mat, mat], axis=0).T * 0.5
    ahigh = adj.astype(jnp.bfloat16).astype(jnp.float32)
    alow = adj - ahigh
    first = lax.broadcasted_iota(jnp.int32, (LANES, LANES), 1) < Z
    adj_ref[0:LANES, :] = jnp.where(first, ahigh, alow).astype(jnp.bfloat16)
    adj_ref[LANES:, :] = jnp.where(first, ahigh, 0.0).astype(jnp.bfloat16)


def matrices(kz):
    return pl.pallas_call(
        matrices_kernel,
        out_shape=(
            jax.ShapeDtypeStruct((2 * Z, 2 * LANES), jnp.bfloat16),
            jax.ShapeDtypeStruct((2 * LANES, LANES), jnp.bfloat16),
        ),
        compiler_params=params(4),
        name="matrices",
    )(kz)


def turn_kernel(groups, corners, where_ref, own_ref, other_ref, *refs):
    if corners:
        halos, refs = refs[:2], refs[2:]
    out_ref, west_ref, east_ref = refs[:3]
    refs = refs[3:]
    own, other, sems, corner_sems = refs[-4:]
    corner_copies = []
    if corners:
        columns = (
            (west_ref, HALF - MARGIN, HALF + CHUNK - MARGIN),
            (east_ref, 0, HALF),
        )
        for side, (strip, near, far) in enumerate(columns):
            for n, halo in enumerate(halos):
                for m, at in enumerate((near, far)):
                    row = GROUP + REACH * (2 * n + m)
                    corner_copies.append(
                        pltpu.make_async_copy(
                            halo.at[:, pl.ds(at, MARGIN), :],
                            strip.at[pl.ds(row, REACH), :, :],
                            corner_sems.at[4 * side + 2 * n + m],
                        )
                    )
    for c in corner_copies:
        c.start()
    half, first = where_ref[0], where_ref[1] == 0
    blocks = [(i, j) for i in range(len(groups)) for j in range(2)]
    copies = []
    for n, (i, j) in enumerate(blocks):
        at = pl.multiple_of(half * HALF + j * CHUNK, CHUNK)
        mine = own_ref.at[0, :, pl.ds(groups[i] * GROUP, GROUP), pl.ds(at, CHUNK)]
        theirs = other_ref.at[:, pl.ds(i * GROUP, GROUP), pl.ds(j * CHUNK, CHUNK)]
        copies.append(
            (
                pltpu.make_async_copy(mine, own.at[n], sems.at[0, n]),
                pltpu.make_async_copy(theirs, other.at[n], sems.at[1, n]),
            )
        )
    for pair in copies:
        for c in pair:
            c.start()
    for n, (i, j) in enumerate(blocks):
        for c in copies[n]:
            c.wait()
        flat = own.at[n].reshape(Z * GROUP, CHUNK)
        flat_other = other.at[n].reshape(Z * GROUP, CHUNK)
        for y in range(GROUP):
            mine = flat[pl.ds(y, Z, stride=GROUP), :]
            theirs = flat_other[pl.ds(y, Z, stride=GROUP), :]
            pair = jnp.concatenate(
                [jnp.where(first, mine, theirs), jnp.where(first, theirs, mine)], axis=0
            ).T
            row = i * GROUP + y
            out_ref[row, pl.ds(j * CHUNK, CHUNK), :] = pair
            if j == 0:
                east_ref[row] = pair[:MARGIN]
            else:
                west_ref[row] = pair[CHUNK - MARGIN :]
    for c in corner_copies:
        c.wait()
    if len(groups) == 1:
        return
    up_ref, down_ref = refs[:2]
    lower = lax.broadcasted_iota(jnp.int32, (CHUNK, LANES), 1) < Z
    low = 2 * GROUP - PAD
    for ref, near, far in ((up_ref, 0, REACH), (down_ref, low + REACH, low)):
        for y in range(REACH):
            ref[y, pl.ds(0, HALF), :] = out_ref[near + y]
            ends = []
            for j in range(2):
                r = out_ref[far + y, pl.ds(j * CHUNK, CHUNK), :]
                ends.append((r + pltpu.roll(r, Z, 1)) * 0.5)
            ref[y, pl.ds(HALF, CHUNK), :] = jnp.where(lower, ends[0], ends[1])


def turn(where, recorded, received, groups, halos=()):
    rows = len(groups) * GROUP
    block = pltpu.VMEM((2 * len(groups), Z, GROUP, CHUNK), jnp.float32)
    strip_rows = rows + (4 * REACH if halos else 0)
    strip = jax.ShapeDtypeStruct((strip_rows, MARGIN, LANES), jnp.float32)
    out = [jax.ShapeDtypeStruct((rows, HALF, LANES), jnp.float32), strip, strip]
    if len(groups) > 1:
        out += [jax.ShapeDtypeStruct((REACH, HALF + CHUNK, LANES), jnp.float32)] * 2
    return pl.pallas_call(
        functools.partial(turn_kernel, groups, bool(halos)),
        out_shape=tuple(out),
        in_specs=[
            pl.BlockSpec(memory_space=pltpu.SMEM),
            pl.BlockSpec(memory_space=pltpu.HBM),
            pl.BlockSpec(memory_space=pl.ANY),
        ]
        + [pl.BlockSpec(memory_space=pl.ANY)] * len(halos),
        out_specs=(pl.BlockSpec(memory_space=pltpu.VMEM),) * len(out),
        scratch_shapes=[
            block,
            block,
            pltpu.SemaphoreType.DMA((2, 2 * len(groups))),
            pltpu.SemaphoreType.DMA((8,)),
        ],
        cost_estimate=pl.CostEstimate(
            flops=0, bytes_accessed=1024, transcendentals=0
        ),
        compiler_params=params(10),
        name="turn",
    )(where, in_hbm(recorded), received, *halos)


GROUPS = tuple((PAD + GROUP * g, GROUP) for g in range(4))
SPANS = ((REACH, REACH),) + GROUPS + ((EXT_R - PAD, REACH),)
FIRST_SPANS = ((0, REACH),) + SPANS + ((EXT_R - REACH, REACH),)
NEXT_SPANS = ((0, PAD),) + GROUPS + ((EXT_R - PAD, PAD),)
HOMES = (
    ((2, 8), (0, 0), (7, 8)),
    ((1, 0), (3, 0), (6, 0)),
    ((1, 16), (4, 0), (6, 16)),
    ((2, 0), (5, 0), (7, 0)),
    ((1, 8), (3, 8), (6, 8)),
    ((2, 14), (8, 0), (7, 14)),
)
OUTER = (11, 17)


def iterate_kernel(first, row0, n_out, present, *refs):
    n_in = n_out + 2 * PAD
    width = EXT_C if first else EXT_C - 2 * SIDE
    shift = 0 if first else SIDE
    inner = width - 2 * SIDE
    fold = (EXT_C - 2 * SIDE) // 2
    pieces = iter(refs)
    taken = [next(pieces) if there else None for there in present]
    recorded, field, refs = taken[:9], taken[9:], tuple(pieces)
    taps_ref, blur_hbm, adj_hbm = refs[:3]
    refs = refs[3:]
    if first:
        out_ref, top_ref, low_ref = refs[:3]
        refs = refs[3:]
    else:
        out_ref, refs = refs[0], refs[1:]
    r_buf, e_buf, xz_buf, xr_buf, pack, tmp, blur_ref, adj_ref, r_sem, e_sem, m_sem = refs
    north, south = recorded[0], recorded[8]
    lower = lax.broadcasted_iota(jnp.int32, (width, LANES), 1) < Z

    def window(span, lo, hi):
        at, count = span
        a, b = max(at, lo), min(at + count, hi)
        return (a, b) if a < b else None

    def r_copies(k):
        got = window(SPANS[k], row0 + REACH, row0 + n_in - REACH)
        if got is None:
            return []
        a, b = got
        rows = pl.ds(a - row0, b - a)
        pairs = []
        ranges = ((0, MARGIN), (MARGIN, MARGIN + HALF), (MARGIN + HALF, EXT_C))
        for (home, base), (lo, hi) in zip(HOMES[k], ranges):
            src = recorded[home]
            c, d = max(lo, shift), min(hi, shift + width)
            pairs.append(
                (
                    src.at[pl.ds(base + a - SPANS[k][0], b - a), pl.ds(c - lo, d - c), :],
                    r_buf.at[rows, pl.ds(c - shift, d - c), :],
                )
            )
        return [
            pltpu.make_async_copy(src, dst, r_sem.at[k, n]) for n, (src, dst) in enumerate(pairs)
        ]

    def e_copies(k):
        if first:
            if 0 < k < 7:
                return []
            n = 0 if k == 0 else 1
            halo, rows = (north if n == 0 else south), pl.ds(OUTER[n], REACH)
            pairs = (
                (recorded[2].at[rows, :, :], pl.ds(0, MARGIN)),
                (halo.at[:, pl.ds(HALF, CHUNK), :], pl.ds(MARGIN, CHUNK)),
                (recorded[7].at[rows, :, :], pl.ds(MARGIN + CHUNK, MARGIN)),
            )
            return [
                pltpu.make_async_copy(src, pack.at[n, :, cols, :], e_sem.at[k, i])
                for i, (src, cols) in enumerate(pairs)
            ]
        got = window(NEXT_SPANS[k], row0, row0 + n_in)
        if got is None:
            return []
        a, b = got
        if k in (0, 5):
            src, dst = (field[0] if k == 0 else field[2]), pack.at[0 if k == 0 else 1]
        else:
            at = GROUP * (k - 1) + a - NEXT_SPANS[k][0]
            src, dst = field[1].at[pl.ds(at, b - a), :, :], e_buf.at[pl.ds(a - row0, b - a), :, :]
        return [pltpu.make_async_copy(src, dst, e_sem.at[k, 0])]

    recorded_in = [r_copies(k) for k in range(6)]
    e_spans = FIRST_SPANS if first else NEXT_SPANS
    field_in = [e_copies(k) for k in range(len(e_spans))]
    matrices_in = [
        pltpu.make_async_copy(blur_hbm, blur_ref, m_sem.at[0]),
        pltpu.make_async_copy(adj_hbm, adj_ref, m_sem.at[1]),
    ]
    for group in [matrices_in] + field_in + recorded_in:
        for c in group:
            c.start()

    def over_rows(start, count, steps, unroll):
        def rows_from(at, many):
            for step in steps:
                for slot in range(many):
                    step(slot, at + slot)

        def body(i, carry):
            rows_from(start + unroll * i, unroll)
            return carry

        lax.fori_loop(0, count // unroll, body, 0)
        if count % unroll:
            rows_from(start + count - count % unroll, count % unroll)

    kx = [taps_ref[t : t + 1, :] for t in range(7)]
    ky = [taps_ref[8 + t : 9 + t, :] for t in range(7)]
    col_blocks = blocks_of(width)

    def cols_pass(slot, taps, dst_ref, row):
        for at, size in col_blocks:
            acc = taps[0] * tmp[slot, pl.ds(5 + at, size), :]
            for t in range(1, 7):
                acc = acc + taps[t] * tmp[slot, pl.ds(5 + t + at, size), :]
            dst_ref[row, pl.ds(at, size), :] = acc

    def blur_row(slot, row, started):
        if not started:
            r = r_buf[row]
            e = (r + pltpu.roll(r, Z, 1)) * 0.5
            e_buf[row] = e
        else:
            e = e_buf[row]
        high = e.astype(jnp.bfloat16).astype(jnp.float32)
        split = jnp.where(lower, high, e - high).astype(jnp.bfloat16)
        both = jnp.dot(split, blur_ref[...], preferred_element_type=jnp.float32)
        tmp[slot, pl.ds(8, width), :] = both[:, :LANES] + both[:, LANES:]

    for slot in range(UNROLL):
        tmp[slot, pl.ds(0, 8), :] = jnp.zeros((8, LANES), jnp.float32)
        tmp[slot, pl.ds(8 + width, 8), :] = jnp.zeros((8, LANES), jnp.float32)

    def both_halves(packed, turned, size, low_first):
        keep = lower[:size] if low_first else jnp.logical_not(lower[:size])
        return jnp.where(keep, packed, turned)

    for c in matrices_in:
        c.wait()
    for k, span in enumerate(e_spans):
        got = window(span, row0, row0 + n_in)
        if got is None:
            continue
        for c in field_in[k]:
            c.wait()
        halo = k in (0, len(e_spans) - 1)
        if first and not halo:
            for c in recorded_in[k - 1]:
                c.wait()
        base, count = got[0] - row0, got[1] - got[0]

        def halo_row(slot, row, halo=halo, k=k, base=base):
            if halo:
                packed = pack[0 if k == 0 else 1, row - base]
                turned = pltpu.roll(packed, Z, 1)
                if first:
                    parts = (
                        (0, 0, MARGIN, False),
                        (MARGIN, MARGIN, CHUNK, True),
                        (MARGIN + CHUNK, MARGIN, CHUNK, False),
                        (MARGIN + HALF, MARGIN + CHUNK, MARGIN, True),
                    )
                else:
                    parts = ((0, 0, fold, True), (fold, 0, fold, False))
                for to, at, size, low_first in parts:
                    e_buf[row, pl.ds(to, size), :] = both_halves(
                        packed[at : at + size], turned[at : at + size], size, low_first
                    )
            blur_row(slot, row, halo or not first)

        over_rows(
            base,
            count,
            (halo_row, lambda slot, row: cols_pass(slot, kx, xz_buf, row)),
            UNROLL,
        )

    if not first:
        for group in recorded_in:
            for c in group:
                c.wait()

    def rows_pass(src_ref, taps, row, at, size):
        acc = taps[0] * src_ref[row - 3, pl.ds(at, size), :]
        for t in range(1, 7):
            acc = acc + taps[t] * src_ref[row - 3 + t, pl.ds(at, size), :]
        return acc

    def ratio_row(slot, row):
        for at, size in col_blocks:
            blurred = rows_pass(xz_buf, ky, row, at, size)
            ratio = r_buf[row, pl.ds(at, size), :] / jnp.maximum(blurred, TINY)
            tmp[slot, pl.ds(8 + at, size), :] = ratio

    over_rows(3, n_in - 6, (ratio_row, lambda slot, row: cols_pass(slot, kx[::-1], xr_buf, row)), UNROLL)

    def update_row(slot, y):
        row = PAD + y
        for at, size in blocks_of(inner, UPDATE):
            spread = rows_pass(xr_buf, ky[::-1], row, SIDE + at, size)
            high = spread.astype(jnp.bfloat16)
            low = (spread - high.astype(jnp.float32)).astype(jnp.bfloat16)
            both = jnp.dot(
                jnp.concatenate([high, low], axis=1),
                adj_ref[...],
                preferred_element_type=jnp.float32,
            )
            factor = both + pltpu.roll(both, Z, 1)
            new = e_buf[row, pl.ds(SIDE + at, size), :] * factor
            if first:
                out_ref[y, pl.ds(at, size), :] = new
            else:
                flat = out_ref.at[at // CHUNK].reshape(Z * GROUP, CHUNK)
                flat[pl.ds(y, Z, stride=GROUP), :] = new.T[:Z]

    over_rows(0, n_out, (update_row,), UNROLL)
    if first:
        for y in range(PAD):
            for ref, row in ((top_ref, y), (low_ref, ROWS - PAD + y)):
                ref[y] = jnp.where(
                    lower[:fold], out_ref[row, pl.ds(0, fold), :], out_ref[row, pl.ds(fold, fold), :]
                )


def iterate(recorded, field, taps, blur, adj, *, first, row0, n_out):
    n_in = n_out + 2 * PAD
    width = EXT_C if first else EXT_C - 2 * SIDE
    fold = (EXT_C - 2 * SIDE) // 2
    pieces = list(recorded) + (list(field) if field is not None else [])
    if not first and row0 >= PAD:
        pieces[0] = pieces[9] = None
    if not first and row0 + n_in <= EXT_R - PAD:
        pieces[8] = pieces[11] = None
    for k in (0, 5, 8):
        if pieces[k] is not None:
            pieces[k] = in_hbm(pieces[k])
    present = tuple(piece is not None for piece in pieces)
    pieces = [piece for piece in pieces if piece is not None]
    if first:
        edge = jax.ShapeDtypeStruct((PAD, fold, LANES), jnp.float32)
        out = (jax.ShapeDtypeStruct((ROWS, EXT_C - 2 * SIDE, LANES), jnp.float32), edge, edge)
        out_specs = (pl.BlockSpec(memory_space=pltpu.VMEM),) * 3
    else:
        out = jax.ShapeDtypeStruct((2, Z, GROUP, CHUNK), jnp.float32)
        out_specs = pl.BlockSpec(memory_space=pltpu.VMEM)
    row = pltpu.VMEM((n_in, width, LANES), jnp.float32)
    vregs = n_in * width // 8
    return pl.pallas_call(
        functools.partial(iterate_kernel, first, row0, n_out, present),
        out_shape=out,
        in_specs=[pl.BlockSpec(memory_space=pl.ANY)] * len(pieces)
        + [pl.BlockSpec(memory_space=pltpu.VMEM)]
        + [pl.BlockSpec(memory_space=pl.ANY)] * 2,
        out_specs=out_specs,
        scratch_shapes=[
            row,
            row,
            row,
            row,
            pltpu.VMEM(
                (2, REACH, CHUNK + 2 * MARGIN, LANES) if first else (2, PAD, fold, LANES),
                jnp.float32,
            ),
            pltpu.VMEM((UNROLL, width + 16, LANES), jnp.float32),
            pltpu.VMEM((2 * Z, 2 * LANES), jnp.bfloat16),
            pltpu.VMEM((2 * LANES, LANES), jnp.bfloat16),
            pltpu.SemaphoreType.DMA((6, 3)),
            pltpu.SemaphoreType.DMA((8, 3)),
            pltpu.SemaphoreType.DMA((2,)),
        ],
        cost_estimate=pl.CostEstimate(
            flops=0, bytes_accessed=vregs * 4096 if first else 4096, transcendentals=0
        ),
        compiler_params=params(30 if first else 13),
        name="iterate",
    )(*pieces, taps, in_hbm(blur), in_hbm(adj))


def place_kernel(where_ref, *refs):
    refs[-1][...] = refs[0][0]


def place(where, block, whole, group):
    args = [where, block]
    in_specs = [pl.BlockSpec((1, Z, GROUP, CHUNK), lambda j, w: (j, 0, 0, 0))]
    aliases = {}
    if whole is not None:
        args.append(whole)
        in_specs.append(pl.BlockSpec(memory_space=pl.ANY))
        aliases = {2: 0}
    return pl.pallas_call(
        place_kernel,
        out_shape=jax.ShapeDtypeStruct((Z, ROWS, 2 * HALF), jnp.float32),
        grid_spec=pltpu.PrefetchScalarGridSpec(
            num_scalar_prefetch=1,
            grid=(2,),
            in_specs=in_specs,
            out_specs=pl.BlockSpec((Z, GROUP, CHUNK), lambda j, w: (0, group, 2 * w[0] + j)),
        ),
        input_output_aliases=aliases,
        cost_estimate=pl.CostEstimate(flops=0, bytes_accessed=1 << 20, transcendentals=0),
        compiler_params=params(4),
        name="place",
    )(*args)


def neighbours(views, tiles):
    right = []
    for v in range(views):
        for t in range(tiles):
            if (t + v) % 2 == 0:
                right.append((v * tiles + t, (1 - v) * tiles + t))
            elif t + 1 < tiles:
                right.append((v * tiles + t, v * tiles + t + 1))
    return right


def per_device(views_data, psf_axial, psf_rows, psf_cols):
    views, tiles, bands = lax.axis_size("view"), lax.axis_size("tx"), lax.axis_size("ty")
    swap = [(0, 1), (1, 0)]
    right = neighbours(views, tiles)
    left = [(b, a) for a, b in right]
    down = [(i, i + 1) for i in range(bands - 1)]
    up = [(b, a) for a, b in down]
    half = lax.rem(lax.axis_index("tx") + lax.axis_index("view"), 2)

    def other_rows(views_data, *starts):
        at = (1 - half) * HALF
        return jnp.concatenate(
            [
                lax.dynamic_slice(views_data, (0, 0, row, at), (1, Z, rows, HALF))[0]
                for row, rows in starts
            ],
            axis=1,
        )

    border = other_rows(views_data, (0, GROUP), (ROWS - GROUP, GROUP))
    later, axial, rows, cols, border = lax.optimization_barrier(
        (views_data, psf_axial, psf_rows, psf_cols, border)
    )
    border_in = lax.ppermute(border, "view", swap)
    raw = jnp.concatenate([axial[0], rows[0], cols[0]])
    raw_other = lax.ppermute(raw, "view", swap)
    upper_in = lax.ppermute(other_rows(later, (GROUP, GROUP)), "view", swap)
    last_rows, raw_other = lax.optimization_barrier(
        (other_rows(later, (2 * GROUP, GROUP)), raw_other)
    )
    lower_in = lax.ppermute(last_rows, "view", swap)

    view = lax.axis_index("view")
    where = jnp.stack([half, view]).astype(jnp.int32)
    there = (1 - half).astype(jnp.int32)[None]

    def sides(west, east):
        return lax.ppermute(west, ("view", "tx"), right), lax.ppermute(east, ("view", "tx"), left)

    border, border_east, border_west, to_up, to_down = turn(where, views_data, border_in, (0, 3))
    raw, raw_other, to_up, to_down = lax.optimization_barrier((raw, raw_other, to_up, to_down))
    north = lax.ppermute(to_down, "ty", down)
    south = lax.ppermute(to_up, "ty", up)

    def norm(taps):
        parts = (taps[:21], taps[21:28], taps[28:35])
        return jnp.concatenate([part / jnp.sum(part) for part in parts])

    own, other = norm(raw), norm(raw_other)
    lanes = jnp.concatenate(
        [
            jnp.broadcast_to(jnp.where(view == 0, own, other)[:, None], (own.shape[0], Z)),
            jnp.broadcast_to(jnp.where(view == 0, other, own)[:, None], (own.shape[0], Z)),
        ],
        axis=1,
    )
    blur, adj = matrices(lanes[:21])
    taps = jnp.zeros((16, LANES), jnp.float32)
    taps = taps.at[0:7].set(lanes[28:35]).at[8:15].set(lanes[21:28])

    upper_in, blur, adj = lax.optimization_barrier((upper_in, blur, adj))
    upper, upper_east, upper_west = turn(where, views_data, upper_in, (1,))
    west, east = sides(
        jnp.concatenate([border_east, upper_east]), jnp.concatenate([border_west, upper_west])
    )
    lower, lower_east, lower_west = turn(
        where, views_data, lower_in, (2,), (north, south)
    )
    last_west, last_east = sides(lower_east, lower_west)
    recorded = (north, west, last_west, border, upper, lower, east, last_east, south)

    estimate, top, low = iterate(
        recorded, None, taps, blur, adj, first=True, row0=0, n_out=ROWS
    )
    def piece(group, field):
        return iterate(
            recorded, field, taps, blur, adj, first=False, row0=GROUP * group, n_out=GROUP
        )

    field = (lax.ppermute(low, "ty", down), estimate, lax.ppermute(top, "ty", up))
    theirs = []
    whole = None
    for group in (1, 2, 0, 3):
        block = piece(group, field)
        theirs.append((group, lax.ppermute(block, "view", swap)))
        whole = place(where[:1], block, whole, group)
    for group, block in theirs:
        whole = place(there, block, whole, group)
    return whole


def solution(mesh):
    placed = (P("view", None, "ty", "tx"), P("view", None), P("view", None), P("view", None))
    return jax.shard_map(
        per_device, mesh=mesh, in_specs=placed, out_specs=P(None, "ty", "tx"), check_vma=False
    )
```

```python
import functools

import jax
import jax.numpy as jnp
from jax import lax
from jax.experimental import pallas as pl
from jax.experimental.pallas import tpu as pltpu
from jax.sharding import PartitionSpec as P

ITERS = 2
Z = 64
LANES = 128
ROWS = 32
HALF = 256
CHUNK = 128
PAD = 6
REACH = 3
SIDE = 8
MARGIN = 16
GROUP = 8
EXT_R = ROWS + 2 * PAD
EXT_C = HALF + 2 * MARGIN
MIB = 1024 * 1024
UNROLL = 8
UPDATE = 128
TINY = 1e-30


def params(mib):
    return pltpu.CompilerParams(vmem_limit_bytes=mib * MIB)


def in_hbm(array):
    return pltpu.with_memory_space_constraint(array, pltpu.HBM)


def blocks_of(total, largest=96):
    out, at = [], 0
    while at < total:
        size = min(largest, total - at)
        out.append((at, size))
        at += size
    return out


def matrices_kernel(kz_ref, blur_ref, adj_ref):
    taps = kz_ref.shape[0]
    lane = lax.broadcasted_iota(jnp.int32, (Z, LANES), 1)
    row = lax.broadcasted_iota(jnp.int32, (Z, LANES), 0)
    offset = row - lax.rem(lane, Z) + taps // 2
    mat = jnp.zeros((Z, LANES), jnp.float32)
    for t in range(taps):
        mat = mat + jnp.where(offset == t, kz_ref[t : t + 1, :], 0.0)
    high = mat.astype(jnp.bfloat16)
    low = (mat - high.astype(jnp.float32)).astype(jnp.bfloat16)
    blur_ref[0:Z, 0:LANES] = high
    blur_ref[0:Z, LANES:] = low
    blur_ref[Z:, 0:LANES] = high
    blur_ref[Z:, LANES:] = jnp.zeros((Z, LANES), jnp.bfloat16)
    adj = jnp.concatenate([mat, mat], axis=0).T * 0.5
    ahigh = adj.astype(jnp.bfloat16).astype(jnp.float32)
    alow = adj - ahigh
    first = lax.broadcasted_iota(jnp.int32, (LANES, LANES), 1) < Z
    adj_ref[0:LANES, :] = jnp.where(first, ahigh, alow).astype(jnp.bfloat16)
    adj_ref[LANES:, :] = jnp.where(first, ahigh, 0.0).astype(jnp.bfloat16)


def matrices(kz):
    return pl.pallas_call(
        matrices_kernel,
        out_shape=(
            jax.ShapeDtypeStruct((2 * Z, 2 * LANES), jnp.bfloat16),
            jax.ShapeDtypeStruct((2 * LANES, LANES), jnp.bfloat16),
        ),
        compiler_params=params(4),
        name="matrices",
    )(kz)


def turn_kernel(groups, corners, where_ref, own_ref, other_ref, *refs):
    if corners:
        halos, refs = refs[:2], refs[2:]
    out_ref, west_ref, east_ref = refs[:3]
    refs = refs[3:]
    own, other, sems, corner_sems = refs[-4:]
    if corners:
        kept, refs = refs[:2], refs[2:]
        out_hbm, out_ref = out_ref, refs[0]
    corner_copies = []
    if corners:
        columns = (
            (west_ref, HALF - MARGIN, HALF + CHUNK - MARGIN),
            (east_ref, 0, HALF),
        )
        for side, (strip, near, far) in enumerate(columns):
            for n, halo in enumerate(halos):
                for m, at in enumerate((near, far)):
                    row = GROUP + REACH * (2 * n + m)
                    corner_copies.append(
                        pltpu.make_async_copy(
                            halo.at[:, pl.ds(at, MARGIN), :],
                            strip.at[pl.ds(row, REACH), :, :],
                            corner_sems.at[4 * side + 2 * n + m],
                        )
                    )
        for n, halo in enumerate(halos):
            corner_copies.append(pltpu.make_async_copy(halo, kept[n], corner_sems.at[9 + n]))
    for c in corner_copies:
        c.start()
    half, first = where_ref[0], where_ref[1] == 0
    blocks = [(i, j) for i in range(len(groups)) for j in range(2)]
    copies = []
    for n, (i, j) in enumerate(blocks):
        at = pl.multiple_of(half * HALF + j * CHUNK, CHUNK)
        mine = own_ref.at[0, :, pl.ds(groups[i] * GROUP, GROUP), pl.ds(at, CHUNK)]
        theirs = other_ref.at[:, pl.ds(i * GROUP, GROUP), pl.ds(j * CHUNK, CHUNK)]
        copies.append(
            (
                pltpu.make_async_copy(mine, own.at[n], sems.at[0, n]),
                pltpu.make_async_copy(theirs, other.at[n], sems.at[1, n]),
            )
        )
    for pair in copies:
        for c in pair:
            c.start()
    for n, (i, j) in enumerate(blocks):
        for c in copies[n]:
            c.wait()
        flat = own.at[n].reshape(Z * GROUP, CHUNK)
        flat_other = other.at[n].reshape(Z * GROUP, CHUNK)
        for y in range(GROUP):
            mine = flat[pl.ds(y, Z, stride=GROUP), :]
            theirs = flat_other[pl.ds(y, Z, stride=GROUP), :]
            pair = jnp.concatenate(
                [jnp.where(first, mine, theirs), jnp.where(first, theirs, mine)], axis=0
            ).T
            row = i * GROUP + y
            out_ref[row, pl.ds(j * CHUNK, CHUNK), :] = pair
            if j == 0:
                east_ref[row] = pair[:MARGIN]
            else:
                west_ref[row] = pair[CHUNK - MARGIN :]
    if corners:
        corner_copies.append(pltpu.make_async_copy(out_ref, out_hbm, corner_sems.at[8]))
        corner_copies[-1].start()
    for c in corner_copies:
        c.wait()
    if len(groups) == 1:
        return
    up_ref, down_ref = refs[:2]
    lower = lax.broadcasted_iota(jnp.int32, (CHUNK, LANES), 1) < Z
    low = 2 * GROUP - PAD
    for ref, near, far in ((up_ref, 0, REACH), (down_ref, low + REACH, low)):
        for y in range(REACH):
            ref[y, pl.ds(0, HALF), :] = out_ref[near + y]
            ends = []
            for j in range(2):
                r = out_ref[far + y, pl.ds(j * CHUNK, CHUNK), :]
                ends.append((r + pltpu.roll(r, Z, 1)) * 0.5)
            ref[y, pl.ds(HALF, CHUNK), :] = jnp.where(lower, ends[0], ends[1])


def turn(where, recorded, received, groups, halos=()):
    rows = len(groups) * GROUP
    block = pltpu.VMEM((2 * len(groups), Z, GROUP, CHUNK), jnp.float32)
    strip_rows = rows + (4 * REACH if halos else 0)
    strip = jax.ShapeDtypeStruct((strip_rows, MARGIN, LANES), jnp.float32)
    main = pltpu.HBM if halos else jax.ShapeDtypeStruct
    out = [main((rows, HALF, LANES), jnp.float32), strip, strip]
    if halos:
        out += [pltpu.HBM(halo.shape, jnp.float32) for halo in halos]
    if len(groups) > 1:
        out += [jax.ShapeDtypeStruct((REACH, HALF + CHUNK, LANES), jnp.float32)] * 2
    return pl.pallas_call(
        functools.partial(turn_kernel, groups, bool(halos)),
        out_shape=tuple(out),
        in_specs=[
            pl.BlockSpec(memory_space=pltpu.SMEM),
            pl.BlockSpec(memory_space=pltpu.HBM),
            pl.BlockSpec(memory_space=pl.ANY),
        ]
        + [pl.BlockSpec(memory_space=pl.ANY)] * len(halos),
        out_specs=(pl.BlockSpec(memory_space=pltpu.HBM if halos else pltpu.VMEM),)
        + (pl.BlockSpec(memory_space=pltpu.VMEM),) * 2
        + (pl.BlockSpec(memory_space=pltpu.HBM if halos else pltpu.VMEM),) * (len(out) - 3),
        scratch_shapes=([pltpu.VMEM((rows, HALF, LANES), jnp.float32)] if halos else [])
        + [
            block,
            block,
            pltpu.SemaphoreType.DMA((2, 2 * len(groups))),
            pltpu.SemaphoreType.DMA((11,)),
        ],
        cost_estimate=pl.CostEstimate(
            flops=0, bytes_accessed=1024, transcendentals=0
        ),
        compiler_params=params(10),
        name="turn",
    )(where, in_hbm(recorded), received, *halos)


GROUPS = tuple((PAD + GROUP * g, GROUP) for g in range(4))
SPANS = ((REACH, REACH),) + GROUPS + ((EXT_R - PAD, REACH),)
FIRST_SPANS = ((0, REACH),) + SPANS + ((EXT_R - REACH, REACH),)
NEXT_SPANS = ((0, PAD),) + GROUPS + ((EXT_R - PAD, PAD),)
HOMES = (
    ((2, 8), (0, 0), (7, 8)),
    ((1, 0), (3, 0), (6, 0)),
    ((1, 16), (4, 0), (6, 16)),
    ((2, 0), (5, 0), (7, 0)),
    ((1, 8), (3, 8), (6, 8)),
    ((2, 14), (8, 0), (7, 14)),
)
OUTER = (11, 17)


def iterate_kernel(first, row0, n_out, present, *refs):
    n_in = n_out + 2 * PAD
    width = EXT_C if first else EXT_C - 2 * SIDE
    shift = 0 if first else SIDE
    inner = width - 2 * SIDE
    fold = (EXT_C - 2 * SIDE) // 2
    pieces = iter(refs)
    taken = [next(pieces) if there else None for there in present]
    recorded, field, refs = taken[:9], taken[9:], tuple(pieces)
    taps_ref, blur_hbm, adj_hbm = refs[:3]
    refs = refs[3:]
    if first:
        out_ref, top_ref, low_ref = refs[:3]
        refs = refs[3:]
    else:
        out_ref, refs = refs[0], refs[1:]
    r_buf, e_buf, xz_buf, xr_buf, pack, tmp, blur_ref, adj_ref, r_sem, e_sem, m_sem = refs
    north, south = recorded[0], recorded[8]
    lower = lax.broadcasted_iota(jnp.int32, (width, LANES), 1) < Z

    def window(span, lo, hi):
        at, count = span
        a, b = max(at, lo), min(at + count, hi)
        return (a, b) if a < b else None

    def r_copies(k):
        got = window(SPANS[k], row0 + REACH, row0 + n_in - REACH)
        if got is None:
            return []
        a, b = got
        rows = pl.ds(a - row0, b - a)
        pairs = []
        ranges = ((0, MARGIN), (MARGIN, MARGIN + HALF), (MARGIN + HALF, EXT_C))
        for (home, base), (lo, hi) in zip(HOMES[k], ranges):
            src = recorded[home]
            c, d = max(lo, shift), min(hi, shift + width)
            pairs.append(
                (
                    src.at[pl.ds(base + a - SPANS[k][0], b - a), pl.ds(c - lo, d - c), :],
                    r_buf.at[rows, pl.ds(c - shift, d - c), :],
                )
            )
        return [
            pltpu.make_async_copy(src, dst, r_sem.at[k, n]) for n, (src, dst) in enumerate(pairs)
        ]

    def e_copies(k):
        if first:
            if 0 < k < 7:
                return []
            n = 0 if k == 0 else 1
            halo, rows = (north if n == 0 else south), pl.ds(OUTER[n], REACH)
            pairs = (
                (recorded[2].at[rows, :, :], pl.ds(0, MARGIN)),
                (halo.at[:, pl.ds(HALF, CHUNK), :], pl.ds(MARGIN, CHUNK)),
                (recorded[7].at[rows, :, :], pl.ds(MARGIN + CHUNK, MARGIN)),
            )
            return [
                pltpu.make_async_copy(src, pack.at[n, :, cols, :], e_sem.at[k, i])
                for i, (src, cols) in enumerate(pairs)
            ]
        got = window(NEXT_SPANS[k], row0, row0 + n_in)
        if got is None:
            return []
        a, b = got
        if k in (0, 5):
            src, dst = (field[0] if k == 0 else field[2]), pack.at[0 if k == 0 else 1]
        else:
            at = GROUP * (k - 1) + a - NEXT_SPANS[k][0]
            src, dst = field[1].at[pl.ds(at, b - a), :, :], e_buf.at[pl.ds(a - row0, b - a), :, :]
        return [pltpu.make_async_copy(src, dst, e_sem.at[k, 0])]

    recorded_in = [r_copies(k) for k in range(6)]
    e_spans = FIRST_SPANS if first else NEXT_SPANS
    field_in = [e_copies(k) for k in range(len(e_spans))]
    matrices_in = [
        pltpu.make_async_copy(blur_hbm, blur_ref, m_sem.at[0]),
        pltpu.make_async_copy(adj_hbm, adj_ref, m_sem.at[1]),
    ]
    for group in [matrices_in] + field_in + recorded_in:
        for c in group:
            c.start()

    def over_rows(start, count, steps, unroll):
        def rows_from(at, many):
            for step in steps:
                for slot in range(many):
                    step(slot, at + slot)

        def body(i, carry):
            rows_from(start + unroll * i, unroll)
            return carry

        lax.fori_loop(0, count // unroll, body, 0)
        if count % unroll:
            rows_from(start + count - count % unroll, count % unroll)

    kx = [taps_ref[t : t + 1, :] for t in range(7)]
    ky = [taps_ref[8 + t : 9 + t, :] for t in range(7)]
    col_blocks = blocks_of(width)

    def cols_pass(slot, taps, dst_ref, row):
        for at, size in col_blocks:
            acc = taps[0] * tmp[slot, pl.ds(5 + at, size), :]
            for t in range(1, 7):
                acc = acc + taps[t] * tmp[slot, pl.ds(5 + t + at, size), :]
            dst_ref[row, pl.ds(at, size), :] = acc

    def blur_row(slot, row, started):
        if not started:
            r = r_buf[row]
            e = (r + pltpu.roll(r, Z, 1)) * 0.5
            e_buf[row] = e
        else:
            e = e_buf[row]
        high = e.astype(jnp.bfloat16).astype(jnp.float32)
        split = jnp.where(lower, high, e - high).astype(jnp.bfloat16)
        both = jnp.dot(split, blur_ref[...], preferred_element_type=jnp.float32)
        tmp[slot, pl.ds(8, width), :] = both[:, :LANES] + both[:, LANES:]

    for slot in range(UNROLL):
        tmp[slot, pl.ds(0, 8), :] = jnp.zeros((8, LANES), jnp.float32)
        tmp[slot, pl.ds(8 + width, 8), :] = jnp.zeros((8, LANES), jnp.float32)

    def both_halves(packed, turned, size, low_first):
        keep = lower[:size] if low_first else jnp.logical_not(lower[:size])
        return jnp.where(keep, packed, turned)

    for c in matrices_in:
        c.wait()
    if first:
        plan = [(0, PAD, field_in[0] + recorded_in[0], 0, range(REACH))]
        plan += [GROUPS[g] + (recorded_in[1 + g], None, ()) for g in range(4)]
        plan += [(EXT_R - PAD, PAD, recorded_in[5] + field_in[7], 1, range(REACH, PAD))]
    else:
        plan = []
        for k, span in enumerate(NEXT_SPANS):
            got = window(span, row0, row0 + n_in)
            if got is not None:
                edge = {0: 0, 5: 1}.get(k)
                packed_slots = () if edge is None else range(PAD)
                plan.append((got[0] - row0, got[1] - got[0], field_in[k], edge, packed_slots))

    for base, count, waits, edge, packed_slots in plan:
        for c in waits:
            c.wait()

        def halo_row(slot, row, edge=edge, packed_slots=packed_slots):
            halo = slot in packed_slots
            if halo:
                packed = pack[edge, slot - packed_slots[0]]
                turned = pltpu.roll(packed, Z, 1)
                if first:
                    parts = (
                        (0, 0, MARGIN, False),
                        (MARGIN, MARGIN, CHUNK, True),
                        (MARGIN + CHUNK, MARGIN, CHUNK, False),
                        (MARGIN + HALF, MARGIN + CHUNK, MARGIN, True),
                    )
                else:
                    parts = ((0, 0, fold, True), (fold, 0, fold, False))
                for to, at, size, low_first in parts:
                    e_buf[row, pl.ds(to, size), :] = both_halves(
                        packed[at : at + size], turned[at : at + size], size, low_first
                    )
            blur_row(slot, row, halo or not first)

        over_rows(
            base,
            count,
            (halo_row, lambda slot, row: cols_pass(slot, kx, xz_buf, row)),
            UNROLL,
        )

    if not first:
        for group in recorded_in:
            for c in group:
                c.wait()

    def rows_pass(src_ref, taps, row, at, size):
        acc = taps[0] * src_ref[row - 3, pl.ds(at, size), :]
        for t in range(1, 7):
            acc = acc + taps[t] * src_ref[row - 3 + t, pl.ds(at, size), :]
        return acc

    def ratio_row(slot, row):
        for at, size in col_blocks:
            blurred = rows_pass(xz_buf, ky, row, at, size)
            ratio = r_buf[row, pl.ds(at, size), :] / jnp.maximum(blurred, TINY)
            tmp[slot, pl.ds(8 + at, size), :] = ratio

    over_rows(3, n_in - 6, (ratio_row, lambda slot, row: cols_pass(slot, kx[::-1], xr_buf, row)), UNROLL)

    def update_row(slot, y):
        row = PAD + y
        for at, size in blocks_of(inner, UPDATE):
            spread = rows_pass(xr_buf, ky[::-1], row, SIDE + at, size)
            high = spread.astype(jnp.bfloat16)
            low = (spread - high.astype(jnp.float32)).astype(jnp.bfloat16)
            both = jnp.dot(
                jnp.concatenate([high, low], axis=1),
                adj_ref[...],
                preferred_element_type=jnp.float32,
            )
            factor = both + pltpu.roll(both, Z, 1)
            new = e_buf[row, pl.ds(SIDE + at, size), :] * factor
            if first:
                out_ref[y, pl.ds(at, size), :] = new
            else:
                flat = out_ref.at[at // CHUNK].reshape(Z * GROUP, CHUNK)
                flat[pl.ds(y, Z, stride=GROUP), :] = new.T[:Z]

    over_rows(0, n_out, (update_row,), UNROLL)
    if first:
        for y in range(PAD):
            for ref, row in ((top_ref, y), (low_ref, ROWS - PAD + y)):
                ref[y] = jnp.where(
                    lower[:fold], out_ref[row, pl.ds(0, fold), :], out_ref[row, pl.ds(fold, fold), :]
                )


def iterate(recorded, field, taps, blur, adj, *, first, row0, n_out):
    n_in = n_out + 2 * PAD
    width = EXT_C if first else EXT_C - 2 * SIDE
    fold = (EXT_C - 2 * SIDE) // 2
    pieces = list(recorded) + (list(field) if field is not None else [])
    if not first and row0 >= PAD:
        pieces[0] = pieces[9] = None
    if not first and row0 + n_in <= EXT_R - PAD:
        pieces[8] = pieces[11] = None
    for k in (0, 5, 8):
        if pieces[k] is not None:
            pieces[k] = in_hbm(pieces[k])
    present = tuple(piece is not None for piece in pieces)
    pieces = [piece for piece in pieces if piece is not None]
    if first:
        edge = jax.ShapeDtypeStruct((PAD, fold, LANES), jnp.float32)
        out = (jax.ShapeDtypeStruct((ROWS, EXT_C - 2 * SIDE, LANES), jnp.float32), edge, edge)
        out_specs = (pl.BlockSpec(memory_space=pltpu.VMEM),) * 3
    else:
        out = jax.ShapeDtypeStruct((2, Z, GROUP, CHUNK), jnp.float32)
        out_specs = pl.BlockSpec(memory_space=pltpu.VMEM)
    row = pltpu.VMEM((n_in, width, LANES), jnp.float32)
    vregs = n_in * width // 8
    return pl.pallas_call(
        functools.partial(iterate_kernel, first, row0, n_out, present),
        out_shape=out,
        in_specs=[pl.BlockSpec(memory_space=pl.ANY)] * len(pieces)
        + [pl.BlockSpec(memory_space=pltpu.VMEM)]
        + [pl.BlockSpec(memory_space=pl.ANY)] * 2,
        out_specs=out_specs,
        scratch_shapes=[
            row,
            row,
            row,
            row,
            pltpu.VMEM(
                (2, REACH, CHUNK + 2 * MARGIN, LANES) if first else (2, PAD, fold, LANES),
                jnp.float32,
            ),
            pltpu.VMEM((UNROLL, width + 16, LANES), jnp.float32),
            pltpu.VMEM((2 * Z, 2 * LANES), jnp.bfloat16),
            pltpu.VMEM((2 * LANES, LANES), jnp.bfloat16),
            pltpu.SemaphoreType.DMA((6, 3)),
            pltpu.SemaphoreType.DMA((8, 3)),
            pltpu.SemaphoreType.DMA((2,)),
        ],
        cost_estimate=pl.CostEstimate(
            flops=0, bytes_accessed=vregs * 4096 if first else 4096, transcendentals=0
        ),
        compiler_params=params(30 if first else 13),
        name="iterate",
    )(*pieces, taps, in_hbm(blur), in_hbm(adj))


def place_kernel(where_ref, *refs):
    refs[-1][...] = refs[0][0]


def place(where, block, whole, group):
    args = [where, block]
    in_specs = [pl.BlockSpec((1, Z, GROUP, CHUNK), lambda j, w: (j, 0, 0, 0))]
    aliases = {}
    if whole is not None:
        args.append(whole)
        in_specs.append(pl.BlockSpec(memory_space=pl.ANY))
        aliases = {2: 0}
    return pl.pallas_call(
        place_kernel,
        out_shape=jax.ShapeDtypeStruct((Z, ROWS, 2 * HALF), jnp.float32),
        grid_spec=pltpu.PrefetchScalarGridSpec(
            num_scalar_prefetch=1,
            grid=(2,),
            in_specs=in_specs,
            out_specs=pl.BlockSpec((Z, GROUP, CHUNK), lambda j, w: (0, group, 2 * w[0] + j)),
        ),
        input_output_aliases=aliases,
        cost_estimate=pl.CostEstimate(flops=0, bytes_accessed=1 << 20, transcendentals=0),
        compiler_params=params(4),
        name="place",
    )(*args)


def neighbours(views, tiles):
    right = []
    for v in range(views):
        for t in range(tiles):
            if (t + v) % 2 == 0:
                right.append((v * tiles + t, (1 - v) * tiles + t))
            elif t + 1 < tiles:
                right.append((v * tiles + t, v * tiles + t + 1))
    return right


def per_device(views_data, psf_axial, psf_rows, psf_cols):
    views, tiles, bands = lax.axis_size("view"), lax.axis_size("tx"), lax.axis_size("ty")
    swap = [(0, 1), (1, 0)]
    right = neighbours(views, tiles)
    left = [(b, a) for a, b in right]
    down = [(i, i + 1) for i in range(bands - 1)]
    up = [(b, a) for a, b in down]
    half = lax.rem(lax.axis_index("tx") + lax.axis_index("view"), 2)

    def other_rows(views_data, *starts):
        at = (1 - half) * HALF
        return jnp.concatenate(
            [
                lax.dynamic_slice(views_data, (0, 0, row, at), (1, Z, rows, HALF))[0]
                for row, rows in starts
            ],
            axis=1,
        )

    border = other_rows(views_data, (0, GROUP), (ROWS - GROUP, GROUP))
    later, axial, rows, cols, border = lax.optimization_barrier(
        (views_data, psf_axial, psf_rows, psf_cols, border)
    )
    border_in = lax.ppermute(border, "view", swap)
    raw = jnp.concatenate([axial[0], rows[0], cols[0]])
    raw_other = lax.ppermute(raw, "view", swap)
    upper_in = lax.ppermute(other_rows(later, (GROUP, GROUP)), "view", swap)
    last_rows, raw_other = lax.optimization_barrier(
        (other_rows(later, (2 * GROUP, GROUP)), raw_other)
    )
    lower_in = lax.ppermute(last_rows, "view", swap)

    view = lax.axis_index("view")
    where = jnp.stack([half, view]).astype(jnp.int32)
    there = (1 - half).astype(jnp.int32)[None]

    def sides(west, east):
        return lax.ppermute(west, ("view", "tx"), right), lax.ppermute(east, ("view", "tx"), left)

    border, border_east, border_west, to_up, to_down = turn(where, views_data, border_in, (0, 3))
    raw, raw_other, to_up, to_down = lax.optimization_barrier((raw, raw_other, to_up, to_down))
    north = lax.ppermute(to_down, "ty", down)
    south = lax.ppermute(to_up, "ty", up)

    def norm(taps):
        parts = (taps[:21], taps[21:28], taps[28:35])
        return jnp.concatenate([part / jnp.sum(part) for part in parts])

    own, other = norm(raw), norm(raw_other)
    lanes = jnp.concatenate(
        [
            jnp.broadcast_to(jnp.where(view == 0, own, other)[:, None], (own.shape[0], Z)),
            jnp.broadcast_to(jnp.where(view == 0, other, own)[:, None], (own.shape[0], Z)),
        ],
        axis=1,
    )
    blur, adj = matrices(lanes[:21])
    taps = jnp.zeros((16, LANES), jnp.float32)
    taps = taps.at[0:7].set(lanes[28:35]).at[8:15].set(lanes[21:28])

    upper_in, blur, adj = lax.optimization_barrier((upper_in, blur, adj))
    upper, upper_east, upper_west = turn(where, views_data, upper_in, (1,))
    west, east = sides(
        jnp.concatenate([border_east, upper_east]), jnp.concatenate([border_west, upper_west])
    )
    lower, lower_east, lower_west, north, south = turn(
        where, views_data, lower_in, (2,), (north, south)
    )
    last_west, last_east = sides(lower_east, lower_west)
    recorded = (north, west, last_west, border, upper, lower, east, last_east, south)

    estimate, top, low = iterate(
        recorded, None, taps, blur, adj, first=True, row0=0, n_out=ROWS
    )
    def piece(group, field):
        return iterate(
            recorded, field, taps, blur, adj, first=False, row0=GROUP * group, n_out=GROUP
        )

    field = (lax.ppermute(low, "ty", down), estimate, lax.ppermute(top, "ty", up))
    theirs = []
    whole = None
    for group in (1, 2, 0, 3):
        block = piece(group, field)
        theirs.append((group, lax.ppermute(block, "view", swap)))
        whole = place(where[:1], block, whole, group)
    for group, block in theirs:
        whole = place(there, block, whole, group)
    return whole


def solution(mesh):
    placed = (P("view", None, "ty", "tx"), P("view", None), P("view", None), P("view", None))
    return jax.shard_map(
        per_device, mesh=mesh, in_specs=placed, out_specs=P(None, "ty", "tx"), check_vma=False
    )
```

```python
import functools

import jax
import jax.numpy as jnp
from jax import lax
from jax.experimental import pallas as pl
from jax.experimental.pallas import tpu as pltpu
from jax.sharding import PartitionSpec as P

ITERS = 2
Z = 64
LANES = 128
ROWS = 32
HALF = 256
CHUNK = 128
PAD = 6
REACH = 3
SIDE = 8
MARGIN = 16
GROUP = 8
EXT_R = ROWS + 2 * PAD
EXT_C = HALF + 2 * MARGIN
MIB = 1024 * 1024
UNROLL = 8
UPDATE = 128
TINY = 1e-30


def params(mib):
    return pltpu.CompilerParams(vmem_limit_bytes=mib * MIB)


def in_hbm(array):
    return pltpu.with_memory_space_constraint(array, pltpu.HBM)


def blocks_of(total, largest=96):
    out, at = [], 0
    while at < total:
        size = min(largest, total - at)
        out.append((at, size))
        at += size
    return out


def matrices_kernel(kz_ref, blur_ref, adj_ref):
    taps = kz_ref.shape[0]
    lane = lax.broadcasted_iota(jnp.int32, (Z, LANES), 1)
    row = lax.broadcasted_iota(jnp.int32, (Z, LANES), 0)
    offset = row - lax.rem(lane, Z) + taps // 2
    mat = jnp.zeros((Z, LANES), jnp.float32)
    for t in range(taps):
        mat = mat + jnp.where(offset == t, kz_ref[t : t + 1, :], 0.0)
    high = mat.astype(jnp.bfloat16)
    low = (mat - high.astype(jnp.float32)).astype(jnp.bfloat16)
    blur_ref[0:Z, 0:LANES] = high
    blur_ref[0:Z, LANES:] = low
    blur_ref[Z:, 0:LANES] = high
    blur_ref[Z:, LANES:] = jnp.zeros((Z, LANES), jnp.bfloat16)
    adj = jnp.concatenate([mat, mat], axis=0).T * 0.5
    ahigh = adj.astype(jnp.bfloat16).astype(jnp.float32)
    alow = adj - ahigh
    first = lax.broadcasted_iota(jnp.int32, (LANES, LANES), 1) < Z
    adj_ref[0:LANES, :] = jnp.where(first, ahigh, alow).astype(jnp.bfloat16)
    adj_ref[LANES:, :] = jnp.where(first, ahigh, 0.0).astype(jnp.bfloat16)


def matrices(kz):
    return pl.pallas_call(
        matrices_kernel,
        out_shape=(
            jax.ShapeDtypeStruct((2 * Z, 2 * LANES), jnp.bfloat16),
            jax.ShapeDtypeStruct((2 * LANES, LANES), jnp.bfloat16),
        ),
        compiler_params=params(4),
        name="matrices",
    )(kz)


def turn_kernel(groups, corners, where_ref, own_ref, other_ref, *refs):
    if corners:
        halos, refs = refs[:2], refs[2:]
    out_ref, west_ref, east_ref = refs[:3]
    refs = refs[3:]
    own, other, sems, corner_sems = refs[-4:]
    if corners:
        kept, refs = refs[:2], refs[2:]
        out_hbm, out_ref = out_ref, refs[0]
    corner_copies = []
    if corners:
        columns = (
            (west_ref, HALF - MARGIN, HALF + CHUNK - MARGIN),
            (east_ref, 0, HALF),
        )
        for side, (strip, near, far) in enumerate(columns):
            for n, halo in enumerate(halos):
                for m, at in enumerate((near, far)):
                    row = GROUP + REACH * (2 * n + m)
                    corner_copies.append(
                        pltpu.make_async_copy(
                            halo.at[:, pl.ds(at, MARGIN), :],
                            strip.at[pl.ds(row, REACH), :, :],
                            corner_sems.at[4 * side + 2 * n + m],
                        )
                    )
        for n, halo in enumerate(halos):
            corner_copies.append(pltpu.make_async_copy(halo, kept[n], corner_sems.at[9 + n]))
    half, first = where_ref[0], where_ref[1] == 0
    blocks = [(i, j) for i in range(len(groups)) for j in range(2)]
    copies = []
    for n, (i, j) in enumerate(blocks):
        at = pl.multiple_of(half * HALF + j * CHUNK, CHUNK)
        mine = own_ref.at[0, :, pl.ds(groups[i] * GROUP, GROUP), pl.ds(at, CHUNK)]
        theirs = other_ref.at[:, pl.ds(i * GROUP, GROUP), pl.ds(j * CHUNK, CHUNK)]
        copies.append(
            (
                pltpu.make_async_copy(mine, own.at[n], sems.at[0, n]),
                pltpu.make_async_copy(theirs, other.at[n], sems.at[1, n]),
            )
        )
    for pair in copies:
        for c in pair:
            c.start()
    for c in corner_copies:
        c.start()
    for n, (i, j) in enumerate(blocks):
        for c in copies[n]:
            c.wait()
        flat = own.at[n].reshape(Z * GROUP, CHUNK)
        flat_other = other.at[n].reshape(Z * GROUP, CHUNK)
        for y in range(GROUP):
            mine = flat[pl.ds(y, Z, stride=GROUP), :]
            theirs = flat_other[pl.ds(y, Z, stride=GROUP), :]
            pair = jnp.concatenate(
                [jnp.where(first, mine, theirs), jnp.where(first, theirs, mine)], axis=0
            ).T
            row = i * GROUP + y
            out_ref[row, pl.ds(j * CHUNK, CHUNK), :] = pair
            if j == 0:
                east_ref[row] = pair[:MARGIN]
            else:
                west_ref[row] = pair[CHUNK - MARGIN :]
        if corners:
            turned = pl.ds(j * CHUNK, CHUNK)
            corner_copies.append(
                pltpu.make_async_copy(
                    out_ref.at[:, turned, :], out_hbm.at[:, turned, :], corner_sems.at[11 + j]
                )
            )
            corner_copies[-1].start()
    for c in corner_copies:
        c.wait()
    if len(groups) == 1:
        return
    up_ref, down_ref = refs[:2]
    lower = lax.broadcasted_iota(jnp.int32, (CHUNK, LANES), 1) < Z
    low = 2 * GROUP - PAD
    for ref, near, far in ((up_ref, 0, REACH), (down_ref, low + REACH, low)):
        for y in range(REACH):
            ref[y, pl.ds(0, HALF), :] = out_ref[near + y]
            ends = []
            for j in range(2):
                r = out_ref[far + y, pl.ds(j * CHUNK, CHUNK), :]
                ends.append((r + pltpu.roll(r, Z, 1)) * 0.5)
            ref[y, pl.ds(HALF, CHUNK), :] = jnp.where(lower, ends[0], ends[1])


def turn(where, recorded, received, groups, halos=()):
    rows = len(groups) * GROUP
    block = pltpu.VMEM((2 * len(groups), Z, GROUP, CHUNK), jnp.float32)
    strip_rows = rows + (4 * REACH if halos else 0)
    strip = jax.ShapeDtypeStruct((strip_rows, MARGIN, LANES), jnp.float32)
    main = pltpu.HBM if halos else jax.ShapeDtypeStruct
    out = [main((rows, HALF, LANES), jnp.float32), strip, strip]
    if halos:
        out += [pltpu.HBM(halo.shape, jnp.float32) for halo in halos]
    if len(groups) > 1:
        out += [jax.ShapeDtypeStruct((REACH, HALF + CHUNK, LANES), jnp.float32)] * 2
    return pl.pallas_call(
        functools.partial(turn_kernel, groups, bool(halos)),
        out_shape=tuple(out),
        in_specs=[
            pl.BlockSpec(memory_space=pltpu.SMEM),
            pl.BlockSpec(memory_space=pltpu.HBM),
            pl.BlockSpec(memory_space=pl.ANY),
        ]
        + [pl.BlockSpec(memory_space=pl.ANY)] * len(halos),
        out_specs=(pl.BlockSpec(memory_space=pltpu.HBM if halos else pltpu.VMEM),)
        + (pl.BlockSpec(memory_space=pltpu.VMEM),) * 2
        + (pl.BlockSpec(memory_space=pltpu.HBM if halos else pltpu.VMEM),) * (len(out) - 3),
        scratch_shapes=([pltpu.VMEM((rows, HALF, LANES), jnp.float32)] if halos else [])
        + [
            block,
            block,
            pltpu.SemaphoreType.DMA((2, 2 * len(groups))),
            pltpu.SemaphoreType.DMA((13,)),
        ],
        cost_estimate=pl.CostEstimate(
            flops=0, bytes_accessed=1024, transcendentals=0
        ),
        compiler_params=params(10),
        name="turn",
    )(where, in_hbm(recorded), received, *halos)


GROUPS = tuple((PAD + GROUP * g, GROUP) for g in range(4))
SPANS = ((REACH, REACH),) + GROUPS + ((EXT_R - PAD, REACH),)
FIRST_SPANS = ((0, REACH),) + SPANS + ((EXT_R - REACH, REACH),)
NEXT_SPANS = ((0, PAD),) + GROUPS + ((EXT_R - PAD, PAD),)
HOMES = (
    ((2, 8), (0, 0), (7, 8)),
    ((1, 0), (3, 0), (6, 0)),
    ((1, 16), (4, 0), (6, 16)),
    ((2, 0), (5, 0), (7, 0)),
    ((1, 8), (3, 8), (6, 8)),
    ((2, 14), (8, 0), (7, 14)),
)
OUTER = (11, 17)


def iterate_kernel(first, row0, n_out, present, *refs):
    n_in = n_out + 2 * PAD
    width = EXT_C if first else EXT_C - 2 * SIDE
    shift = 0 if first else SIDE
    inner = width - 2 * SIDE
    fold = (EXT_C - 2 * SIDE) // 2
    pieces = iter(refs)
    taken = [next(pieces) if there else None for there in present]
    recorded, field, refs = taken[:9], taken[9:], tuple(pieces)
    taps_ref, blur_hbm, adj_hbm = refs[:3]
    refs = refs[3:]
    if first:
        out_ref, top_ref, low_ref = refs[:3]
        refs = refs[3:]
    else:
        out_ref, refs = refs[0], refs[1:]
    r_buf, e_buf, xz_buf, xr_buf, pack, tmp, blur_ref, adj_ref, r_sem, e_sem, m_sem = refs
    north, south = recorded[0], recorded[8]
    lower = lax.broadcasted_iota(jnp.int32, (width, LANES), 1) < Z

    def window(span, lo, hi):
        at, count = span
        a, b = max(at, lo), min(at + count, hi)
        return (a, b) if a < b else None

    def r_copies(k):
        got = window(SPANS[k], row0 + REACH, row0 + n_in - REACH)
        if got is None:
            return []
        a, b = got
        rows = pl.ds(a - row0, b - a)
        pairs = []
        ranges = ((0, MARGIN), (MARGIN, MARGIN + HALF), (MARGIN + HALF, EXT_C))
        for (home, base), (lo, hi) in zip(HOMES[k], ranges):
            src = recorded[home]
            c, d = max(lo, shift), min(hi, shift + width)
            pairs.append(
                (
                    src.at[pl.ds(base + a - SPANS[k][0], b - a), pl.ds(c - lo, d - c), :],
                    r_buf.at[rows, pl.ds(c - shift, d - c), :],
                )
            )
        return [
            pltpu.make_async_copy(src, dst, r_sem.at[k, n]) for n, (src, dst) in enumerate(pairs)
        ]

    def e_copies(k):
        if first:
            if 0 < k < 7:
                return []
            n = 0 if k == 0 else 1
            halo, rows = (north if n == 0 else south), pl.ds(OUTER[n], REACH)
            pairs = (
                (recorded[2].at[rows, :, :], pl.ds(0, MARGIN)),
                (halo.at[:, pl.ds(HALF, CHUNK), :], pl.ds(MARGIN, CHUNK)),
                (recorded[7].at[rows, :, :], pl.ds(MARGIN + CHUNK, MARGIN)),
            )
            return [
                pltpu.make_async_copy(src, pack.at[n, :, cols, :], e_sem.at[k, i])
                for i, (src, cols) in enumerate(pairs)
            ]
        got = window(NEXT_SPANS[k], row0, row0 + n_in)
        if got is None:
            return []
        a, b = got
        if k in (0, 5):
            src, dst = (field[0] if k == 0 else field[2]), pack.at[0 if k == 0 else 1]
        else:
            at = GROUP * (k - 1) + a - NEXT_SPANS[k][0]
            src, dst = field[1].at[pl.ds(at, b - a), :, :], e_buf.at[pl.ds(a - row0, b - a), :, :]
        return [pltpu.make_async_copy(src, dst, e_sem.at[k, 0])]

    recorded_in = [r_copies(k) for k in range(6)]
    e_spans = FIRST_SPANS if first else NEXT_SPANS
    field_in = [e_copies(k) for k in range(len(e_spans))]
    matrices_in = [
        pltpu.make_async_copy(blur_hbm, blur_ref, m_sem.at[0]),
        pltpu.make_async_copy(adj_hbm, adj_ref, m_sem.at[1]),
    ]
    for group in [matrices_in] + field_in + recorded_in:
        for c in group:
            c.start()

    def over_rows(start, count, steps, unroll):
        def rows_from(at, many):
            for step in steps:
                for slot in range(many):
                    step(slot, at + slot)

        def body(i, carry):
            rows_from(start + unroll * i, unroll)
            return carry

        lax.fori_loop(0, count // unroll, body, 0)
        if count % unroll:
            rows_from(start + count - count % unroll, count % unroll)

    kx = [taps_ref[t : t + 1, :] for t in range(7)]
    ky = [taps_ref[8 + t : 9 + t, :] for t in range(7)]
    col_blocks = blocks_of(width)

    def cols_pass(slot, taps, dst_ref, row):
        for at, size in col_blocks:
            acc = taps[0] * tmp[slot, pl.ds(5 + at, size), :]
            for t in range(1, 7):
                acc = acc + taps[t] * tmp[slot, pl.ds(5 + t + at, size), :]
            dst_ref[row, pl.ds(at, size), :] = acc

    def blur_row(slot, row, started):
        if not started:
            r = r_buf[row]
            e = (r + pltpu.roll(r, Z, 1)) * 0.5
            e_buf[row] = e
        else:
            e = e_buf[row]
        high = e.astype(jnp.bfloat16).astype(jnp.float32)
        split = jnp.where(lower, high, e - high).astype(jnp.bfloat16)
        both = jnp.dot(split, blur_ref[...], preferred_element_type=jnp.float32)
        tmp[slot, pl.ds(8, width), :] = both[:, :LANES] + both[:, LANES:]

    for slot in range(UNROLL):
        tmp[slot, pl.ds(0, 8), :] = jnp.zeros((8, LANES), jnp.float32)
        tmp[slot, pl.ds(8 + width, 8), :] = jnp.zeros((8, LANES), jnp.float32)

    def both_halves(packed, turned, size, low_first):
        keep = lower[:size] if low_first else jnp.logical_not(lower[:size])
        return jnp.where(keep, packed, turned)

    for c in matrices_in:
        c.wait()
    if first:
        plan = [(0, PAD, field_in[0] + recorded_in[0], 0, range(REACH))]
        plan += [GROUPS[g] + (recorded_in[1 + g], None, ()) for g in range(4)]
        plan += [(EXT_R - PAD, PAD, recorded_in[5] + field_in[7], 1, range(REACH, PAD))]
    else:
        plan = []
        for k, span in enumerate(NEXT_SPANS):
            got = window(span, row0, row0 + n_in)
            if got is not None:
                edge = {0: 0, 5: 1}.get(k)
                packed_slots = () if edge is None else range(PAD)
                plan.append((got[0] - row0, got[1] - got[0], field_in[k], edge, packed_slots))

    for base, count, waits, edge, packed_slots in plan:
        for c in waits:
            c.wait()

        def halo_row(slot, row, edge=edge, packed_slots=packed_slots):
            halo = slot in packed_slots
            if halo:
                packed = pack[edge, slot - packed_slots[0]]
                turned = pltpu.roll(packed, Z, 1)
                if first:
                    parts = (
                        (0, 0, MARGIN, False),
                        (MARGIN, MARGIN, CHUNK, True),
                        (MARGIN + CHUNK, MARGIN, CHUNK, False),
                        (MARGIN + HALF, MARGIN + CHUNK, MARGIN, True),
                    )
                else:
                    parts = ((0, 0, fold, True), (fold, 0, fold, False))
                for to, at, size, low_first in parts:
                    e_buf[row, pl.ds(to, size), :] = both_halves(
                        packed[at : at + size], turned[at : at + size], size, low_first
                    )
            blur_row(slot, row, halo or not first)

        over_rows(
            base,
            count,
            (halo_row, lambda slot, row: cols_pass(slot, kx, xz_buf, row)),
            UNROLL,
        )

    if not first:
        for group in recorded_in:
            for c in group:
                c.wait()

    def rows_pass(src_ref, taps, row, at, size):
        acc = taps[0] * src_ref[row - 3, pl.ds(at, size), :]
        for t in range(1, 7):
            acc = acc + taps[t] * src_ref[row - 3 + t, pl.ds(at, size), :]
        return acc

    def ratio_row(slot, row):
        for at, size in col_blocks:
            blurred = rows_pass(xz_buf, ky, row, at, size)
            ratio = r_buf[row, pl.ds(at, size), :] / jnp.maximum(blurred, TINY)
            tmp[slot, pl.ds(8 + at, size), :] = ratio

    over_rows(3, n_in - 6, (ratio_row, lambda slot, row: cols_pass(slot, kx[::-1], xr_buf, row)), UNROLL)

    def update_row(slot, y):
        row = PAD + y
        for at, size in blocks_of(inner, UPDATE):
            spread = rows_pass(xr_buf, ky[::-1], row, SIDE + at, size)
            high = spread.astype(jnp.bfloat16)
            low = (spread - high.astype(jnp.float32)).astype(jnp.bfloat16)
            both = jnp.dot(
                jnp.concatenate([high, low], axis=1),
                adj_ref[...],
                preferred_element_type=jnp.float32,
            )
            factor = both + pltpu.roll(both, Z, 1)
            new = e_buf[row, pl.ds(SIDE + at, size), :] * factor
            if first:
                out_ref[y, pl.ds(at, size), :] = new
            else:
                flat = out_ref.at[at // CHUNK].reshape(Z * GROUP, CHUNK)
                flat[pl.ds(y, Z, stride=GROUP), :] = new.T[:Z]

    over_rows(0, n_out, (update_row,), UNROLL)
    if first:
        for y in range(PAD):
            for ref, row in ((top_ref, y), (low_ref, ROWS - PAD + y)):
                ref[y] = jnp.where(
                    lower[:fold], out_ref[row, pl.ds(0, fold), :], out_ref[row, pl.ds(fold, fold), :]
                )


def iterate(recorded, field, taps, blur, adj, *, first, row0, n_out):
    n_in = n_out + 2 * PAD
    width = EXT_C if first else EXT_C - 2 * SIDE
    fold = (EXT_C - 2 * SIDE) // 2
    pieces = list(recorded) + (list(field) if field is not None else [])
    if not first and row0 >= PAD:
        pieces[0] = pieces[9] = None
    if not first and row0 + n_in <= EXT_R - PAD:
        pieces[8] = pieces[11] = None
    for k in (0, 5, 8):
        if pieces[k] is not None:
            pieces[k] = in_hbm(pieces[k])
    present = tuple(piece is not None for piece in pieces)
    pieces = [piece for piece in pieces if piece is not None]
    if first:
        edge = jax.ShapeDtypeStruct((PAD, fold, LANES), jnp.float32)
        out = (jax.ShapeDtypeStruct((ROWS, EXT_C - 2 * SIDE, LANES), jnp.float32), edge, edge)
        out_specs = (pl.BlockSpec(memory_space=pltpu.VMEM),) * 3
    else:
        out = jax.ShapeDtypeStruct((2, Z, GROUP, CHUNK), jnp.float32)
        out_specs = pl.BlockSpec(memory_space=pltpu.VMEM)
    row = pltpu.VMEM((n_in, width, LANES), jnp.float32)
    vregs = n_in * width // 8
    return pl.pallas_call(
        functools.partial(iterate_kernel, first, row0, n_out, present),
        out_shape=out,
        in_specs=[pl.BlockSpec(memory_space=pl.ANY)] * len(pieces)
        + [pl.BlockSpec(memory_space=pltpu.VMEM)]
        + [pl.BlockSpec(memory_space=pl.ANY)] * 2,
        out_specs=out_specs,
        scratch_shapes=[
            row,
            row,
            row,
            row,
            pltpu.VMEM(
                (2, REACH, CHUNK + 2 * MARGIN, LANES) if first else (2, PAD, fold, LANES),
                jnp.float32,
            ),
            pltpu.VMEM((UNROLL, width + 16, LANES), jnp.float32),
            pltpu.VMEM((2 * Z, 2 * LANES), jnp.bfloat16),
            pltpu.VMEM((2 * LANES, LANES), jnp.bfloat16),
            pltpu.SemaphoreType.DMA((6, 3)),
            pltpu.SemaphoreType.DMA((8, 3)),
            pltpu.SemaphoreType.DMA((2,)),
        ],
        cost_estimate=pl.CostEstimate(
            flops=0, bytes_accessed=vregs * 4096 if first else 4096, transcendentals=0
        ),
        compiler_params=params(30 if first else 13),
        name="iterate",
    )(*pieces, taps, in_hbm(blur), in_hbm(adj))


def place_kernel(where_ref, *refs):
    refs[-1][...] = refs[0][0]


def place(where, block, whole, group):
    args = [where, block]
    in_specs = [pl.BlockSpec((1, Z, GROUP, CHUNK), lambda j, w: (j, 0, 0, 0))]
    aliases = {}
    if whole is not None:
        args.append(whole)
        in_specs.append(pl.BlockSpec(memory_space=pl.ANY))
        aliases = {2: 0}
    return pl.pallas_call(
        place_kernel,
        out_shape=jax.ShapeDtypeStruct((Z, ROWS, 2 * HALF), jnp.float32),
        grid_spec=pltpu.PrefetchScalarGridSpec(
            num_scalar_prefetch=1,
            grid=(2,),
            in_specs=in_specs,
            out_specs=pl.BlockSpec((Z, GROUP, CHUNK), lambda j, w: (0, group, 2 * w[0] + j)),
        ),
        input_output_aliases=aliases,
        cost_estimate=pl.CostEstimate(flops=0, bytes_accessed=1 << 20, transcendentals=0),
        compiler_params=params(4),
        name="place",
    )(*args)


def neighbours(views, tiles):
    right = []
    for v in range(views):
        for t in range(tiles):
            if (t + v) % 2 == 0:
                right.append((v * tiles + t, (1 - v) * tiles + t))
            elif t + 1 < tiles:
                right.append((v * tiles + t, v * tiles + t + 1))
    return right


def per_device(views_data, psf_axial, psf_rows, psf_cols):
    views, tiles, bands = lax.axis_size("view"), lax.axis_size("tx"), lax.axis_size("ty")
    swap = [(0, 1), (1, 0)]
    right = neighbours(views, tiles)
    left = [(b, a) for a, b in right]
    down = [(i, i + 1) for i in range(bands - 1)]
    up = [(b, a) for a, b in down]
    half = lax.rem(lax.axis_index("tx") + lax.axis_index("view"), 2)

    def other_rows(views_data, *starts):
        at = (1 - half) * HALF
        return jnp.concatenate(
            [
                lax.dynamic_slice(views_data, (0, 0, row, at), (1, Z, rows, HALF))[0]
                for row, rows in starts
            ],
            axis=1,
        )

    border = other_rows(views_data, (0, GROUP), (ROWS - GROUP, GROUP))
    later, axial, rows, cols, border = lax.optimization_barrier(
        (views_data, psf_axial, psf_rows, psf_cols, border)
    )
    border_in = lax.ppermute(border, "view", swap)
    raw = jnp.concatenate([axial[0], rows[0], cols[0]])
    raw_other = lax.ppermute(raw, "view", swap)
    upper_in = lax.ppermute(other_rows(later, (GROUP, GROUP)), "view", swap)
    last_rows, raw_other = lax.optimization_barrier(
        (other_rows(later, (2 * GROUP, GROUP)), raw_other)
    )
    lower_in = lax.ppermute(last_rows, "view", swap)

    view = lax.axis_index("view")
    where = jnp.stack([half, view]).astype(jnp.int32)
    there = (1 - half).astype(jnp.int32)[None]

    def sides(west, east):
        return lax.ppermute(west, ("view", "tx"), right), lax.ppermute(east, ("view", "tx"), left)

    border, border_east, border_west, to_up, to_down = turn(where, views_data, border_in, (0, 3))
    raw, raw_other, to_up, to_down = lax.optimization_barrier((raw, raw_other, to_up, to_down))
    north = lax.ppermute(to_down, "ty", down)
    south = lax.ppermute(to_up, "ty", up)

    def norm(taps):
        parts = (taps[:21], taps[21:28], taps[28:35])
        return jnp.concatenate([part / jnp.sum(part) for part in parts])

    own, other = norm(raw), norm(raw_other)
    lanes = jnp.concatenate(
        [
            jnp.broadcast_to(jnp.where(view == 0, own, other)[:, None], (own.shape[0], Z)),
            jnp.broadcast_to(jnp.where(view == 0, other, own)[:, None], (own.shape[0], Z)),
        ],
        axis=1,
    )
    blur, adj = matrices(lanes[:21])
    taps = jnp.zeros((16, LANES), jnp.float32)
    taps = taps.at[0:7].set(lanes[28:35]).at[8:15].set(lanes[21:28])

    upper_in, blur, adj = lax.optimization_barrier((upper_in, blur, adj))
    upper, upper_east, upper_west = turn(where, views_data, upper_in, (1,))
    west, east = sides(
        jnp.concatenate([border_east, upper_east]), jnp.concatenate([border_west, upper_west])
    )
    lower, lower_east, lower_west, north, south = turn(
        where, views_data, lower_in, (2,), (north, south)
    )
    last_west, last_east = sides(lower_east, lower_west)
    recorded = (north, west, last_west, border, upper, lower, east, last_east, south)

    estimate, top, low = iterate(
        recorded, None, taps, blur, adj, first=True, row0=0, n_out=ROWS
    )
    def piece(group, field):
        return iterate(
            recorded, field, taps, blur, adj, first=False, row0=GROUP * group, n_out=GROUP
        )

    field = (lax.ppermute(low, "ty", down), estimate, lax.ppermute(top, "ty", up))
    theirs = []
    whole = None
    for group in (1, 2, 0, 3):
        block = piece(group, field)
        theirs.append((group, lax.ppermute(block, "view", swap)))
        whole = place(where[:1], block, whole, group)
    for group, block in theirs:
        whole = place(there, block, whole, group)
    return whole


def solution(mesh):
    placed = (P("view", None, "ty", "tx"), P("view", None), P("view", None), P("view", None))
    return jax.shard_map(
        per_device, mesh=mesh, in_specs=placed, out_specs=P(None, "ty", "tx"), check_vma=False
    )
```

```python
import functools

import jax
import jax.numpy as jnp
from jax import lax
from jax.experimental import pallas as pl
from jax.experimental.pallas import tpu as pltpu
from jax.sharding import PartitionSpec as P

ITERS = 2
Z = 64
LANES = 128
ROWS = 32
HALF = 256
CHUNK = 128
PAD = 6
REACH = 3
SIDE = 8
MARGIN = 16
GROUP = 8
EXT_R = ROWS + 2 * PAD
EXT_C = HALF + 2 * MARGIN
MIB = 1024 * 1024
UNROLL = 16
UPDATE = 128
TINY = 1e-30


def params(mib):
    return pltpu.CompilerParams(vmem_limit_bytes=mib * MIB)


def in_hbm(array):
    return pltpu.with_memory_space_constraint(array, pltpu.HBM)


def blocks_of(total, largest=96):
    out, at = [], 0
    while at < total:
        size = min(largest, total - at)
        out.append((at, size))
        at += size
    return out


def matrices_kernel(kz_ref, blur_ref, adj_ref):
    taps = kz_ref.shape[0]
    lane = lax.broadcasted_iota(jnp.int32, (Z, LANES), 1)
    row = lax.broadcasted_iota(jnp.int32, (Z, LANES), 0)
    offset = row - lax.rem(lane, Z) + taps // 2
    mat = jnp.zeros((Z, LANES), jnp.float32)
    for t in range(taps):
        mat = mat + jnp.where(offset == t, kz_ref[t : t + 1, :], 0.0)
    high = mat.astype(jnp.bfloat16)
    low = (mat - high.astype(jnp.float32)).astype(jnp.bfloat16)
    blur_ref[0:Z, 0:LANES] = high
    blur_ref[0:Z, LANES:] = low
    blur_ref[Z:, 0:LANES] = high
    blur_ref[Z:, LANES:] = jnp.zeros((Z, LANES), jnp.bfloat16)
    adj = jnp.concatenate([mat, mat], axis=0).T * 0.5
    ahigh = adj.astype(jnp.bfloat16).astype(jnp.float32)
    alow = adj - ahigh
    first = lax.broadcasted_iota(jnp.int32, (LANES, LANES), 1) < Z
    adj_ref[0:LANES, :] = jnp.where(first, ahigh, alow).astype(jnp.bfloat16)
    adj_ref[LANES:, :] = jnp.where(first, ahigh, 0.0).astype(jnp.bfloat16)


def matrices(kz):
    return pl.pallas_call(
        matrices_kernel,
        out_shape=(
            jax.ShapeDtypeStruct((2 * Z, 2 * LANES), jnp.bfloat16),
            jax.ShapeDtypeStruct((2 * LANES, LANES), jnp.bfloat16),
        ),
        compiler_params=params(4),
        name="matrices",
    )(kz)


def turn_kernel(groups, corners, where_ref, own_ref, other_ref, *refs):
    if corners:
        halos, refs = refs[:2], refs[2:]
    out_ref, west_ref, east_ref = refs[:3]
    refs = refs[3:]
    own, other, sems, corner_sems = refs[-4:]
    if corners:
        kept, refs = refs[:2], refs[2:]
        out_hbm, out_ref = out_ref, refs[0]
    corner_copies = []
    if corners:
        columns = (
            (west_ref, HALF - MARGIN, HALF + CHUNK - MARGIN),
            (east_ref, 0, HALF),
        )
        for side, (strip, near, far) in enumerate(columns):
            for n, halo in enumerate(halos):
                for m, at in enumerate((near, far)):
                    row = GROUP + REACH * (2 * n + m)
                    corner_copies.append(
                        pltpu.make_async_copy(
                            halo.at[:, pl.ds(at, MARGIN), :],
                            strip.at[pl.ds(row, REACH), :, :],
                            corner_sems.at[4 * side + 2 * n + m],
                        )
                    )
        for n, halo in enumerate(halos):
            corner_copies.append(pltpu.make_async_copy(halo, kept[n], corner_sems.at[9 + n]))
    half, first = where_ref[0], where_ref[1] == 0
    blocks = [(i, j) for i in range(len(groups)) for j in range(2)]
    copies = []
    for n, (i, j) in enumerate(blocks):
        at = pl.multiple_of(half * HALF + j * CHUNK, CHUNK)
        mine = own_ref.at[0, :, pl.ds(groups[i] * GROUP, GROUP), pl.ds(at, CHUNK)]
        theirs = other_ref.at[:, pl.ds(i * GROUP, GROUP), pl.ds(j * CHUNK, CHUNK)]
        copies.append(
            (
                pltpu.make_async_copy(mine, own.at[n], sems.at[0, n]),
                pltpu.make_async_copy(theirs, other.at[n], sems.at[1, n]),
            )
        )
    for pair in copies:
        for c in pair:
            c.start()
    for c in corner_copies:
        c.start()
    for n, (i, j) in enumerate(blocks):
        for c in copies[n]:
            c.wait()
        flat = own.at[n].reshape(Z * GROUP, CHUNK)
        flat_other = other.at[n].reshape(Z * GROUP, CHUNK)
        for y in range(GROUP):
            mine = flat[pl.ds(y, Z, stride=GROUP), :]
            theirs = flat_other[pl.ds(y, Z, stride=GROUP), :]
            pair = jnp.concatenate(
                [jnp.where(first, mine, theirs), jnp.where(first, theirs, mine)], axis=0
            ).T
            row = i * GROUP + y
            out_ref[row, pl.ds(j * CHUNK, CHUNK), :] = pair
            if j == 0:
                east_ref[row] = pair[:MARGIN]
            else:
                west_ref[row] = pair[CHUNK - MARGIN :]
        if corners:
            turned = pl.ds(j * CHUNK, CHUNK)
            corner_copies.append(
                pltpu.make_async_copy(
                    out_ref.at[:, turned, :], out_hbm.at[:, turned, :], corner_sems.at[11 + j]
                )
            )
            corner_copies[-1].start()
    for c in corner_copies:
        c.wait()
    if len(groups) == 1:
        return
    up_ref, down_ref = refs[:2]
    lower = lax.broadcasted_iota(jnp.int32, (CHUNK, LANES), 1) < Z
    low = 2 * GROUP - PAD
    for ref, near, far in ((up_ref, 0, REACH), (down_ref, low + REACH, low)):
        for y in range(REACH):
            ref[y, pl.ds(0, HALF), :] = out_ref[near + y]
            ends = []
            for j in range(2):
                r = out_ref[far + y, pl.ds(j * CHUNK, CHUNK), :]
                ends.append((r + pltpu.roll(r, Z, 1)) * 0.5)
            ref[y, pl.ds(HALF, CHUNK), :] = jnp.where(lower, ends[0], ends[1])


def turn(where, recorded, received, groups, halos=()):
    rows = len(groups) * GROUP
    block = pltpu.VMEM((2 * len(groups), Z, GROUP, CHUNK), jnp.float32)
    strip_rows = rows + (4 * REACH if halos else 0)
    strip = jax.ShapeDtypeStruct((strip_rows, MARGIN, LANES), jnp.float32)
    main = pltpu.HBM if halos else jax.ShapeDtypeStruct
    out = [main((rows, HALF, LANES), jnp.float32), strip, strip]
    if halos:
        out += [pltpu.HBM(halo.shape, jnp.float32) for halo in halos]
    if len(groups) > 1:
        out += [jax.ShapeDtypeStruct((REACH, HALF + CHUNK, LANES), jnp.float32)] * 2
    return pl.pallas_call(
        functools.partial(turn_kernel, groups, bool(halos)),
        out_shape=tuple(out),
        in_specs=[
            pl.BlockSpec(memory_space=pltpu.SMEM),
            pl.BlockSpec(memory_space=pltpu.HBM),
            pl.BlockSpec(memory_space=pl.ANY),
        ]
        + [pl.BlockSpec(memory_space=pl.ANY)] * len(halos),
        out_specs=(pl.BlockSpec(memory_space=pltpu.HBM if halos else pltpu.VMEM),)
        + (pl.BlockSpec(memory_space=pltpu.VMEM),) * 2
        + (pl.BlockSpec(memory_space=pltpu.HBM if halos else pltpu.VMEM),) * (len(out) - 3),
        scratch_shapes=([pltpu.VMEM((rows, HALF, LANES), jnp.float32)] if halos else [])
        + [
            block,
            block,
            pltpu.SemaphoreType.DMA((2, 2 * len(groups))),
            pltpu.SemaphoreType.DMA((13,)),
        ],
        cost_estimate=pl.CostEstimate(
            flops=0, bytes_accessed=1024, transcendentals=0
        ),
        compiler_params=params(10),
        name="turn",
    )(where, in_hbm(recorded), received, *halos)


GROUPS = tuple((PAD + GROUP * g, GROUP) for g in range(4))
SPANS = ((REACH, REACH),) + GROUPS + ((EXT_R - PAD, REACH),)
FIRST_SPANS = ((0, REACH),) + SPANS + ((EXT_R - REACH, REACH),)
NEXT_SPANS = ((0, PAD),) + GROUPS + ((EXT_R - PAD, PAD),)
HOMES = (
    ((2, 8), (0, 0), (7, 8)),
    ((1, 0), (3, 0), (6, 0)),
    ((1, 16), (4, 0), (6, 16)),
    ((2, 0), (5, 0), (7, 0)),
    ((1, 8), (3, 8), (6, 8)),
    ((2, 14), (8, 0), (7, 14)),
)
OUTER = (11, 17)


def iterate_kernel(first, row0, n_out, present, *refs):
    n_in = n_out + 2 * PAD
    width = EXT_C if first else EXT_C - 2 * SIDE
    shift = 0 if first else SIDE
    inner = width - 2 * SIDE
    fold = (EXT_C - 2 * SIDE) // 2
    pieces = iter(refs)
    taken = [next(pieces) if there else None for there in present]
    recorded, field, refs = taken[:9], taken[9:], tuple(pieces)
    taps_ref, blur_hbm, adj_hbm = refs[:3]
    refs = refs[3:]
    if first:
        out_ref, top_ref, low_ref = refs[:3]
        refs = refs[3:]
    else:
        out_ref, refs = refs[0], refs[1:]
    r_buf, e_buf, xz_buf, xr_buf, pack, tmp, blur_ref, adj_ref, r_sem, e_sem, m_sem = refs
    north, south = recorded[0], recorded[8]
    lower = lax.broadcasted_iota(jnp.int32, (width, LANES), 1) < Z

    def window(span, lo, hi):
        at, count = span
        a, b = max(at, lo), min(at + count, hi)
        return (a, b) if a < b else None

    def r_copies(k):
        got = window(SPANS[k], row0 + REACH, row0 + n_in - REACH)
        if got is None:
            return []
        a, b = got
        rows = pl.ds(a - row0, b - a)
        pairs = []
        ranges = ((0, MARGIN), (MARGIN, MARGIN + HALF), (MARGIN + HALF, EXT_C))
        for (home, base), (lo, hi) in zip(HOMES[k], ranges):
            src = recorded[home]
            c, d = max(lo, shift), min(hi, shift + width)
            pairs.append(
                (
                    src.at[pl.ds(base + a - SPANS[k][0], b - a), pl.ds(c - lo, d - c), :],
                    r_buf.at[rows, pl.ds(c - shift, d - c), :],
                )
            )
        return [
            pltpu.make_async_copy(src, dst, r_sem.at[k, n]) for n, (src, dst) in enumerate(pairs)
        ]

    def e_copies(k):
        if first:
            if 0 < k < 7:
                return []
            n = 0 if k == 0 else 1
            halo, rows = (north if n == 0 else south), pl.ds(OUTER[n], REACH)
            pairs = (
                (recorded[2].at[rows, :, :], pl.ds(0, MARGIN)),
                (halo.at[:, pl.ds(HALF, CHUNK), :], pl.ds(MARGIN, CHUNK)),
                (recorded[7].at[rows, :, :], pl.ds(MARGIN + CHUNK, MARGIN)),
            )
            return [
                pltpu.make_async_copy(src, pack.at[n, :, cols, :], e_sem.at[k, i])
                for i, (src, cols) in enumerate(pairs)
            ]
        got = window(NEXT_SPANS[k], row0, row0 + n_in)
        if got is None:
            return []
        a, b = got
        if k in (0, 5):
            src, dst = (field[0] if k == 0 else field[2]), pack.at[0 if k == 0 else 1]
        else:
            at = GROUP * (k - 1) + a - NEXT_SPANS[k][0]
            src, dst = field[1].at[pl.ds(at, b - a), :, :], e_buf.at[pl.ds(a - row0, b - a), :, :]
        return [pltpu.make_async_copy(src, dst, e_sem.at[k, 0])]

    recorded_in = [r_copies(k) for k in range(6)]
    e_spans = FIRST_SPANS if first else NEXT_SPANS
    field_in = [e_copies(k) for k in range(len(e_spans))]
    matrices_in = [
        pltpu.make_async_copy(blur_hbm, blur_ref, m_sem.at[0]),
        pltpu.make_async_copy(adj_hbm, adj_ref, m_sem.at[1]),
    ]
    for group in [matrices_in] + field_in + recorded_in:
        for c in group:
            c.start()

    def over_rows(start, count, steps, unroll):
        def rows_from(at, many):
            for step in steps:
                for slot in range(many):
                    step(slot, at + slot)

        def body(i, carry):
            rows_from(start + unroll * i, unroll)
            return carry

        lax.fori_loop(0, count // unroll, body, 0)
        if count % unroll:
            rows_from(start + count - count % unroll, count % unroll)

    kx = [taps_ref[t : t + 1, :] for t in range(7)]
    ky = [taps_ref[8 + t : 9 + t, :] for t in range(7)]
    col_blocks = blocks_of(width)

    def cols_pass(slot, taps, dst_ref, row):
        for at, size in col_blocks:
            acc = taps[0] * tmp[slot, pl.ds(5 + at, size), :]
            for t in range(1, 7):
                acc = acc + taps[t] * tmp[slot, pl.ds(5 + t + at, size), :]
            dst_ref[row, pl.ds(at, size), :] = acc

    def blur_row(slot, row, started):
        if not started:
            r = r_buf[row]
            e = (r + pltpu.roll(r, Z, 1)) * 0.5
            e_buf[row] = e
        else:
            e = e_buf[row]
        high = e.astype(jnp.bfloat16).astype(jnp.float32)
        split = jnp.where(lower, high, e - high).astype(jnp.bfloat16)
        both = jnp.dot(split, blur_ref[...], preferred_element_type=jnp.float32)
        tmp[slot, pl.ds(8, width), :] = both[:, :LANES] + both[:, LANES:]

    for slot in range(UNROLL):
        tmp[slot, pl.ds(0, 8), :] = jnp.zeros((8, LANES), jnp.float32)
        tmp[slot, pl.ds(8 + width, 8), :] = jnp.zeros((8, LANES), jnp.float32)

    def both_halves(packed, turned, size, low_first):
        keep = lower[:size] if low_first else jnp.logical_not(lower[:size])
        return jnp.where(keep, packed, turned)

    for c in matrices_in:
        c.wait()
    if first:
        plan = [(0, PAD, field_in[0] + recorded_in[0], 0, range(REACH))]
        plan += [GROUPS[g] + (recorded_in[1 + g], None, ()) for g in range(4)]
        plan += [(EXT_R - PAD, PAD, recorded_in[5] + field_in[7], 1, range(REACH, PAD))]
    else:
        plan = []
        for k, span in enumerate(NEXT_SPANS):
            got = window(span, row0, row0 + n_in)
            if got is not None:
                edge = {0: 0, 5: 1}.get(k)
                packed_slots = () if edge is None else range(PAD)
                plan.append((got[0] - row0, got[1] - got[0], field_in[k], edge, packed_slots))

    for base, count, waits, edge, packed_slots in plan:
        for c in waits:
            c.wait()

        def halo_row(slot, row, edge=edge, packed_slots=packed_slots):
            halo = slot in packed_slots
            if halo:
                packed = pack[edge, slot - packed_slots[0]]
                turned = pltpu.roll(packed, Z, 1)
                if first:
                    parts = (
                        (0, 0, MARGIN, False),
                        (MARGIN, MARGIN, CHUNK, True),
                        (MARGIN + CHUNK, MARGIN, CHUNK, False),
                        (MARGIN + HALF, MARGIN + CHUNK, MARGIN, True),
                    )
                else:
                    parts = ((0, 0, fold, True), (fold, 0, fold, False))
                for to, at, size, low_first in parts:
                    e_buf[row, pl.ds(to, size), :] = both_halves(
                        packed[at : at + size], turned[at : at + size], size, low_first
                    )
            blur_row(slot, row, halo or not first)

        over_rows(
            base,
            count,
            (halo_row, lambda slot, row: cols_pass(slot, kx, xz_buf, row)),
            UNROLL,
        )

    if not first:
        for group in recorded_in:
            for c in group:
                c.wait()

    def rows_pass(src_ref, taps, row, at, size):
        acc = taps[0] * src_ref[row - 3, pl.ds(at, size), :]
        for t in range(1, 7):
            acc = acc + taps[t] * src_ref[row - 3 + t, pl.ds(at, size), :]
        return acc

    def ratio_row(slot, row):
        for at, size in col_blocks:
            blurred = rows_pass(xz_buf, ky, row, at, size)
            ratio = r_buf[row, pl.ds(at, size), :] / jnp.maximum(blurred, TINY)
            tmp[slot, pl.ds(8 + at, size), :] = ratio

    over_rows(3, n_in - 6, (ratio_row, lambda slot, row: cols_pass(slot, kx[::-1], xr_buf, row)), UNROLL)

    def update_row(slot, y):
        row = PAD + y
        for at, size in blocks_of(inner, UPDATE):
            spread = rows_pass(xr_buf, ky[::-1], row, SIDE + at, size)
            high = spread.astype(jnp.bfloat16)
            low = (spread - high.astype(jnp.float32)).astype(jnp.bfloat16)
            both = jnp.dot(
                jnp.concatenate([high, low], axis=1),
                adj_ref[...],
                preferred_element_type=jnp.float32,
            )
            factor = both + pltpu.roll(both, Z, 1)
            new = e_buf[row, pl.ds(SIDE + at, size), :] * factor
            if first:
                out_ref[y, pl.ds(at, size), :] = new
            else:
                flat = out_ref.at[at // CHUNK].reshape(Z * GROUP, CHUNK)
                flat[pl.ds(y, Z, stride=GROUP), :] = new.T[:Z]

    over_rows(0, n_out, (update_row,), UNROLL)
    if first:
        for y in range(PAD):
            for ref, row in ((top_ref, y), (low_ref, ROWS - PAD + y)):
                ref[y] = jnp.where(
                    lower[:fold], out_ref[row, pl.ds(0, fold), :], out_ref[row, pl.ds(fold, fold), :]
                )


def iterate(recorded, field, taps, blur, adj, *, first, row0, n_out):
    n_in = n_out + 2 * PAD
    width = EXT_C if first else EXT_C - 2 * SIDE
    fold = (EXT_C - 2 * SIDE) // 2
    pieces = list(recorded) + (list(field) if field is not None else [])
    if not first and row0 >= PAD:
        pieces[0] = pieces[9] = None
    if not first and row0 + n_in <= EXT_R - PAD:
        pieces[8] = pieces[11] = None
    for k in (0, 5, 8):
        if pieces[k] is not None:
            pieces[k] = in_hbm(pieces[k])
    present = tuple(piece is not None for piece in pieces)
    pieces = [piece for piece in pieces if piece is not None]
    if first:
        edge = jax.ShapeDtypeStruct((PAD, fold, LANES), jnp.float32)
        out = (jax.ShapeDtypeStruct((ROWS, EXT_C - 2 * SIDE, LANES), jnp.float32), edge, edge)
        out_specs = (pl.BlockSpec(memory_space=pltpu.VMEM),) * 3
    else:
        out = jax.ShapeDtypeStruct((2, Z, GROUP, CHUNK), jnp.float32)
        out_specs = pl.BlockSpec(memory_space=pltpu.VMEM)
    row = pltpu.VMEM((n_in, width, LANES), jnp.float32)
    vregs = n_in * width // 8
    return pl.pallas_call(
        functools.partial(iterate_kernel, first, row0, n_out, present),
        out_shape=out,
        in_specs=[pl.BlockSpec(memory_space=pl.ANY)] * len(pieces)
        + [pl.BlockSpec(memory_space=pltpu.VMEM)]
        + [pl.BlockSpec(memory_space=pl.ANY)] * 2,
        out_specs=out_specs,
        scratch_shapes=[
            row,
            row,
            row,
            row,
            pltpu.VMEM(
                (2, REACH, CHUNK + 2 * MARGIN, LANES) if first else (2, PAD, fold, LANES),
                jnp.float32,
            ),
            pltpu.VMEM((UNROLL, width + 16, LANES), jnp.float32),
            pltpu.VMEM((2 * Z, 2 * LANES), jnp.bfloat16),
            pltpu.VMEM((2 * LANES, LANES), jnp.bfloat16),
            pltpu.SemaphoreType.DMA((6, 3)),
            pltpu.SemaphoreType.DMA((8, 3)),
            pltpu.SemaphoreType.DMA((2,)),
        ],
        cost_estimate=pl.CostEstimate(
            flops=0, bytes_accessed=vregs * 4096 if first else 4096, transcendentals=0
        ),
        compiler_params=params(31 if first else 15),
        name="iterate",
    )(*pieces, taps, in_hbm(blur), in_hbm(adj))


def place_kernel(where_ref, *refs):
    refs[-1][...] = refs[0][0]


def place(where, block, whole, group):
    args = [where, block]
    in_specs = [pl.BlockSpec((1, Z, GROUP, CHUNK), lambda j, w: (j, 0, 0, 0))]
    aliases = {}
    if whole is not None:
        args.append(whole)
        in_specs.append(pl.BlockSpec(memory_space=pl.ANY))
        aliases = {2: 0}
    return pl.pallas_call(
        place_kernel,
        out_shape=jax.ShapeDtypeStruct((Z, ROWS, 2 * HALF), jnp.float32),
        grid_spec=pltpu.PrefetchScalarGridSpec(
            num_scalar_prefetch=1,
            grid=(2,),
            in_specs=in_specs,
            out_specs=pl.BlockSpec((Z, GROUP, CHUNK), lambda j, w: (0, group, 2 * w[0] + j)),
        ),
        input_output_aliases=aliases,
        cost_estimate=pl.CostEstimate(flops=0, bytes_accessed=1 << 20, transcendentals=0),
        compiler_params=params(4),
        name="place",
    )(*args)


def neighbours(views, tiles):
    right = []
    for v in range(views):
        for t in range(tiles):
            if (t + v) % 2 == 0:
                right.append((v * tiles + t, (1 - v) * tiles + t))
            elif t + 1 < tiles:
                right.append((v * tiles + t, v * tiles + t + 1))
    return right


def per_device(views_data, psf_axial, psf_rows, psf_cols):
    views, tiles, bands = lax.axis_size("view"), lax.axis_size("tx"), lax.axis_size("ty")
    swap = [(0, 1), (1, 0)]
    right = neighbours(views, tiles)
    left = [(b, a) for a, b in right]
    down = [(i, i + 1) for i in range(bands - 1)]
    up = [(b, a) for a, b in down]
    half = lax.rem(lax.axis_index("tx") + lax.axis_index("view"), 2)

    def other_rows(views_data, *starts):
        at = (1 - half) * HALF
        return jnp.concatenate(
            [
                lax.dynamic_slice(views_data, (0, 0, row, at), (1, Z, rows, HALF))[0]
                for row, rows in starts
            ],
            axis=1,
        )

    border = other_rows(views_data, (0, GROUP), (ROWS - GROUP, GROUP))
    later, axial, rows, cols, border = lax.optimization_barrier(
        (views_data, psf_axial, psf_rows, psf_cols, border)
    )
    border_in = lax.ppermute(border, "view", swap)
    raw = jnp.concatenate([axial[0], rows[0], cols[0]])
    raw_other = lax.ppermute(raw, "view", swap)
    upper_in = lax.ppermute(other_rows(later, (GROUP, GROUP)), "view", swap)
    last_rows, raw_other = lax.optimization_barrier(
        (other_rows(later, (2 * GROUP, GROUP)), raw_other)
    )
    lower_in = lax.ppermute(last_rows, "view", swap)

    view = lax.axis_index("view")
    where = jnp.stack([half, view]).astype(jnp.int32)
    there = (1 - half).astype(jnp.int32)[None]

    def sides(west, east):
        return lax.ppermute(west, ("view", "tx"), right), lax.ppermute(east, ("view", "tx"), left)

    border, border_east, border_west, to_up, to_down = turn(where, views_data, border_in, (0, 3))
    raw, raw_other, to_up, to_down = lax.optimization_barrier((raw, raw_other, to_up, to_down))
    north = lax.ppermute(to_down, "ty", down)
    south = lax.ppermute(to_up, "ty", up)

    def norm(taps):
        parts = (taps[:21], taps[21:28], taps[28:35])
        return jnp.concatenate([part / jnp.sum(part) for part in parts])

    own, other = norm(raw), norm(raw_other)
    lanes = jnp.concatenate(
        [
            jnp.broadcast_to(jnp.where(view == 0, own, other)[:, None], (own.shape[0], Z)),
            jnp.broadcast_to(jnp.where(view == 0, other, own)[:, None], (own.shape[0], Z)),
        ],
        axis=1,
    )
    blur, adj = matrices(lanes[:21])
    taps = jnp.zeros((16, LANES), jnp.float32)
    taps = taps.at[0:7].set(lanes[28:35]).at[8:15].set(lanes[21:28])

    upper_in, blur, adj = lax.optimization_barrier((upper_in, blur, adj))
    upper, upper_east, upper_west = turn(where, views_data, upper_in, (1,))
    west, east = sides(
        jnp.concatenate([border_east, upper_east]), jnp.concatenate([border_west, upper_west])
    )
    lower, lower_east, lower_west, north, south = turn(
        where, views_data, lower_in, (2,), (north, south)
    )
    last_west, last_east = sides(lower_east, lower_west)
    recorded = (north, west, last_west, border, upper, lower, east, last_east, south)

    estimate, top, low = iterate(
        recorded, None, taps, blur, adj, first=True, row0=0, n_out=ROWS
    )
    def piece(group, field):
        return iterate(
            recorded, field, taps, blur, adj, first=False, row0=GROUP * group, n_out=GROUP
        )

    field = (lax.ppermute(low, "ty", down), estimate, lax.ppermute(top, "ty", up))
    theirs = []
    whole = None
    for group in (1, 2, 0, 3):
        block = piece(group, field)
        theirs.append((group, lax.ppermute(block, "view", swap)))
        whole = place(where[:1], block, whole, group)
    for group, block in theirs:
        whole = place(there, block, whole, group)
    return whole


def solution(mesh):
    placed = (P("view", None, "ty", "tx"), P("view", None), P("view", None), P("view", None))
    return jax.shard_map(
        per_device, mesh=mesh, in_specs=placed, out_specs=P(None, "ty", "tx"), check_vma=False
    )
```
